32 devices in a mesh: space: 8 (over z, x), chan: 4 (over y, core).
Axes of the slice: x: 2, y: 2, z: 4, core: 2. Of those that a mesh axis runs over, the one named last changes fastest.
Arguments:
- features: bfloat16 [512, 32, 512], P(('space', 'chan')), may hold values from -6 to 6
- occupancy: int32 [512], P(('space', 'chan')), may hold values 0 or 1
- neighbours: int32 [512, 6], P(('space', 'chan')), may hold values from -1 to 511, as said below
- conv_weight: bfloat16 [27, 32, 32], replicated, may hold values from -0.21875 to 0.21875
- conv_bias: float32 [32], replicated, may hold values from -3 to 3
- latent: bfloat16 [32768, 512], P(('space', 'chan')), may hold values from -6 to 6
- token_proj: bfloat16 [32, 512], replicated, may hold values from -1 to 1
- norm_gain: float32 [512], replicated, may hold values from 0.25 to 1.75
- qkv_weight: bfloat16 [3, 512, 512], replicated
- out_weight: bfloat16 [512, 512], replicated, may hold values from -0.25 to 0.25
Outputs:
- conv_out: bfloat16 [512, 32, 512], P(('space', 'chan'))
- tokens_out: bfloat16 [512, 32768], P(None, ('space', 'chan'))
The draws below stay inside these ranges and needn't reach their ends.
Inputs may be any that keep to these rules, and one draw needn't show every extreme that they name: `neighbours`: entry [b, d] is the brick across face d of brick b (d = 0..5 for -x, +x, -y, +y, -z, +z), or -1 where there is none. Brick b lies on device b // 16 in the order of space+chan, and a neighbour lies on a device whose index differs from its brick's by at most 2.
All inputs are finite; a program needn't handle non-finite values. No bound on the sum of `occupancy` on one device may be relied on, other than what follows from the above.
Results may differ from the reference program's by a relative error of at most 0.0054.
Values may be sent and summed in bfloat16 or wider, within the bound.
No kernel may reach another device: no remote copies, remote signals or barrier semaphores. Data moves between devices by JAX's collectives and lax.ppermute only.
A program may use at most 128 MiB of HBM per device.

```python
import jax
import jax.numpy as jnp
from jax import lax

C = 32
D = 512
HEADS = 8
HD = 64
WIN = 1024
REACH = 2
BR_DEV = 16
BRICKS = 512
TOKENS = 32768
N_SPACE = 8
N_CHAN = 4


def draw_neighbours(key, part):
    key_offset, key_slot, key_keep = jax.random.split(key, 3)
    brick_ids = jnp.arange(BRICKS, dtype=jnp.int32)[:, None]
    owner = brick_ids // BR_DEV
    spread = jax.random.randint(key_offset, (BRICKS, 6), -REACH, REACH + 1)
    target = jnp.clip(owner + spread, 0, BRICKS // BR_DEV - 1)
    slots = jax.random.randint(key_slot, (BRICKS, 6), 0, BR_DEV)
    keep_draw = jax.random.randint(key_keep, (BRICKS, 6), 0, 8)
    linked = jnp.where(keep_draw < 7, target * BR_DEV + slots, -1)
    linked = linked.at[0, 0].set(-1)
    linked = linked.at[BRICKS - 2, 5].set(BRICKS - 1)
    return linked.astype(jnp.int32)


def draw_qkv_weight(key, part):
    key_q, key_k, key_v = jax.random.split(key, 3)
    scale_in = D ** (-0.5)
    query_part = jax.random.normal(key_q, (D, D), jnp.float32) * scale_in
    key_part = jax.random.normal(key_k, (D, D), jnp.float32) * scale_in
    value_part = jax.random.normal(key_v, (D, D), jnp.float32) * scale_in
    return jnp.stack([query_part, key_part, value_part]).astype(jnp.bfloat16)


def plant(values, stream_key, smallest, high):
    extent = values.shape
    place = [jax.random.randint(jax.random.fold_in(stream_key, axis), (), 0, extent[axis]) for axis in range(len(extent))]
    values = values.at[tuple(place)].set(smallest)
    longest = extent.index(max(extent))
    place[longest] = (place[longest] + 1) % extent[longest]
    return values.at[tuple(place)].set(high)


def steps_of(rng, dims, cuts, least, high):
    level = 1.0
    for dim, parts in cuts:
        draws = jax.random.uniform(jax.random.fold_in(jax.random.fold_in(rng, 6), dim), (parts,), jnp.float32, least / len(cuts), high / len(cuts))
        level = level * jnp.repeat(jnp.exp(draws), dims[dim] // parts).reshape((-1,) + (1,) * (len(dims) - 1 - dim))
    return level


def normal_values(stream_key, shape, width, reach, cuts=(), kind=jnp.bfloat16):
    array = width * jax.random.normal(stream_key, shape, jnp.float32)
    if cuts:
        array = array * steps_of(stream_key, shape, cuts, -0.22, 0.18)
    return jnp.clip(array, -reach, reach).astype(kind)


def setup_inputs(seed: int = 0) -> dict:
    key_of = jax.random.split(jax.random.key(seed), 11)
    return {
        "features": normal_values(key_of[0], (BRICKS, C, 512), 1.0, 6.0, ((0, 32),)),
        "occupancy": plant((jax.random.randint(key_of[1], (BRICKS,), 0, 4) < 3).astype(jnp.int32), jax.random.fold_in(key_of[1], 1), 0, 1),
        "neighbours": draw_neighbours(jax.random.fold_in(key_of[10], 71), 0),
        "conv_weight": normal_values(key_of[3], (27, C, C), (27 * C) ** -0.5, 0.21875),
        "conv_bias": normal_values(key_of[4], (C,), 0.5, 3.0, (), jnp.float32),
        "latent": normal_values(key_of[5], (TOKENS, D), 1.0, 6.0, ((0, 32),)),
        "token_proj": normal_values(key_of[6], (C, D), C ** -0.5, 1.0),
        "norm_gain": jnp.clip(1.0 + 0.15 * jax.random.normal(key_of[7], (D,), jnp.float32), 0.25, 1.75),
        "qkv_weight": draw_qkv_weight(jax.random.fold_in(key_of[10], 71), 0),
        "out_weight": normal_values(key_of[9], (D, D), D ** -0.5, 0.25),
    }


def face_table(voxels):
    brick_count, channels = (voxels.shape[0], voxels.shape[1])
    sheets = [voxels[:, :, 7, :, :], voxels[:, :, 0, :, :], voxels[:, :, :, 7, :], voxels[:, :, :, 0, :], voxels[:, :, :, :, 7], voxels[:, :, :, :, 0]]
    return jnp.stack([sheet.reshape(brick_count, channels, 64) for sheet in sheets], axis=1)

def extend(voxels, gathered):
    brick_count, channels = (voxels.shape[0], voxels.shape[1])
    sheets = gathered.reshape(brick_count, 6, channels, 8, 8)
    padded = jnp.pad(voxels, ((0, 0), (0, 0), (1, 1), (1, 1), (1, 1)))
    padded = padded.at[:, :, 0, 1:9, 1:9].set(sheets[:, 0])
    padded = padded.at[:, :, 9, 1:9, 1:9].set(sheets[:, 1])
    padded = padded.at[:, :, 1:9, 0, 1:9].set(sheets[:, 2])
    padded = padded.at[:, :, 1:9, 9, 1:9].set(sheets[:, 3])
    padded = padded.at[:, :, 1:9, 1:9, 0].set(sheets[:, 4])
    padded = padded.at[:, :, 1:9, 1:9, 9].set(sheets[:, 5])
    return padded

def convolve(padded, weight):
    brick_count, channels = (padded.shape[0], padded.shape[1])
    running = jnp.zeros((brick_count, weight.shape[1], 512), jnp.float32)
    for step_x in range(3):
        for step_y in range(3):
            for step_z in range(3):
                slab = padded[:, :, step_x:step_x + 8, step_y:step_y + 8, step_z:step_z + 8]
                slab = slab.reshape(brick_count, channels, 512).astype(jnp.float32)
                kernel_tap = weight[step_x * 9 + step_y * 3 + step_z].astype(jnp.float32)
                running = running + jnp.einsum('kc,bcv->bkv', kernel_tap, slab)
    return running

def pool_tokens(conv_out):
    brick_count, channels = (conv_out.shape[0], conv_out.shape[1])
    cells = conv_out.astype(jnp.float32).reshape(brick_count, channels, 2, 2, 2, 2, 2, 2, 2, 2, 2)
    means = lax.optimization_barrier(jnp.mean(cells, axis=(4, 7, 10)))
    means = jnp.transpose(means, (1, 0, 2, 4, 6, 3, 5, 7))
    return means.reshape(channels, brick_count * 64).astype(jnp.bfloat16)

def rms_norm(mixed_in, norm_gain):
    scale_row = lax.rsqrt(lax.optimization_barrier(jnp.mean(mixed_in * mixed_in, axis=-1, keepdims=True)) + 1e-06)
    return (mixed_in * scale_row * norm_gain[None, :]).astype(jnp.bfloat16)

def reference(features, occupancy, neighbours, conv_weight, conv_bias, latent, token_proj, norm_gain, qkv_weight, out_weight):
    alive = occupancy.astype(jnp.float32)
    masked = (features.astype(jnp.float32) * alive[:, None, None]).astype(jnp.bfloat16)
    voxels = masked.reshape(BRICKS, C, 8, 8, 8)
    faces = face_table(voxels).reshape(BRICKS * 6, C, 64)
    has_peer = neighbours >= 0
    face_index = jnp.where(has_peer, neighbours, 0) * 6 + jnp.arange(6, dtype=jnp.int32)[None, :]

    def per_block(first_row):
        block_vox = lax.dynamic_slice_in_dim(voxels, first_row, BR_DEV, 0)
        block_index = lax.dynamic_slice_in_dim(face_index, first_row, BR_DEV, 0)
        block_peer = lax.dynamic_slice_in_dim(has_peer, first_row, BR_DEV, 0)
        gathered = jnp.take(faces, block_index.reshape(-1), axis=0).reshape(BR_DEV, 6, C, 64)
        gathered = jnp.where(block_peer[:, :, None, None], gathered, jnp.zeros_like(gathered))
        summed = convolve(extend(block_vox, gathered), conv_weight)
        own_part = lax.dynamic_slice_in_dim(masked, first_row, BR_DEV, 0).astype(jnp.float32)
        block_alive = lax.dynamic_slice_in_dim(alive, first_row, BR_DEV, 0)
        mixed = own_part + jax.nn.silu(summed + conv_bias[None, :, None])
        return (block_alive[:, None, None] * mixed).astype(jnp.bfloat16)
    starts = jnp.arange(N_SPACE * N_CHAN, dtype=jnp.int32) * BR_DEV
    conv_out = lax.map(per_block, starts).reshape(BRICKS, C, 512)
    pooled = pool_tokens(conv_out)
    mixed_in = latent.astype(jnp.float32) + jnp.dot(pooled.T, token_proj, preferred_element_type=jnp.float32)
    normed = rms_norm(mixed_in, norm_gain)
    queries = jnp.dot(normed, qkv_weight[0], preferred_element_type=jnp.float32).astype(jnp.bfloat16)
    keys = jnp.dot(normed, qkv_weight[1], preferred_element_type=jnp.float32).astype(jnp.bfloat16)
    values = jnp.dot(normed, qkv_weight[2], preferred_element_type=jnp.float32).astype(jnp.bfloat16)
    token_alive = jnp.broadcast_to(occupancy[:, None], (BRICKS, 64)).reshape(TOKENS)
    half_win = WIN // 2
    window_count = TOKENS // WIN
    rolled_q = jnp.roll(queries, -half_win, axis=0).reshape(window_count, WIN, HEADS, HD)
    rolled_k = jnp.roll(keys, -half_win, axis=0).reshape(window_count, WIN, HEADS, HD)
    rolled_v = jnp.roll(values, -half_win, axis=0).reshape(window_count, WIN, HEADS, HD)
    rolled_alive = jnp.roll(token_alive, -half_win).reshape(window_count, WIN)
    diagonal = jnp.eye(WIN, dtype=bool)

    def per_window(inputs):
        win_q, win_k, win_v, win_alive = inputs
        scores = jnp.einsum('qhd,khd->hqk', win_q.astype(jnp.float32), win_k.astype(jnp.float32)) * HD ** (-0.5)
        allowed = (win_alive[None, None, :] > 0) | diagonal[None]
        row_peak = lax.optimization_barrier(jnp.max(jnp.where(allowed, scores, -1e+30), axis=-1, keepdims=True))
        raw = jnp.where(allowed, jnp.exp(scores - row_peak), 0.0)
        weights_bf = (raw / lax.optimization_barrier(jnp.sum(raw, axis=-1, keepdims=True))).astype(jnp.bfloat16)
        return jnp.einsum('hqk,khd->qhd', weights_bf.astype(jnp.float32), win_v.astype(jnp.float32)).astype(jnp.bfloat16)
    attended = lax.map(per_window, (rolled_q, rolled_k, rolled_v, rolled_alive))
    attended = jnp.roll(attended.reshape(TOKENS, D), half_win, axis=0)
    mixing = jnp.dot(attended, out_weight, preferred_element_type=jnp.float32)
    tokens_out = (mixed_in + mixing).T.astype(jnp.bfloat16)
    return (conv_out, tokens_out)
```

```python
import math

import jax
import jax.numpy as jnp
import numpy as np
from jax import lax
from jax.experimental import pallas as pl
from jax.experimental.pallas import tpu as pltpu
from jax.sharding import PartitionSpec as P

HD = 64
WIN = 1024
REACH = 2
AXES = ("space", "chan")
NEG = -1e30
TILES = 96
F32 = jnp.float32
BF16 = jnp.bfloat16
VM = pltpu.VMEM
ANY = pl.ANY


def vmem(count):
    return [pl.BlockSpec(memory_space=pltpu.VMEM)] * count


def smem(count):
    return [pl.BlockSpec(memory_space=pltpu.SMEM)] * count


def anyspace(count):
    return [pl.BlockSpec(memory_space=pl.ANY)] * count


def cost(flops, moved, trans=0):
    return pl.CostEstimate(flops=flops, bytes_accessed=moved, transcendentals=trans)


def swap_blocks(four):
    lane = lax.broadcasted_iota(jnp.int32, four[0].shape, 1)
    low = lane < 64
    even = (lane // 32) % 2 == 0
    half = []
    for a, b in ((0, 2), (1, 3)):
        half.append(jnp.where(low, four[a], pltpu.roll(four[b], 64, 1)))
        half.append(jnp.where(low, pltpu.roll(four[a], 64, 1), four[b]))
    a0, a2, a1, a3 = half
    return [
        jnp.where(even, a0, pltpu.roll(a1, 32, 1)),
        jnp.where(even, pltpu.roll(a0, 96, 1), a1),
        jnp.where(even, a2, pltpu.roll(a3, 32, 1)),
        jnp.where(even, pltpu.roll(a2, 96, 1), a3),
    ]


def prep_kernel(occ, feat, xb, faces, turned, wide):
    for g in range(4):
        rows = [
            feat[4 * g + j].astype(F32) * (occ[4 * g + j]).astype(F32) for j in range(4)
        ]
        turned[g] = jnp.concatenate(rows, axis=0).T
    for g in range(4):
        sheets = [turned[g, pl.ds(z, 64, stride=8), :] for z in range(8)]
        for face, z in ((0, 0), (1, 7)):
            for xq in range(4):
                tile = jnp.concatenate(
                    [sheets[z][8 * xq : 8 * xq + 8], sheets[z][8 * xq + 32 : 8 * xq + 40]], axis=1
                )
                faces[64 + (2 * g + face) * 4 + xq] = tile.astype(BF16)
        for half in range(2):
            for j, block in enumerate(swap_blocks(sheets[4 * half : 4 * half + 4])):
                wide[half, 4 * g + j] = block
                xb[4 * g + j, :, 128 * half : 128 * half + 128] = block
    for b in range(16):
        for half in range(2):
            lanes = slice(128 * half, 128 * half + 128)
            faces[4 * b, :, lanes] = wide[half, b, 56:64, :].astype(BF16)
            faces[4 * b + 1, :, lanes] = wide[half, b, 0:8, :].astype(BF16)
            faces[4 * b + 2, :, lanes] = wide[half, b, pl.ds(7, 8, stride=8), :].astype(BF16)
            faces[4 * b + 3, :, lanes] = wide[half, b, pl.ds(0, 8, stride=8), :].astype(BF16)


def prep(occ, feat):
    return pl.pallas_call(
        prep_kernel,
        name="prep",
        out_shape=(
            jax.ShapeDtypeStruct((16, 64, 256), F32),
            jax.ShapeDtypeStruct((TILES, 8, 256), BF16),
        ),
        in_specs=smem(1) + vmem(1),
        out_specs=tuple(vmem(2)),
        scratch_shapes=[VM((4, 512, 128), F32), VM((2, 16, 64, 128), F32)],
        cost_estimate=cost(1 << 20, 2 << 20),
    )(occ, feat)


def shifted_rows(tile, step):
    if step == 0:
        return tile
    row = lax.broadcasted_iota(jnp.int32, tile.shape, 0) % 8
    if step < 0:
        moved = pltpu.roll(tile, 1, 0)
        return jnp.where(row == 0, 0.0, moved)
    moved = pltpu.roll(tile, tile.shape[0] - 1, 0)
    return jnp.where(row == 7, 0.0, moved)


def write_patches(lhs, brick, tiles):
    zero = jnp.zeros((8, 256), F32)
    rows = pl.ds(pl.multiple_of(brick * 64, 64), 64)
    for dy in (-1, 0, 1):
        moved = [shifted_rows(t, dy) for t in tiles]
        for dx in (-1, 0, 1):
            picked = [moved[x + dx] if 0 <= x + dx < 8 else zero for x in range(8)]
            tap = (dx + 1) * 3 + dy + 1
            lhs[rows, 256 * tap : 256 * tap + 256] = jnp.concatenate(picked, axis=0).astype(BF16)


def bands_kernel(taps, spread, band, band_z, wide):
    wide[...] = jnp.dot(taps[...], spread[...], preferred_element_type=F32)
    block = lax.broadcasted_iota(jnp.int32, (32, 256), 1) // 32

    def per_tap(t, carry):
        base = [
            wide[pl.ds(pl.multiple_of((t * 3 + k) * 32, 32), 32), :] for k in range(3)
        ]
        for z in range(8):
            value = jnp.where(block == z, base[1], 0.0)
            value = jnp.where(block == z + 1, base[0], value)
            value = jnp.where(block == z - 1, base[2], value)
            band[pl.ds(pl.multiple_of(t * 256 + 32 * z, 32), 32), :] = value.astype(BF16)
        for face, k in ((0, 0), (1, 2)):
            value = jnp.where(block == 7 * face, base[k], 0.0).astype(BF16)
            for j in range(4):
                start = pl.multiple_of(t * 256 + 128 * face + 32 * j, 32)
                band_z[pl.ds(start, 32), :] = value
        return carry

    lax.fori_loop(0, 9, per_tap, 0)


def bands(conv_weight):
    taps = conv_weight.transpose(0, 2, 1).reshape(27 * 32, 32)
    spread = jnp.asarray(np.tile(np.eye(32, dtype=np.float32), (1, 8)), BF16)
    return pl.pallas_call(
        bands_kernel,
        name="bands",
        out_shape=(
            jax.ShapeDtypeStruct((2304, 256), BF16),
            jax.ShapeDtypeStruct((2304, 256), BF16),
        ),
        in_specs=vmem(2),
        out_specs=tuple(vmem(2)),
        scratch_shapes=[VM((864, 256), F32)],
        cost_estimate=cost(1 << 24, 3 << 20),
    )(taps, spread)


def inner_kernel(xb, band, acc, lhs):
    def per_brick(b, carry):
        write_patches(lhs, b, [xb[b, 8 * x : 8 * x + 8, :] for x in range(8)])
        return carry

    lax.fori_loop(0, 16, per_brick, 0)

    def per_rows(i, carry):
        rows = pl.ds(pl.multiple_of(i * 512, 512), 512)
        acc[rows, :] = jnp.dot(lhs[rows, :], band[...], preferred_element_type=F32)
        return carry

    lax.fori_loop(0, 2, per_rows, 0)


def inner(xb, band):
    return pl.pallas_call(
        inner_kernel,
        name="inner",
        out_shape=jax.ShapeDtypeStruct((1024, 256), F32),
        in_specs=vmem(2),
        out_specs=vmem(1)[0],
        scratch_shapes=[VM((1024, 2304), BF16)],
        cost_estimate=cost(2 * 1024 * 2304 * 256, 4 << 20),
    )(xb, band)


def outer_kernel(
    index, occ, core, own, back, ahead, partner, relay, xb, acc, band, band_z, bias, pool, pick,
    latent, proj, gain,
    blocks, pooled, to_partner, to_cross,
    store, lhs, flat, edges, sums, halves, sems,
):
    copies = [
        pltpu.make_async_copy(ref, store.at[slot], sems.at[slot])
        for slot, ref in enumerate((own, back, ahead, partner, relay))
    ]
    for copy in copies:
        copy.start()
    for copy in copies:
        copy.wait()
    lane = lax.broadcasted_iota(jnp.int32, (8, 256), 1) % 128 // 32

    def gather(b, carry):
        for face in range(4):
            at = index[b * 6 + face]
            valid = (at >= 0).astype(F32)
            at = jnp.maximum(at, 0)
            tile = store[at // 16, (at % 16) * 4 + face].astype(F32) * valid
            flat[face, pl.ds(pl.multiple_of(b * 8, 8), 8), :] = tile
        low, high = [], []
        for face, into in ((0, low), (1, high)):
            at = index[b * 6 + 4 + face]
            valid = (at >= 0).astype(F32)
            at = jnp.maximum(at, 0)
            brick = at % 16
            base = 64 + (brick // 4 * 2 + (1 - face)) * 4
            mask = jnp.where(lane == brick % 4, valid, 0.0)
            for xq in range(4):
                into.append(store[at // 16, base + xq].astype(F32) * mask)
        tiles = []
        for x in range(8):
            lanes = slice(128 * (x // 4), 128 * (x // 4) + 128)
            tiles.append(jnp.concatenate([low[x % 4][:, lanes], high[x % 4][:, lanes]], axis=1))
        write_patches(lhs, b, tiles)
        return carry

    lax.fori_loop(0, 16, gather, 0)
    for face in range(4):
        sheet = flat[face]
        side = 0 if face % 2 == 0 else 2
        total = None
        for step in (-1, 0, 1):
            tap = side * 3 + step + 1 if face < 2 else (step + 1) * 3 + side
            part = jnp.dot(
                shifted_rows(sheet, step).astype(BF16),
                band[256 * tap : 256 * tap + 256, :],
                preferred_element_type=F32,
            )
            total = part if total is None else total + part
        edges[face] = total

    def per_rows(i, carry):
        rows = pl.ds(pl.multiple_of(i * 512, 512), 512)
        sums[rows, :] = acc[rows, :] + jnp.dot(
            lhs[rows, :], band_z[...], preferred_element_type=F32
        )
        return carry

    lax.fori_loop(0, 2, per_rows, 0)
    row = lax.broadcasted_iota(jnp.int32, (8, 256), 0)

    def finish(b, carry):
        start = pl.multiple_of(b * 64, 64)
        alive = occ[b].astype(F32)
        sheet_rows = pl.ds(pl.multiple_of(b * 8, 8), 8)
        y_low, y_high = edges[2, sheet_rows, :], edges[3, sheet_rows, :]
        done = []
        for x in range(8):
            total = sums[pl.ds(start + 8 * x, 8), :]
            total = total + jnp.where(row == 0, y_low[x : x + 1, :], 0.0)
            total = total + jnp.where(row == 7, y_high[x : x + 1, :], 0.0)
            if x == 0:
                total = total + edges[0, sheet_rows, :]
            if x == 7:
                total = total + edges[1, sheet_rows, :]
            value = total + bias[...]
            mixed = xb[b, 8 * x : 8 * x + 8, :] + value / (1.0 + jnp.exp(-value))
            done.append(alive * mixed)
        block = jnp.concatenate(done, axis=0).astype(BF16)
        blocks[b] = block.astype(F32)
        cells = jnp.dot(pool[...], block, preferred_element_type=F32) * pick[...]
        cells = cells[:, :128] + cells[:, 128:]
        cells = cells + pltpu.roll(cells, 64, 1)
        cells = cells + pltpu.roll(cells, 32, 1)
        pooled[pl.ds(start, 64), :] = cells.astype(BF16)
        return carry

    lax.fori_loop(0, 16, finish, 0)

    def norm(i, carry):
        rows = pl.ds(pl.multiple_of(i * 256, 256), 256)
        lifted = jnp.dot(pooled[rows, :], proj[...], preferred_element_type=F32)
        mixed = latent[rows, :].astype(F32) + lifted
        scale = lax.rsqrt(jnp.mean(mixed * mixed, axis=-1, keepdims=True) + 1e-06)
        halves[i // 2, pl.ds(pl.multiple_of(i % 2 * 256, 256), 256), :] = (
            mixed * scale * gain[...]
        ).astype(BF16)
        return carry

    lax.fori_loop(0, 4, norm, 0)
    for half in range(2):
        block_row = lax.broadcasted_iota(jnp.int32, (16, 512), 0)
        flags = jnp.zeros((16, 512), F32)
        for b in range(8):
            flags = jnp.where(block_row == b, occ[8 * half + b].astype(F32), flags)
        halves[half, 512:528, :] = flags.astype(BF16)
    out = [
        pltpu.make_async_copy(halves.at[1 - core[0]], to_partner, sems.at[5]),
        pltpu.make_async_copy(halves.at[core[0]], to_cross, sems.at[6]),
    ]
    for copy in out:
        copy.start()
    for copy in out:
        copy.wait()


def outer(index, occ, core, stores, xb, acc, band, band_z, bias, pool, pick, latent, proj, gain):
    return pl.pallas_call(
        outer_kernel,
        name="outer",
        out_shape=(
            jax.ShapeDtypeStruct((16, 64, 256), F32),
            jax.ShapeDtypeStruct((1024, 128), BF16),
            jax.ShapeDtypeStruct((528, 512), BF16),
            jax.ShapeDtypeStruct((528, 512), BF16),
        ),
        in_specs=smem(3) + anyspace(5) + vmem(10),
        out_specs=tuple(vmem(2) + anyspace(2)),
        scratch_shapes=[
            VM((5, TILES, 8, 256), BF16),
            VM((1024, 2304), BF16),
            VM((4, 128, 256), F32),
            VM((4, 128, 256), F32),
            VM((1024, 256), F32),
            VM((2, 528, 512), BF16),
            pltpu.SemaphoreType.DMA((7,)),
        ],
        cost_estimate=cost(2 * 1024 * 2304 * 256, 8 << 20, 1 << 18),
    )(index, occ, core, *stores, xb, acc, band, band_z, bias, pool, pick, latent, proj, gain)


def restore_kernel(blocks, out, turned):
    for g in range(4):
        for half in range(2):
            lanes = slice(128 * half, 128 * half + 128)
            four = [blocks[4 * g + j, :, lanes] for j in range(4)]
            for k, sheet in enumerate(swap_blocks(four)):
                turned[g, pl.ds(4 * half + k, 64, stride=8), :] = sheet
    for g in range(4):
        rows = turned[g].T
        for j in range(4):
            out[4 * g + j] = rows[32 * j : 32 * j + 32].astype(BF16)


def restore(blocks):
    return pl.pallas_call(
        restore_kernel,
        name="restore",
        out_shape=jax.ShapeDtypeStruct((16, 32, 512), BF16),
        in_specs=vmem(1),
        out_specs=vmem(1)[0],
        scratch_shapes=[VM((4, 512, 128), F32)],
        cost_estimate=cost(1 << 20, 2 << 20),
    )(blocks)


NT = (((1,), (1,)), ((), ()))
SCALE = HD ** (-0.5) * math.log2(math.e)


def column_max(part):
    return jnp.max(part, axis=0, keepdims=True)


def own_kernel(
    occ, core, to_partner, to_cross, wq, wk, wv_t, query, state, peak, normed, keys, values, sems
):
    copies = [
        pltpu.make_async_copy(
            to_partner.at[pl.ds(0, 512)], normed.at[1 - core[0]], sems.at[0]
        ),
        pltpu.make_async_copy(to_cross.at[pl.ds(0, 512)], normed.at[core[0]], sems.at[1]),
    ]
    for copy in copies:
        copy.start()
    for copy in copies:
        copy.wait()
    lane = lax.broadcasted_iota(jnp.int32, (512, 128), 1)
    for half in range(2):
        rows = normed[half]
        found = jnp.dot(rows, wq[...], preferred_element_type=F32) * SCALE
        for head in range(8):
            pair = found[:, 128 * (head // 2) : 128 * (head // 2) + 128]
            keep = lane < 64 if head % 2 == 0 else lane >= 64
            query[head, half] = jnp.where(keep, pair, 0.0).astype(BF16)
        found = jnp.dot(rows, wk[...], preferred_element_type=F32)
        for pair in range(4):
            keys[pair, half] = found[:, 128 * pair : 128 * pair + 128].astype(BF16)
        found = lax.dot_general(wv_t[...], rows, NT, preferred_element_type=F32)
        for head in range(8):
            values[head, half, 0:64, :] = found[64 * head : 64 * head + 64].astype(BF16)
            values[head, half, 64:80, :] = jnp.ones((16, 512), BF16)

    row = lax.broadcasted_iota(jnp.int32, (128, 128), 0)
    col = lax.broadcasted_iota(jnp.int32, (128, 128), 1)
    eye = row == col

    def per_head(head, carry):
        for half in range(2):
            bias = [
                jnp.where(occ[8 * half + b] > 0, 0.0, NEG).astype(F32) for b in range(8)
            ]
            for tile in range(2):
                lanes = slice(256 * tile, 256 * tile + 256)
                scores = lax.dot_general(
                    keys[head // 2, half],
                    query[head, half, lanes, :],
                    NT,
                    preferred_element_type=F32,
                )
                top = None
                for b in range(8):
                    part = scores[64 * b : 64 * b + 8]
                    for k in range(1, 8):
                        part = jnp.maximum(part, scores[64 * b + 8 * k : 64 * b + 8 * k + 8])
                    part = part + bias[b]
                    top = part if top is None else jnp.maximum(top, part)
                top = column_max(top)
                selves, dead = [], []
                for k in range(2):
                    first = 256 * tile + 128 * k
                    block = scores[first : first + 128, 128 * k : 128 * k + 128]
                    selves.append(column_max(jnp.where(eye, block, NEG)))
                    brick = first // 64
                    one = lax.broadcasted_iota(jnp.int32, (1, 128), 1)
                    dead.append(jnp.where(one < 64, bias[brick], bias[brick + 1]))
                own = jnp.concatenate(selves, axis=1)
                dead = jnp.concatenate(dead, axis=1)
                own = jnp.where(dead < 0.0, own, NEG)
                top = jnp.maximum(top, own)
                parts = []
                for b in range(8):
                    parts.append(
                        jnp.exp2(scores[64 * b : 64 * b + 64] - (top - bias[b])).astype(BF16)
                    )
                weights = jnp.concatenate(parts, axis=0)
                out = jnp.dot(values[head, half], weights, preferred_element_type=F32)
                extra = jnp.where(dead < 0.0, jnp.exp2(own - top), 0.0)
                out = out + extra * values[head, half, :, lanes].astype(F32)
                state[head, half, :, lanes] = out[0:72]
                peak[head, half, :, lanes] = jnp.broadcast_to(top, (8, 256))
        return carry

    lax.fori_loop(0, 8, per_head, 0)


def own_attention(occ, core, to_partner, to_cross, wq, wk, wv_t):
    return pl.pallas_call(
        own_kernel,
        name="own_attention",
        out_shape=(
            jax.ShapeDtypeStruct((8, 2, 512, 128), BF16),
            jax.ShapeDtypeStruct((8, 2, 72, 512), F32),
            jax.ShapeDtypeStruct((8, 2, 8, 512), F32),
        ),
        in_specs=smem(2) + anyspace(2) + vmem(3),
        out_specs=tuple(vmem(3)),
        scratch_shapes=[
            VM((2, 512, 512), BF16),
            VM((4, 2, 512, 128), BF16),
            VM((8, 2, 80, 512), BF16),
            pltpu.SemaphoreType.DMA((2,)),
        ],
        cost_estimate=cost(6 << 30, 8 << 20, 1 << 22),
    )(occ, core, to_partner, to_cross, wq, wk, wv_t)


def side_kernel(
    half_ref, remote, query, state, peak, wk, wv_t, wo_t, latent_t, proj_t, pooled, *rest
):
    if len(rest) == 7:
        other, out, keys, values, attended, spare, sems = rest
    else:
        out, keys, values, attended, sems = rest
    half = half_ref[0]
    rows = remote[0:512, :]
    found = jnp.dot(rows, wk[...], preferred_element_type=F32)
    for pair in range(4):
        keys[pair] = found[:, 128 * pair : 128 * pair + 128].astype(BF16)
    found = lax.dot_general(wv_t[...], rows, NT, preferred_element_type=F32)
    for head in range(8):
        values[head, 0:64, :] = found[64 * head : 64 * head + 64].astype(BF16)
        values[head, 64:80, :] = jnp.ones((16, 512), BF16)
    flags = remote[512:528, :].astype(F32)
    biases = [jnp.where(flags[b : b + 1, 0:256] > 0.5, 0.0, NEG) for b in range(8)]

    def per_head(head, carry):
        for tile in range(2):
            lanes = slice(256 * tile, 256 * tile + 256)
            scores = lax.dot_general(
                keys[head // 2], query[head, half, lanes, :], NT, preferred_element_type=F32
            )
            top = None
            for b in range(8):
                part = scores[64 * b : 64 * b + 8]
                for k in range(1, 8):
                    part = jnp.maximum(part, scores[64 * b + 8 * k : 64 * b + 8 * k + 8])
                part = part + biases[b]
                top = part if top is None else jnp.maximum(top, part)
            before = peak[head, half, 0:1, lanes]
            top = jnp.maximum(column_max(top), before)
            parts = []
            for b in range(8):
                parts.append(
                    jnp.exp2(scores[64 * b : 64 * b + 64] - (top - biases[b])).astype(BF16)
                )
            weights = jnp.concatenate(parts, axis=0)
            total = jnp.dot(values[head], weights, preferred_element_type=F32)[0:72]
            total = total + state[head, half, :, lanes] * jnp.exp2(before - top)
            result = total[0:64] / total[64:65]
            attended[pl.ds(pl.multiple_of(head * 64, 64), 64), lanes] = result.astype(BF16)
        return carry

    lax.fori_loop(0, 8, per_head, 0)
    place = pl.ds(pl.multiple_of(half * 512, 512), 512)
    mixing = jnp.dot(wo_t[...], attended[...], preferred_element_type=F32)
    lifted = lax.dot_general(proj_t[...], pooled[place, :], NT, preferred_element_type=F32)
    result = ((latent_t[:, place].astype(F32) + lifted) + mixing).astype(BF16)
    if len(rest) == 7:
        out[:, place] = result
        out[:, pl.ds(pl.multiple_of((1 - half) * 512, 512), 512)] = other[...]
    else:
        out[...] = result


def side_attention(half, remote, query, state, peak, wk, wv_t, wo_t, latent_t, proj_t, pooled, other):
    last = other is not None
    return pl.pallas_call(
        side_kernel,
        name="last_attention" if last else "side_attention",
        out_shape=jax.ShapeDtypeStruct((512, 1024 if last else 512), BF16),
        in_specs=smem(1) + vmem(11 if last else 10),
        out_specs=vmem(1)[0],
        scratch_shapes=[
            VM((4, 512, 128), BF16),
            VM((8, 80, 512), BF16),
            VM((512, 512), BF16),
        ]
        + ([VM((8, 128), F32)] if last else [])
        + [pltpu.SemaphoreType.DMA((1,))],
        cost_estimate=cost(4 << 30, 6 << 20, 1 << 21),
    )(
        half, remote, query, state, peak, wk, wv_t, wo_t, latent_t, proj_t, pooled,
        *([other] if last else []),
    )


def pool_tables():
    pool = np.zeros((64, 64), np.float32)
    pick = np.zeros((64, 256), np.float32)
    for token in range(64):
        p = (token // 32) * 2 + token // 4 % 2
        q = (token // 16 % 2) * 2 + token // 2 % 2
        r = (token // 8 % 2) * 2 + token % 2
        for x in (2 * p, 2 * p + 1):
            for y in (2 * q, 2 * q + 1):
                pool[token, 8 * x + y] = 0.125
        pick[token, 64 * r : 64 * r + 64] = 1.0
    return jnp.asarray(pool, BF16), jnp.asarray(pick, F32)


def moved(array, by):
    size = lax.axis_size(AXES)
    pairs = [(i, i + by) for i in range(size) if 0 <= i + by < size]
    return lax.ppermute(array, AXES, pairs)


def swapped(array):
    size = lax.axis_size(AXES)
    return lax.ppermute(array, AXES, [(i, i ^ 1) for i in range(size)])


def crossed(array):
    size = lax.axis_size(AXES)
    pairs = [(i, (i - 1) % size if i % 2 == 0 else (i + 1) % size) for i in range(size)]
    return lax.ppermute(array, AXES, pairs)


def local(
    features, occupancy, neighbours, conv_weight, conv_bias, latent, token_proj, norm_gain,
    qkv_weight, out_weight,
):
    me = lax.axis_index(AXES)
    core = me % 2
    count = features.shape[0]
    xb, faces = prep(occupancy, features)
    back = moved(faces, 2)
    ahead = moved(faces, -2)
    partner = swapped(faces)
    relay = swapped(jnp.where(core == 1, back, ahead))
    (
        conv_weight, conv_bias, latent_in, token_proj, qkv_weight, out_weight, neighbours, _
    ) = lax.optimization_barrier(
        (conv_weight, conv_bias, latent, token_proj, qkv_weight, out_weight, neighbours, faces)
    )
    band, band_z = bands(conv_weight)
    bias = jnp.tile(conv_bias, 8)[None, :]
    pool, pick = pool_tables()
    proj = jnp.pad(token_proj, ((0, 96), (0, 0)))
    proj_t = proj.T
    wq, wk = qkv_weight[0], qkv_weight[1]
    wv_t, wo_t = qkv_weight[2].T, out_weight.T
    latent_t = latent_in.T
    has_peer = neighbours >= 0
    peer = jnp.where(has_peer, neighbours, 0)
    away = jnp.clip(peer // count - me, -REACH, REACH)
    slots = jnp.where(core == 0, jnp.array([1, 4, 0, 3, 2]), jnp.array([1, 3, 0, 4, 2]))
    slot = jnp.zeros_like(away)
    for spread in range(-REACH, REACH + 1):
        slot = jnp.where(away == spread, slots[spread + REACH], slot)
    index = jnp.where(has_peer, slot * count + peer % count, -1).reshape(-1).astype(jnp.int32)
    core_ref = core.astype(jnp.int32).reshape(1)

    acc = inner(xb, band)
    blocks, pooled, to_partner, to_cross = outer(
        index, occupancy, core_ref, (faces, back, ahead, partner, relay), xb, acc, band, band_z,
        bias, pool, pick, latent, proj, norm_gain[None, :],
    )
    from_cross = crossed(to_cross)
    from_partner = swapped(to_partner)
    query, state, peak = own_attention(occupancy, core_ref, to_partner, to_cross, wq, wk, wv_t)
    conv_out = restore(blocks)
    shared = (query, state, peak, wk, wv_t, wo_t, latent_t, proj_t, pooled)
    first = side_attention(1 - core_ref, from_partner, *shared, None)
    tokens_out = side_attention(core_ref, from_cross, *shared, first)
    return (conv_out, tokens_out)


def solution(mesh):
    return jax.shard_map(
        local,
        mesh=mesh,
        in_specs=(
            P(AXES, None, None),
            P(AXES),
            P(AXES, None),
            P(),
            P(),
            P(AXES, None),
            P(),
            P(),
            P(),
            P(),
        ),
        out_specs=(P(AXES, None, None), P(None, AXES)),
        check_vma=False,
    )
```

```python
import math

import jax
import jax.numpy as jnp
import numpy as np
from jax import lax
from jax.experimental import pallas as pl
from jax.experimental.pallas import tpu as pltpu
from jax.sharding import PartitionSpec as P

HD = 64
WIN = 1024
REACH = 2
AXES = ("space", "chan")
NEG = -1e30
TILES = 96
F32 = jnp.float32
BF16 = jnp.bfloat16
VM = pltpu.VMEM
NT = (((1,), (1,)), ((), ()))
SCALE = HD ** (-0.5) * math.log2(math.e)
LIMIT = pltpu.CompilerParams(vmem_limit_bytes=20 << 20)


def vmem(count):
    return [pl.BlockSpec(memory_space=pltpu.VMEM)] * count


def smem(count):
    return [pl.BlockSpec(memory_space=pltpu.SMEM)] * count


def anyspace(count):
    return [pl.BlockSpec(memory_space=pl.ANY)] * count


def cost(flops, moved, trans=0):
    return pl.CostEstimate(flops=flops, bytes_accessed=moved, transcendentals=trans)


def swap_blocks(four):
    lane = lax.broadcasted_iota(jnp.int32, four[0].shape, 1)
    low = lane < 64
    even = (lane // 32) % 2 == 0
    half = []
    for a, b in ((0, 2), (1, 3)):
        half.append(jnp.where(low, four[a], pltpu.roll(four[b], 64, 1)))
        half.append(jnp.where(low, pltpu.roll(four[a], 64, 1), four[b]))
    a0, a2, a1, a3 = half
    return [
        jnp.where(even, a0, pltpu.roll(a1, 32, 1)),
        jnp.where(even, pltpu.roll(a0, 96, 1), a1),
        jnp.where(even, a2, pltpu.roll(a3, 32, 1)),
        jnp.where(even, pltpu.roll(a2, 96, 1), a3),
    ]


def lanes_of(half):
    return slice(128 * half, 128 * half + 128)


def prep_kernel(occ, feat, order, xb, faces, masked):
    for b in range(16):
        rows = feat[b].astype(F32) * occ[b].astype(F32)
        masked[32 * b : 32 * b + 32, :] = rows.astype(BF16)
    for two in range(2):
        found = lax.dot_general(
            order[...], masked[256 * two : 256 * two + 256, :], NT, preferred_element_type=F32
        )
        for g in (2 * two, 2 * two + 1):
            sheets = [found[64 * z : 64 * z + 64, lanes_of(g % 2)] for z in range(8)]
            for face, z in ((0, 0), (1, 7)):
                for xq in range(4):
                    tile = jnp.concatenate(
                        [sheets[z][8 * xq : 8 * xq + 8], sheets[z][8 * xq + 32 : 8 * xq + 40]],
                        axis=1,
                    )
                    faces[64 + (2 * g + face) * 4 + xq] = tile.astype(BF16)
            for half in range(2):
                for j, block in enumerate(swap_blocks(sheets[4 * half : 4 * half + 4])):
                    b = 4 * g + j
                    xb[half, b] = block
                    faces[4 * b, :, lanes_of(half)] = block[56:64].astype(BF16)
                    faces[4 * b + 1, :, lanes_of(half)] = block[0:8].astype(BF16)
    for b in range(16):
        for half in range(2):
            for face, y in ((2, 7), (3, 0)):
                sheet = xb[half, b, pl.ds(y, 8, stride=8), :]
                faces[4 * b + face, :, lanes_of(half)] = sheet.astype(BF16)


def prep(occ, feat):
    order = np.zeros((512, 512), np.float32)
    at = np.arange(512)
    order[at, at % 64 * 8 + at // 64] = 1.0
    return pl.pallas_call(
        prep_kernel,
        name="prep",
        out_shape=(
            jax.ShapeDtypeStruct((2, 16, 64, 128), F32),
            jax.ShapeDtypeStruct((TILES, 8, 256), BF16),
        ),
        in_specs=smem(1) + vmem(2),
        out_specs=tuple(vmem(2)),
        scratch_shapes=[VM((512, 512), BF16)],
        compiler_params=LIMIT,
        cost_estimate=cost(1 << 28, 2 << 20),
    )(occ, feat, jnp.asarray(order, BF16))


def shifted_rows(tile, step):
    if step == 0:
        return tile
    row = lax.broadcasted_iota(jnp.int32, tile.shape, 0) % 8
    if step < 0:
        moved = pltpu.roll(tile, 1, 0)
        return jnp.where(row == 0, 0.0, moved)
    moved = pltpu.roll(tile, tile.shape[0] - 1, 0)
    return jnp.where(row == 7, 0.0, moved)


def joined(pair, *at):
    return jnp.concatenate([pair[(0, *at)], pair[(1, *at)]], axis=1)


def write_patches(lhs, brick, tiles):
    zero = jnp.zeros((8, 256), F32)
    rows = pl.ds(pl.multiple_of(brick * 64, 64), 64)
    for dy in (-1, 0, 1):
        moved = [shifted_rows(t, dy) for t in tiles]
        for dx in (-1, 0, 1):
            picked = [moved[x + dx] if 0 <= x + dx < 8 else zero for x in range(8)]
            tap = (dx + 1) * 3 + dy + 1
            lhs[rows, 256 * tap : 256 * tap + 256] = jnp.concatenate(picked, axis=0).astype(BF16)


def turn(eye, array):
    return lax.dot_general(eye, array, NT, preferred_element_type=F32).astype(BF16)


def weights_kernel(
    conv, spread, qkv, out_weight, latent, token_proj,
    band, band_z, wv_t, wo_t, latent_t, proj_t, wide,
):
    for tap in range(27):
        wide[32 * tap : 32 * tap + 32, :] = jnp.dot(
            conv[tap].astype(F32).T.astype(BF16), spread[...], preferred_element_type=F32
        )
    block = lax.broadcasted_iota(jnp.int32, (32, 256), 1) // 32

    def per_tap(t, carry):
        base = [
            wide[pl.ds(pl.multiple_of((t * 3 + k) * 32, 32), 32), :] for k in range(3)
        ]
        for z in range(8):
            value = jnp.where(block == z, base[1], 0.0)
            value = jnp.where(block == z + 1, base[0], value)
            value = jnp.where(block == z - 1, base[2], value)
            band[pl.ds(pl.multiple_of(t * 256 + 32 * z, 32), 32), :] = value.astype(BF16)
        return carry

    lax.fori_loop(0, 9, per_tap, 0)
    for dy in range(3):
        for face, k in ((0, 0), (1, 2)):
            value = jnp.zeros((32, 256), F32)
            for dx in range(3):
                start = ((dx * 3 + dy) * 3 + k) * 32
                value = jnp.where(block == 2 * dx + face, wide[start : start + 32, :], value)
            for j in range(4):
                start = dy * 256 + 128 * face + 32 * j
                band_z[start : start + 32, :] = value.astype(BF16)
    row = lax.broadcasted_iota(jnp.int32, (512, 512), 0)
    col = lax.broadcasted_iota(jnp.int32, (512, 512), 1)
    eye = jnp.where(row == col, 1.0, 0.0).astype(BF16)
    wv_t[...] = turn(eye, qkv[2])
    wo_t[...] = turn(eye, out_weight[...])
    latent_t[...] = turn(eye, latent[...])
    proj_t[...] = turn(
        eye, jnp.concatenate([token_proj[...], jnp.zeros((96, 512), BF16)], axis=0)
    )


def weights(conv_weight, qkv, out_weight, latent, token_proj):
    spread = jnp.asarray(np.tile(np.eye(32, dtype=np.float32), (1, 8)), BF16)
    return pl.pallas_call(
        weights_kernel,
        name="weights",
        out_shape=(
            jax.ShapeDtypeStruct((2304, 256), BF16),
            jax.ShapeDtypeStruct((768, 256), BF16),
            jax.ShapeDtypeStruct((512, 512), BF16),
            jax.ShapeDtypeStruct((512, 512), BF16),
            jax.ShapeDtypeStruct((512, 1024), BF16),
            jax.ShapeDtypeStruct((512, 128), BF16),
        ),
        in_specs=vmem(6),
        out_specs=tuple(vmem(6)),
        scratch_shapes=[VM((864, 256), F32)],
        compiler_params=LIMIT,
        cost_estimate=cost(1 << 31, 8 << 20),
    )(conv_weight, spread, qkv, out_weight, latent, token_proj)


def inner_kernel(xb, band, acc, lhs):
    def per_brick(b, carry):
        write_patches(lhs, b, [joined(xb, b, slice(8 * x, 8 * x + 8)) for x in range(8)])
        return carry

    lax.fori_loop(0, 16, per_brick, 0)

    def per_rows(i, carry):
        rows = pl.ds(pl.multiple_of(i * 512, 512), 512)
        acc[rows, :] = jnp.dot(lhs[rows, :], band[...], preferred_element_type=F32)
        return carry

    lax.fori_loop(0, 2, per_rows, 0)


def inner(xb, band):
    return pl.pallas_call(
        inner_kernel,
        name="inner",
        out_shape=jax.ShapeDtypeStruct((1024, 256), F32),
        in_specs=vmem(2),
        out_specs=vmem(1)[0],
        scratch_shapes=[VM((1024, 2304), BF16)],
        compiler_params=LIMIT,
        cost_estimate=cost(2 * 1024 * 2304 * 256, 4 << 20),
    )(xb, band)


def outer_kernel(
    neighbours, occ, me, own, back, ahead, partner, relay, xb, acc, band, band_z, bias, pool, pick,
    latent, proj, gain,
    blocks, pooled, to_partner, to_cross,
    table, store, lhs, flat, edges, sums, halves, sems,
):
    copies = [
        pltpu.make_async_copy(ref, store.at[slot], sems.at[slot])
        for slot, ref in enumerate((own, back, ahead, partner, relay))
    ]
    for copy in copies:
        copy.start()
    core = me[0] % 2
    for away, slot in enumerate((1, 4 - core, 0, 3 + core, 2)):
        table[away] = slot
    for copy in copies:
        copy.wait()
    lane = lax.broadcasted_iota(jnp.int32, (8, 256), 1) % 128 // 32

    def where_from(b, face):
        peer = neighbours[b, face]
        valid = (peer >= 0).astype(F32)
        peer = jnp.maximum(peer, 0)
        away = jnp.clip(peer // 16 - me[0], -REACH, REACH)
        return table[away + REACH], peer % 16, valid

    def gather(b, carry):
        for face in range(4):
            slot, brick, valid = where_from(b, face)
            tile = store[slot, brick * 4 + face].astype(F32) * valid
            flat[face, pl.ds(pl.multiple_of(b * 8, 8), 8), :] = tile
        low, high = [], []
        for face, into in ((0, low), (1, high)):
            slot, brick, valid = where_from(b, 4 + face)
            base = 64 + (brick // 4 * 2 + (1 - face)) * 4
            mask = jnp.where(lane == brick % 4, valid, 0.0)
            for xq in range(4):
                into.append(store[slot, base + xq].astype(F32) * mask)
        tiles = []
        for x in range(8):
            part = lanes_of(x // 4)
            tiles.append(jnp.concatenate([low[x % 4][:, part], high[x % 4][:, part]], axis=1))
        rows = pl.ds(pl.multiple_of(b * 64, 64), 64)
        for dy in (-1, 0, 1):
            moved = [shifted_rows(t, dy) for t in tiles]
            start = 256 * (dy + 1)
            lhs[rows, start : start + 256] = jnp.concatenate(moved, axis=0).astype(BF16)
        return carry

    lax.fori_loop(0, 16, gather, 0)
    for face in range(4):
        sheet = flat[face]
        side = 0 if face % 2 == 0 else 2
        total = None
        for step in (-1, 0, 1):
            tap = side * 3 + step + 1 if face < 2 else (step + 1) * 3 + side
            part = jnp.dot(
                shifted_rows(sheet, step).astype(BF16),
                band[256 * tap : 256 * tap + 256, :],
                preferred_element_type=F32,
            )
            total = part if total is None else total + part
        edges[face] = total
    for i in range(2):
        rows = slice(512 * i, 512 * i + 512)
        sums[rows, :] = jnp.dot(lhs[rows, :], band_z[...], preferred_element_type=F32)
    row = lax.broadcasted_iota(jnp.int32, (8, 256), 0)
    one = lax.broadcasted_iota(jnp.int32, (8, 128), 1)

    def finish(b, alive):
        start = pl.multiple_of(b * 64, 64)
        sheet_rows = pl.ds(pl.multiple_of(b * 8, 8), 8)
        y_low, y_high = edges[2, sheet_rows, :], edges[3, sheet_rows, :]
        done = []
        for x in range(8):
            tile_rows = pl.ds(start + 8 * x, 8)
            rim = pltpu.roll(sums[tile_rows, 0:128], 64, 1)
            if x > 0:
                rim = rim + sums[pl.ds(start + 8 * x - 8, 8), 0:128]
            if x < 7:
                rim = rim + sums[pl.ds(start + 8 * x + 8, 8), 128:256]
            rim = jnp.concatenate(
                [
                    jnp.where(one < 32, rim, 0.0),
                    jnp.where(one >= 96, pltpu.roll(rim, 64, 1), 0.0),
                ],
                axis=1,
            )
            total = acc[tile_rows, :] + rim
            total = total + jnp.where(row == 0, y_low[x : x + 1, :], 0.0)
            total = total + jnp.where(row == 7, y_high[x : x + 1, :], 0.0)
            if x == 0:
                total = total + edges[0, sheet_rows, :]
            if x == 7:
                total = total + edges[1, sheet_rows, :]
            value = total + bias[...]
            kept = joined(xb, b, slice(8 * x, 8 * x + 8))
            done.append(alive * (kept + value / (1.0 + jnp.exp(-value))))
        block = jnp.concatenate(done, axis=0).astype(BF16)
        for half in range(2):
            blocks[half, b] = block[:, lanes_of(half)].astype(F32)
        cells = jnp.dot(pool[...], block, preferred_element_type=F32) * pick[...]
        cells = cells[:, :128] + cells[:, 128:]
        cells = cells + pltpu.roll(cells, 64, 1)
        cells = cells + pltpu.roll(cells, 32, 1)
        pooled[pl.ds(start, 64), :] = cells.astype(BF16)

    def finish_two(i, carry):
        for k in range(2):
            finish(2 * i + k, occ[2 * i + k].astype(F32))
        return carry

    lax.fori_loop(0, 8, finish_two, 0)

    def norm(i, carry):
        rows = pl.ds(pl.multiple_of(i * 256, 256), 256)
        lifted = jnp.dot(pooled[rows, 0:32], proj[...], preferred_element_type=F32)
        mixed = latent[rows, :].astype(F32) + lifted
        scale = lax.rsqrt(jnp.mean(mixed * mixed, axis=-1, keepdims=True) + 1e-06)
        halves[i // 2, pl.ds(pl.multiple_of(i % 2 * 256, 256), 256), :] = (
            mixed * scale * gain[...]
        ).astype(BF16)
        return carry

    lax.fori_loop(0, 4, norm, 0)
    flag_row = lax.broadcasted_iota(jnp.int32, (16, 512), 0)
    flag_lane = lax.broadcasted_iota(jnp.int32, (16, 512), 1) // 64
    for half in range(2):
        flags = jnp.zeros((16, 512), F32)
        for b in range(8):
            here = (flag_row == 8 + b) | ((flag_row == 0) & (flag_lane == b))
            flags = jnp.where(here, occ[8 * half + b].astype(F32), flags)
        halves[half, 512:528, :] = flags.astype(BF16)
    out = [
        pltpu.make_async_copy(halves.at[1 - core], to_partner, sems.at[5]),
        pltpu.make_async_copy(halves.at[core], to_cross, sems.at[6]),
    ]
    for copy in out:
        copy.start()
    for copy in out:
        copy.wait()


def outer(neighbours, occ, me, stores, xb, acc, band, band_z, bias, latent, proj, gain):
    return pl.pallas_call(
        outer_kernel,
        name="outer",
        out_shape=(
            jax.ShapeDtypeStruct((2, 16, 64, 128), F32),
            jax.ShapeDtypeStruct((1024, 128), BF16),
            jax.ShapeDtypeStruct((528, 512), BF16),
            jax.ShapeDtypeStruct((528, 512), BF16),
        ),
        in_specs=smem(3) + anyspace(5) + vmem(10),
        out_specs=tuple(vmem(2) + anyspace(2)),
        scratch_shapes=[
            pltpu.SMEM((8,), jnp.int32),
            VM((5, TILES, 8, 256), BF16),
            VM((1024, 768), BF16),
            VM((4, 128, 256), F32),
            VM((4, 128, 256), F32),
            VM((1024, 256), F32),
            VM((2, 528, 512), BF16),
            pltpu.SemaphoreType.DMA((7,)),
        ],
        compiler_params=LIMIT,
        cost_estimate=cost(2 * 1024 * 2304 * 256, 8 << 20, 1 << 18),
    )(neighbours, occ, me, *stores, xb, acc, band, band_z, bias, *pool_tables(), latent, proj, gain)


def restore_kernel(blocks, out, turned):
    row = lax.broadcasted_iota(jnp.int32, (128, 128), 0)
    col = lax.broadcasted_iota(jnp.int32, (128, 128), 1)
    eye = jnp.where(row == col, 1.0, 0.0).astype(BF16)
    for g in range(4):
        for half in range(2):
            four = [blocks[half, 4 * g + j] for j in range(4)]
            for k, sheet in enumerate(swap_blocks(four)):
                turned[g, pl.ds(4 * half + k, 64, stride=8), :] = sheet
    for g in range(4):
        rows = turn(eye, turned[g].astype(BF16))
        for j in range(4):
            out[4 * g + j] = rows[32 * j : 32 * j + 32]


def restore(blocks):
    return pl.pallas_call(
        restore_kernel,
        name="restore",
        out_shape=jax.ShapeDtypeStruct((16, 32, 512), BF16),
        in_specs=vmem(1),
        out_specs=vmem(1)[0],
        scratch_shapes=[VM((4, 512, 128), F32)],
        compiler_params=LIMIT,
        cost_estimate=cost(1 << 20, 2 << 20),
    )(blocks)


def column_max(part):
    return jnp.max(part, axis=0, keepdims=True)


def largest_norm(array):
    row = lax.broadcasted_iota(jnp.int32, (512, 128), 0) // 64
    col = lax.broadcasted_iota(jnp.int32, (512, 128), 1)
    heads = jnp.where(row == col, 1.0, 0.0).astype(BF16)
    return jnp.max(jnp.dot((array * array).astype(BF16), heads, preferred_element_type=F32))


def bounded(query_norm, key_norm, value_peak):
    return (query_norm * key_norm < 3300.0) & (value_peak < 1e12)


def block_max(scores, biases):
    top = None
    for b in range(8):
        part = scores[64 * b : 64 * b + 8]
        for k in range(1, 8):
            part = jnp.maximum(part, scores[64 * b + 8 * k : 64 * b + 8 * k + 8])
        part = part + biases[b]
        top = part if top is None else jnp.maximum(top, part)
    return column_max(top)


def shifted_weights(scores, top, biases):
    parts = [
        jnp.exp2(scores[64 * b : 64 * b + 64] - (top - biases[b])).astype(BF16) for b in range(8)
    ]
    return jnp.concatenate(parts, axis=0)


def keys_values(rows, wk, wv_t, alive, keys, values, raw):
    found = jnp.dot(rows, wk, preferred_element_type=F32)
    for pair in range(4):
        keys[pair] = found[:, 128 * pair : 128 * pair + 128].astype(BF16)
    key_norm = largest_norm(found)
    found = lax.dot_general(wv_t, rows, NT, preferred_element_type=F32)
    ones = jnp.ones((16, 512), F32)
    for head in range(8):
        block = found[64 * head : 64 * head + 64]
        if raw is not None:
            raw[head, 0:64, :] = block.astype(BF16)
            raw[head, 64:80, :] = ones.astype(BF16)
        values[head, 0:64, :] = (block * alive).astype(BF16)
        values[head, 64:80, :] = (ones * alive).astype(BF16)
    return key_norm, jnp.max(jnp.abs(found))


def own_kernel(
    occ, me, to_partner, to_cross, qkv, wv_t, query, state, peak, stats,
    normed, keys, values, raw, sems,
):
    core = me[0] % 2
    copies = [
        pltpu.make_async_copy(to_partner, normed.at[1 - core], sems.at[0]),
        pltpu.make_async_copy(to_cross, normed.at[core], sems.at[1]),
    ]
    for copy in copies:
        copy.start()
    for copy in copies:
        copy.wait()
    lane = lax.broadcasted_iota(jnp.int32, (512, 128), 1)
    alive = [normed[half, 512:528, :].astype(F32)[0:1] for half in range(2)]
    norms, tops = [], []
    for half in range(2):
        rows = normed[half, 0:512, :]
        found = jnp.dot(rows, qkv[0], preferred_element_type=F32) * SCALE
        norms.append(largest_norm(found))
        for head in range(8):
            pair = found[:, 128 * (head // 2) : 128 * (head // 2) + 128]
            keep = lane < 64 if head % 2 == 0 else lane >= 64
            query[head, half] = jnp.where(keep, pair, 0.0).astype(BF16)
        tops.append(
            keys_values(
                rows, qkv[1], wv_t[...], alive[half], keys.at[half], values.at[half], raw.at[half]
            )
        )
    query_norm = jnp.maximum(norms[0], norms[1])
    key_norm = jnp.maximum(tops[0][0], tops[1][0])
    fast = bounded(query_norm, key_norm, jnp.maximum(tops[0][1], tops[1][1]))
    stats[0] = query_norm
    stats[1] = fast.astype(F32)
    row = lax.broadcasted_iota(jnp.int32, (128, 128), 0)
    col = lax.broadcasted_iota(jnp.int32, (128, 128), 1)
    eye = row == col

    @pl.when(fast)
    def plain():
        def per_head(head, carry):
            for half in range(2):
                for tile in range(2):
                    lanes = slice(256 * tile, 256 * tile + 256)
                    parts, own = [], []
                    for chunk in range(2):
                        scores = lax.dot_general(
                            keys[half, head // 2, 256 * chunk : 256 * chunk + 256, :],
                            query[head, half, lanes, :],
                            NT,
                            preferred_element_type=F32,
                        )
                        weights = jnp.exp2(scores)
                        if chunk == tile:
                            for k in (0, 128):
                                block = weights[k : k + 128, k : k + 128]
                                own.append(
                                    jnp.sum(jnp.where(eye, block, 0.0), axis=0, keepdims=True)
                                )
                        parts.append(weights.astype(BF16))
                    out = jnp.dot(
                        values[half, head],
                        jnp.concatenate(parts, axis=0),
                        preferred_element_type=F32,
                    )
                    extra = jnp.concatenate(own, axis=1) * (1.0 - alive[half][:, lanes])
                    out = out + extra * raw[half, head, :, lanes].astype(F32)
                    state[head, half, :, lanes] = out[0:72]
                    peak[head, half, :, lanes] = jnp.zeros((8, 256), F32)
            return carry

        lax.fori_loop(0, 8, per_head, 0)

    @pl.when(jnp.logical_not(fast))
    def general():
        def per_head(head, carry):
            for half in range(2):
                biases = [
                    jnp.where(occ[8 * half + b] > 0, 0.0, NEG).astype(F32) for b in range(8)
                ]
                for tile in range(2):
                    lanes = slice(256 * tile, 256 * tile + 256)
                    scores = lax.dot_general(
                        keys[half, head // 2],
                        query[head, half, lanes, :],
                        NT,
                        preferred_element_type=F32,
                    )
                    selves = []
                    for k in range(2):
                        first = 256 * tile + 128 * k
                        block = scores[first : first + 128, 128 * k : 128 * k + 128]
                        selves.append(column_max(jnp.where(eye, block, NEG)))
                    dead = alive[half][:, lanes] < 0.5
                    own = jnp.where(dead, jnp.concatenate(selves, axis=1), NEG)
                    top = jnp.maximum(block_max(scores, biases), own)
                    out = jnp.dot(
                        values[half, head],
                        shifted_weights(scores, top, biases),
                        preferred_element_type=F32,
                    )
                    extra = jnp.where(dead, jnp.exp2(own - top), 0.0)
                    out = out + extra * raw[half, head, :, lanes].astype(F32)
                    state[head, half, :, lanes] = out[0:72]
                    peak[head, half, :, lanes] = jnp.broadcast_to(top, (8, 256))
            return carry

        lax.fori_loop(0, 8, per_head, 0)


def own_attention(occ, me, to_partner, to_cross, qkv, wv_t):
    return pl.pallas_call(
        own_kernel,
        name="own_attention",
        out_shape=(
            jax.ShapeDtypeStruct((8, 2, 512, 128), BF16),
            jax.ShapeDtypeStruct((8, 2, 72, 512), F32),
            jax.ShapeDtypeStruct((8, 2, 8, 512), F32),
            jax.ShapeDtypeStruct((8,), F32),
        ),
        in_specs=smem(2) + anyspace(2) + vmem(2),
        out_specs=tuple(vmem(3) + smem(1)),
        scratch_shapes=[
            VM((2, 528, 512), BF16),
            VM((2, 4, 512, 128), BF16),
            VM((2, 8, 80, 512), BF16),
            VM((2, 8, 80, 512), BF16),
            pltpu.SemaphoreType.DMA((2,)),
        ],
        compiler_params=LIMIT,
        cost_estimate=cost(6 << 30, 8 << 20, 1 << 22),
    )(occ, me, to_partner, to_cross, qkv, wv_t)


def side_kernel(
    me, stats, remote, query, state, peak, qkv, wv_t, wo_t, latent_t, proj_t, pooled, *rest
):
    last = len(rest) == 5
    if last:
        other, out, keys, values, attended = rest
        half = me[0] % 2
    else:
        out, keys, values, attended = rest
        half = 1 - me[0] % 2
    flags = remote[512:528, :].astype(F32)
    key_norm, value_peak = keys_values(
        remote[0:512, :], qkv[1], wv_t[...], flags[0:1], keys, values, None
    )
    fast = bounded(stats[0], key_norm, value_peak) & (stats[1] > 0.5)

    def finish(head, lanes, total):
        result = total[0:64] / total[64:65]
        attended[pl.ds(pl.multiple_of(head * 64, 64), 64), lanes] = result.astype(BF16)

    @pl.when(fast)
    def plain():
        def per_two(i, carry):
            for head in (2 * i, 2 * i + 1):
                for tile in range(2):
                    lanes = slice(256 * tile, 256 * tile + 256)
                    parts = []
                    for chunk in range(2):
                        scores = lax.dot_general(
                            keys[i, 256 * chunk : 256 * chunk + 256, :],
                            query[head, half, lanes, :],
                            NT,
                            preferred_element_type=F32,
                        )
                        parts.append(jnp.exp2(scores).astype(BF16))
                    total = jnp.dot(
                        values[head], jnp.concatenate(parts, axis=0), preferred_element_type=F32
                    )
                    finish(head, lanes, total[0:72] + state[head, half, :, lanes])
            return carry

        lax.fori_loop(0, 4, per_two, 0)

    @pl.when(jnp.logical_not(fast))
    def general():
        biases = [jnp.where(flags[8 + b : 9 + b, 0:256] > 0.5, 0.0, NEG) for b in range(8)]

        def per_head(head, carry):
            for tile in range(2):
                lanes = slice(256 * tile, 256 * tile + 256)
                scores = lax.dot_general(
                    keys[head // 2], query[head, half, lanes, :], NT, preferred_element_type=F32
                )
                before = peak[head, half, 0:1, lanes]
                top = jnp.maximum(block_max(scores, biases), before)
                total = jnp.dot(
                    values[head], shifted_weights(scores, top, biases), preferred_element_type=F32
                )
                finish(
                    head, lanes, total[0:72] + state[head, half, :, lanes] * jnp.exp2(before - top)
                )
            return carry

        lax.fori_loop(0, 8, per_head, 0)

    place = pl.ds(pl.multiple_of(half * 512, 512), 512)
    mixing = jnp.dot(wo_t[...], attended[...], preferred_element_type=F32)
    lifted = lax.dot_general(proj_t[...], pooled[place, :], NT, preferred_element_type=F32)
    result = ((latent_t[:, place].astype(F32) + lifted) + mixing).astype(BF16)
    if last:
        out[:, place] = result
        out[:, pl.ds(pl.multiple_of((1 - half) * 512, 512), 512)] = other[...]
    else:
        out[...] = result


def side_attention(me, stats, remote, *shared, other):
    last = other is not None
    return pl.pallas_call(
        side_kernel,
        name="last_attention" if last else "side_attention",
        out_shape=jax.ShapeDtypeStruct((512, 1024 if last else 512), BF16),
        in_specs=smem(2) + vmem(len(shared) + 1 + last),
        out_specs=vmem(1)[0],
        scratch_shapes=[
            VM((4, 512, 128), BF16),
            VM((8, 80, 512), BF16),
            VM((512, 512), BF16),
        ],
        compiler_params=LIMIT,
        cost_estimate=cost(4 << 30, 6 << 20, 1 << 21),
    )(me, stats, remote, *shared, *([other] if last else []))


def pool_tables():
    pool = np.zeros((64, 64), np.float32)
    pick = np.zeros((64, 256), np.float32)
    for token in range(64):
        p = (token // 32) * 2 + token // 4 % 2
        q = (token // 16 % 2) * 2 + token // 2 % 2
        r = (token // 8 % 2) * 2 + token % 2
        for x in (2 * p, 2 * p + 1):
            for y in (2 * q, 2 * q + 1):
                pool[token, 8 * x + y] = 0.125
        pick[token, 64 * r : 64 * r + 64] = 1.0
    return jnp.asarray(pool, BF16), jnp.asarray(pick, F32)


def moved(array, by):
    size = lax.axis_size(AXES)
    pairs = [(i, i + by) for i in range(size) if 0 <= i + by < size]
    return lax.ppermute(array, AXES, pairs)


def swapped(array):
    size = lax.axis_size(AXES)
    return lax.ppermute(array, AXES, [(i, i ^ 1) for i in range(size)])


def crossed(array):
    size = lax.axis_size(AXES)
    pairs = [(i, (i - 1) % size if i % 2 == 0 else (i + 1) % size) for i in range(size)]
    return lax.ppermute(array, AXES, pairs)


def local(
    features, occupancy, neighbours, conv_weight, conv_bias, latent, token_proj, norm_gain,
    qkv_weight, out_weight,
):
    me = lax.axis_index(AXES)
    core = me % 2
    me_ref = me.astype(jnp.int32).reshape(1)
    xb, faces = prep(occupancy, features)
    back = moved(faces, 2)
    ahead = moved(faces, -2)
    partner = swapped(faces)
    relay = swapped(jnp.where(core == 1, back, ahead))
    conv_weight, faces_after = lax.optimization_barrier((conv_weight, faces))
    band, band_z, wv_t, wo_t, latent_t, proj_t = weights(
        conv_weight, qkv_weight, out_weight, latent, token_proj
    )
    bias = jnp.tile(conv_bias, 8)[None, :]
    acc = inner(xb, band)
    blocks, pooled, to_partner, to_cross = outer(
        neighbours, occupancy, me_ref, (faces, back, ahead, partner, relay), xb, acc, band, band_z,
        bias, latent, token_proj, norm_gain[None, :],
    )
    from_cross = crossed(to_cross)
    from_partner = swapped(to_partner)
    query, state, peak, stats = own_attention(
        occupancy, me_ref, to_partner, to_cross, qkv_weight, wv_t
    )
    conv_out = restore(blocks)
    shared = (query, state, peak, qkv_weight, wv_t, wo_t, latent_t, proj_t, pooled)
    first = side_attention(me_ref, stats, from_partner, *shared, other=None)
    tokens_out = side_attention(me_ref, stats, from_cross, *shared, other=first)
    return (conv_out, tokens_out)


def solution(mesh):
    return jax.shard_map(
        local,
        mesh=mesh,
        in_specs=(
            P(AXES, None, None),
            P(AXES),
            P(AXES, None),
            P(),
            P(),
            P(AXES, None),
            P(),
            P(),
            P(),
            P(),
        ),
        out_specs=(P(AXES, None, None), P(None, AXES)),
        check_vma=False,
    )
```

```python
import math

import jax
import jax.numpy as jnp
import numpy as np
from jax import lax
from jax.experimental import pallas as pl
from jax.experimental.pallas import tpu as pltpu
from jax.sharding import PartitionSpec as P

HD = 64
WIN = 1024
REACH = 2
AXES = ("space", "chan")
NEG = -1e30
TILES = 88
F32 = jnp.float32
BF16 = jnp.bfloat16
VM = pltpu.VMEM
NT = (((1,), (1,)), ((), ()))
SCALE = HD ** (-0.5) * math.log2(math.e)
LIMIT = pltpu.CompilerParams(vmem_limit_bytes=20 << 20)
PACKED = pltpu.CompilerParams(
    vmem_limit_bytes=20 << 20
)


def vmem(count):
    return [pl.BlockSpec(memory_space=pltpu.VMEM)] * count


def smem(count):
    return [pl.BlockSpec(memory_space=pltpu.SMEM)] * count


def anyspace(count):
    return [pl.BlockSpec(memory_space=pl.ANY)] * count


def cost(flops, moved, trans=0):
    return pl.CostEstimate(flops=flops, bytes_accessed=moved, transcendentals=trans)


def swap_blocks(four):
    lane = lax.broadcasted_iota(jnp.int32, four[0].shape, 1)
    low = lane < 64
    even = (lane // 32) % 2 == 0
    half = []
    for a, b in ((0, 2), (1, 3)):
        half.append(jnp.where(low, four[a], pltpu.roll(four[b], 64, 1)))
        half.append(jnp.where(low, pltpu.roll(four[a], 64, 1), four[b]))
    a0, a2, a1, a3 = half
    return [
        jnp.where(even, a0, pltpu.roll(a1, 32, 1)),
        jnp.where(even, pltpu.roll(a0, 96, 1), a1),
        jnp.where(even, a2, pltpu.roll(a3, 32, 1)),
        jnp.where(even, pltpu.roll(a2, 96, 1), a3),
    ]


def lanes_of(half):
    return slice(128 * half, 128 * half + 128)


def picker(voxel_of, count):
    row = lax.broadcasted_iota(jnp.int32, (count, 512), 0)
    col = lax.broadcasted_iota(jnp.int32, (count, 512), 1)
    return jnp.where(voxel_of(row) == col, 1.0, 0.0).astype(BF16)


def rim_voxel(row):
    z, face, i = row // 32, row // 8 % 4, row % 8
    end = jnp.where(face % 2 == 0, 7, 0)
    return jnp.where(face < 2, 64 * end + 8 * i, 64 * i + 8 * end) + z


def prep_kernel(occ, feat, faces, masked, sems):
    copies = [
        pltpu.make_async_copy(
            feat.at[pl.ds(8 * two, 8)], masked.at[pl.ds(8 * two, 8)], sems.at[two]
        )
        for two in range(2)
    ]
    for copy in copies:
        copy.start()
    rims = picker(rim_voxel, 256)
    ends = picker(lambda row: row % 64 * 8 + row // 64 * 7, 128)
    for two in range(2):
        copies[two].wait()
        rows = []
        for b in range(8 * two, 8 * two + 8):
            rows.append((masked[b].astype(F32) * occ[b].astype(F32)).astype(BF16))
        rows = jnp.concatenate(rows, axis=0)
        rim = lax.dot_general(rims, rows, NT, preferred_element_type=F32)
        end = lax.dot_general(ends, rows, NT, preferred_element_type=F32)
        for g in (2 * two, 2 * two + 1):
            for face in range(2):
                sheet = end[64 * face : 64 * face + 64, lanes_of(g % 2)]
                for x in range(1, 4):
                    tile = jnp.concatenate(
                        [sheet[8 * x : 8 * x + 8], sheet[8 * x + 24 : 8 * x + 32]], axis=1
                    )
                    faces[64 + (2 * g + face) * 3 + x - 1] = tile.astype(BF16)
            for half in range(2):
                four = [
                    rim[32 * z : 32 * z + 32, lanes_of(g % 2)] for z in range(4 * half, 4 * half + 4)
                ]
                for j, block in enumerate(swap_blocks(four)):
                    for face in range(4):
                        faces[4 * (4 * g + j) + face, :, lanes_of(half)] = block[
                            8 * face : 8 * face + 8
                        ].astype(BF16)


def prep(occ, feat):
    return pl.pallas_call(
        prep_kernel,
        name="prep",
        out_shape=jax.ShapeDtypeStruct((TILES, 8, 256), BF16),
        in_specs=smem(1) + [pl.BlockSpec(memory_space=pltpu.HBM)],
        out_specs=vmem(1)[0],
        scratch_shapes=[VM((16, 32, 512), BF16), pltpu.SemaphoreType.DMA((2,))],
        compiler_params=LIMIT,
        cost_estimate=cost(1 << 28, 2 << 20),
    )(occ, feat)


def shifted_rows(tile, step):
    if step == 0:
        return tile
    row = lax.broadcasted_iota(jnp.int32, tile.shape, 0) % 8
    if step < 0:
        moved = pltpu.roll(tile, 1, 0)
        return jnp.where(row == 0, 0.0, moved)
    moved = pltpu.roll(tile, tile.shape[0] - 1, 0)
    return jnp.where(row == 7, 0.0, moved)


def joined(pair, *at):
    return jnp.concatenate([pair[(0, *at)], pair[(1, *at)]], axis=1)


def write_patches(lhs, brick, tiles):
    zero = jnp.zeros((8, 256), F32)
    rows = pl.ds(pl.multiple_of(brick * 64, 64), 64)
    for dy in (-1, 0, 1):
        moved = [shifted_rows(t, dy) for t in tiles]
        for dx in (-1, 0, 1):
            picked = [moved[x + dx] if 0 <= x + dx < 8 else zero for x in range(8)]
            tap = (dx + 1) * 3 + dy + 1
            lhs[rows, 256 * tap : 256 * tap + 256] = jnp.concatenate(picked, axis=0).astype(BF16)


def turn(eye, array):
    return lax.dot_general(eye, array, NT, preferred_element_type=F32).astype(BF16)


def weights_kernel(
    neighbours, me, conv, spread, qkv, out_weight, latent, token_proj,
    source, band, band_z, wv_t, wo_t, latent_t, proj_t, wide, table,
):
    core = me[0] % 2
    for away, slot in enumerate((1, 4 - core, 0, 3 + core, 2)):
        table[away] = slot

    def per_brick(b, carry):
        for face in range(6):
            peer = neighbours[b, face]
            safe = jnp.maximum(peer, 0)
            away = jnp.clip(safe // 16 - me[0], -REACH, REACH)
            start = table[away + REACH] * TILES
            brick = safe % 16
            source[b * 16 + face] = jnp.where(peer >= 0, start + brick * 4, 5 * TILES)
            if face >= 4:
                sheet = start + 64 + (brick // 4 * 2 + (5 - face)) * 3
                source[b * 16 + face + 2] = jnp.where(peer >= 0, sheet, 5 * TILES)
                source[b * 16 + face + 4] = brick % 4
        return carry

    lax.fori_loop(0, 16, per_brick, 0)
    for tap in range(27):
        wide[32 * tap : 32 * tap + 32, :] = jnp.dot(
            conv[tap].astype(F32).T.astype(BF16), spread[...], preferred_element_type=F32
        )
    block = lax.broadcasted_iota(jnp.int32, (32, 256), 1) // 32

    def per_tap(t, carry):
        base = [
            wide[pl.ds(pl.multiple_of((t * 3 + k) * 32, 32), 32), :] for k in range(3)
        ]
        for z in range(8):
            value = jnp.where(block == z, base[1], 0.0)
            value = jnp.where(block == z + 1, base[0], value)
            value = jnp.where(block == z - 1, base[2], value)
            band[pl.ds(pl.multiple_of(t * 256 + 32 * z, 32), 32), :] = value.astype(BF16)
        return carry

    lax.fori_loop(0, 9, per_tap, 0)
    for dy in range(3):
        for face, k in ((0, 0), (1, 2)):
            value = jnp.zeros((32, 256), F32)
            for dx in range(3):
                start = ((dx * 3 + dy) * 3 + k) * 32
                value = jnp.where(block == 2 * dx + face, wide[start : start + 32, :], value)
            for j in range(4):
                start = dy * 256 + 128 * face + 32 * j
                band_z[start : start + 32, :] = value.astype(BF16)
    row = lax.broadcasted_iota(jnp.int32, (512, 512), 0)
    col = lax.broadcasted_iota(jnp.int32, (512, 512), 1)
    eye = jnp.where(row == col, 1.0, 0.0).astype(BF16)
    wv_t[...] = turn(eye, qkv[2])
    wo_t[...] = turn(eye, out_weight[...])
    latent_t[...] = turn(eye, latent[...])
    proj_t[...] = turn(
        eye, jnp.concatenate([token_proj[...], jnp.zeros((96, 512), BF16)], axis=0)
    )


def weights(neighbours, me, conv_weight, qkv, out_weight, latent, token_proj):
    spread = jnp.asarray(np.tile(np.eye(32, dtype=np.float32), (1, 8)), BF16)
    return pl.pallas_call(
        weights_kernel,
        name="weights",
        out_shape=(
            jax.ShapeDtypeStruct((256,), jnp.int32),
            jax.ShapeDtypeStruct((2304, 256), BF16),
            jax.ShapeDtypeStruct((768, 256), BF16),
            jax.ShapeDtypeStruct((512, 512), BF16),
            jax.ShapeDtypeStruct((512, 512), BF16),
            jax.ShapeDtypeStruct((512, 1024), BF16),
            jax.ShapeDtypeStruct((512, 128), BF16),
        ),
        in_specs=smem(2) + vmem(6),
        out_specs=tuple(smem(1) + vmem(6)),
        scratch_shapes=[VM((864, 256), F32), pltpu.SMEM((8,), jnp.int32)],
        compiler_params=LIMIT,
        cost_estimate=cost(1 << 31, 8 << 20),
    )(neighbours, me, conv_weight, spread, qkv, out_weight, latent, token_proj)


def inner_kernel(occ, feat, band, xb, acc, masked, lhs):
    for b in range(16):
        rows = feat[b].astype(F32) * occ[b].astype(F32)
        masked[32 * b : 32 * b + 32, :] = rows.astype(BF16)
    order = picker(lambda row: row % 64 * 8 + row // 64, 512)
    for two in range(2):
        found = lax.dot_general(
            order, masked[256 * two : 256 * two + 256, :], NT, preferred_element_type=F32
        )
        for g in (2 * two, 2 * two + 1):
            for half in range(2):
                four = [
                    found[64 * z : 64 * z + 64, lanes_of(g % 2)]
                    for z in range(4 * half, 4 * half + 4)
                ]
                for j, block in enumerate(swap_blocks(four)):
                    xb[half, 4 * g + j] = block

    def per_brick(b, carry):
        write_patches(lhs, b, [joined(xb, b, slice(8 * x, 8 * x + 8)) for x in range(8)])
        return carry

    lax.fori_loop(0, 16, per_brick, 0)

    def per_rows(i, carry):
        rows = pl.ds(pl.multiple_of(i * 512, 512), 512)
        acc[rows, :] = jnp.dot(lhs[rows, :], band[...], preferred_element_type=F32)
        return carry

    lax.fori_loop(0, 2, per_rows, 0)


def inner(occ, feat, band):
    return pl.pallas_call(
        inner_kernel,
        name="inner",
        out_shape=(
            jax.ShapeDtypeStruct((2, 16, 64, 128), F32),
            jax.ShapeDtypeStruct((1024, 256), F32),
        ),
        in_specs=smem(1) + vmem(2),
        out_specs=tuple(vmem(2)),
        scratch_shapes=[VM((512, 512), BF16), VM((1024, 2304), BF16)],
        compiler_params=LIMIT,
        cost_estimate=cost(2 * 1024 * 2304 * 256, 4 << 20),
    )(occ, feat, band)


def outer_kernel(
    source, occ, me, own, back, ahead, partner, relay, xb, acc, band, band_z, bias, pool, pick,
    latent, proj, gain,
    blocks, pooled, to_partner, to_cross,
    store, lhs, flat, edges, sums, halves, sems,
):
    copies = [
        pltpu.make_async_copy(ref, store.at[pl.ds(slot * TILES, TILES)], sems.at[slot])
        for slot, ref in enumerate((own, back, ahead, partner, relay))
    ]
    for copy in copies:
        copy.start()
    core = me[0] % 2
    store[5 * TILES : 5 * TILES + 8] = jnp.zeros((8, 8, 256), BF16)
    for copy in copies:
        copy.wait()
    lane = lax.broadcasted_iota(jnp.int32, (8, 256), 1) % 128 // 32

    def gather(b, carry):
        for face in range(4):
            tile = store[source[b * 16 + face] + face].astype(F32)
            flat[face, pl.ds(pl.multiple_of(b * 8, 8), 8), :] = tile
        pair = []
        for face in range(2):
            edge = source[b * 16 + 4 + face]
            sheet = source[b * 16 + 6 + face]
            mask = lane == source[b * 16 + 8 + face]
            part = lanes_of(1 - face)
            rim = lane[:, :128] == (3 if face == 0 else 0)
            first = jnp.where(rim, store[edge + 1].astype(F32)[:, part], 0.0)
            final = jnp.where(rim, store[edge].astype(F32)[:, part], 0.0)
            mids = [jnp.where(mask, store[sheet + k].astype(F32), 0.0) for k in range(3)]
            pair.append(
                [first] + [m[:, :128] for m in mids] + [m[:, 128:] for m in mids] + [final]
            )
        tiles = [jnp.concatenate([pair[0][x], pair[1][x]], axis=1) for x in range(8)]
        rows = pl.ds(pl.multiple_of(b * 64, 64), 64)
        for dy in (-1, 0, 1):
            moved = [shifted_rows(t, dy) for t in tiles]
            start = 256 * (dy + 1)
            lhs[rows, start : start + 256] = jnp.concatenate(moved, axis=0).astype(BF16)
        return carry

    lax.fori_loop(0, 16, gather, 0)
    for face in range(4):
        sheet = flat[face]
        side = 0 if face % 2 == 0 else 2
        total = None
        for step in (-1, 0, 1):
            tap = side * 3 + step + 1 if face < 2 else (step + 1) * 3 + side
            part = jnp.dot(
                shifted_rows(sheet, step).astype(BF16),
                band[256 * tap : 256 * tap + 256, :],
                preferred_element_type=F32,
            )
            total = part if total is None else total + part
        edges[face] = total
    sums[...] = jnp.dot(lhs[...], band_z[...], preferred_element_type=F32)
    row = lax.broadcasted_iota(jnp.int32, (8, 256), 0)
    one = lax.broadcasted_iota(jnp.int32, (8, 128), 1)

    def finish(b, alive):
        start = pl.multiple_of(b * 64, 64)
        sheet_rows = pl.ds(pl.multiple_of(b * 8, 8), 8)
        y_low, y_high = edges[2, sheet_rows, :], edges[3, sheet_rows, :]
        done = []
        for x in range(8):
            tile_rows = pl.ds(start + 8 * x, 8)
            rim = pltpu.roll(sums[tile_rows, 0:128], 64, 1)
            if x > 0:
                rim = rim + sums[pl.ds(start + 8 * x - 8, 8), 0:128]
            if x < 7:
                rim = rim + sums[pl.ds(start + 8 * x + 8, 8), 128:256]
            rim = jnp.concatenate(
                [
                    jnp.where(one < 32, rim, 0.0),
                    jnp.where(one >= 96, pltpu.roll(rim, 64, 1), 0.0),
                ],
                axis=1,
            )
            total = acc[tile_rows, :] + rim
            total = total + jnp.where(row == 0, y_low[x : x + 1, :], 0.0)
            total = total + jnp.where(row == 7, y_high[x : x + 1, :], 0.0)
            if x == 0:
                total = total + edges[0, sheet_rows, :]
            if x == 7:
                total = total + edges[1, sheet_rows, :]
            value = total + bias[...]
            kept = joined(xb, b, slice(8 * x, 8 * x + 8))
            done.append(alive * (kept + value / (1.0 + jnp.exp(-value))))
        block = jnp.concatenate(done, axis=0).astype(BF16)
        for half in range(2):
            blocks[half, b] = block[:, lanes_of(half)].astype(F32)
        cells = jnp.dot(pool[...], block, preferred_element_type=F32) * pick[...]
        cells = cells[:, :128] + cells[:, 128:]
        cells = cells + pltpu.roll(cells, 64, 1)
        cells = cells + pltpu.roll(cells, 32, 1)
        pooled[pl.ds(start, 64), :] = cells.astype(BF16)

    def finish_four(i, carry):
        for k in range(4):
            finish(4 * i + k, occ[4 * i + k].astype(F32))
        return carry

    lax.fori_loop(0, 4, finish_four, 0)

    def norm(i, carry):
        rows = pl.ds(pl.multiple_of(i * 256, 256), 256)
        lifted = jnp.dot(pooled[rows, 0:32], proj[...], preferred_element_type=F32)
        mixed = latent[rows, :].astype(F32) + lifted
        scale = lax.rsqrt(jnp.mean(mixed * mixed, axis=-1, keepdims=True) + 1e-06)
        halves[i // 2, pl.ds(pl.multiple_of(i % 2 * 256, 256), 256), :] = (
            mixed * scale * gain[...]
        ).astype(BF16)
        return carry

    lax.fori_loop(0, 4, norm, 0)
    flag_row = lax.broadcasted_iota(jnp.int32, (16, 512), 0)
    flag_lane = lax.broadcasted_iota(jnp.int32, (16, 512), 1) // 64
    for half in range(2):
        flags = jnp.zeros((16, 512), F32)
        for b in range(8):
            here = (flag_row == 8 + b) | ((flag_row == 0) & (flag_lane == b))
            flags = jnp.where(here, occ[8 * half + b].astype(F32), flags)
        halves[half, 512:528, :] = flags.astype(BF16)
    out = [
        pltpu.make_async_copy(halves.at[1 - core], to_partner, sems.at[5]),
        pltpu.make_async_copy(halves.at[core], to_cross, sems.at[6]),
    ]
    for copy in out:
        copy.start()
    for copy in out:
        copy.wait()


def outer(source, occ, me, stores, xb, acc, band, band_z, bias, latent, proj, gain):
    return pl.pallas_call(
        outer_kernel,
        name="outer",
        out_shape=(
            jax.ShapeDtypeStruct((2, 16, 64, 128), F32),
            jax.ShapeDtypeStruct((1024, 128), BF16),
            jax.ShapeDtypeStruct((528, 512), BF16),
            jax.ShapeDtypeStruct((528, 512), BF16),
        ),
        in_specs=smem(3) + anyspace(5) + vmem(10),
        out_specs=tuple(vmem(2) + anyspace(2)),
        scratch_shapes=[
            VM((5 * TILES + 8, 8, 256), BF16),
            VM((1024, 768), BF16),
            VM((4, 128, 256), F32),
            VM((4, 128, 256), F32),
            VM((1024, 256), F32),
            VM((2, 528, 512), BF16),
            pltpu.SemaphoreType.DMA((7,)),
        ],
        compiler_params=LIMIT,
        cost_estimate=cost(2 * 1024 * 2304 * 256, 8 << 20, 1 << 18),
    )(source, occ, me, *stores, xb, acc, band, band_z, bias, *pool_tables(), latent, proj, gain)


def restore_kernel(blocks, out, turned):
    row = lax.broadcasted_iota(jnp.int32, (128, 128), 0)
    col = lax.broadcasted_iota(jnp.int32, (128, 128), 1)
    eye = jnp.where(row == col, 1.0, 0.0).astype(BF16)
    for g in range(4):
        for half in range(2):
            four = [blocks[half, 4 * g + j] for j in range(4)]
            for k, sheet in enumerate(swap_blocks(four)):
                turned[g, pl.ds(4 * half + k, 64, stride=8), :] = sheet
    for g in range(4):
        rows = turn(eye, turned[g].astype(BF16))
        for j in range(4):
            out[4 * g + j] = rows[32 * j : 32 * j + 32]


def restore(blocks):
    return pl.pallas_call(
        restore_kernel,
        name="restore",
        out_shape=jax.ShapeDtypeStruct((16, 32, 512), BF16),
        in_specs=vmem(1),
        out_specs=vmem(1)[0],
        scratch_shapes=[VM((4, 512, 128), F32)],
        compiler_params=LIMIT,
        cost_estimate=cost(1 << 20, 2 << 20),
    )(blocks)


def column_max(part):
    return jnp.max(part, axis=0, keepdims=True)


def in_range(total):
    return jnp.where((total > 2.0**-60) & (total < 2.0**60), 1.0, 0.0)


def block_max(scores, biases):
    top = None
    for b in range(8):
        part = scores[64 * b : 64 * b + 8]
        for k in range(1, 8):
            part = jnp.maximum(part, scores[64 * b + 8 * k : 64 * b + 8 * k + 8])
        part = part + biases[b]
        top = part if top is None else jnp.maximum(top, part)
    return column_max(top)


def shifted_weights(scores, top, biases):
    parts = [
        jnp.exp2(scores[64 * b : 64 * b + 64] - (top - biases[b])).astype(BF16) for b in range(8)
    ]
    return jnp.concatenate(parts, axis=0)


def keys_values(rows, wk, wv_t, alive, keys, values, raw):
    found = jnp.dot(rows, wk, preferred_element_type=F32)
    for pair in range(4):
        keys[pair] = found[:, 128 * pair : 128 * pair + 128].astype(BF16)
    found = lax.dot_general(wv_t, rows, NT, preferred_element_type=F32)
    ones = jnp.ones((16, 512), F32)
    for head in range(8):
        block = found[64 * head : 64 * head + 64]
        if raw is not None:
            raw[head, 0:64, :] = block.astype(BF16)
            raw[head, 64:80, :] = ones.astype(BF16)
        values[head, 0:64, :] = (block * alive).astype(BF16)
        values[head, 64:80, :] = (ones * alive).astype(BF16)
    return jnp.max(jnp.abs(found))


def own_kernel(
    occ, me, to_partner, to_cross, qkv, wv_t, query, state, peak, stats,
    normed, keys, values, raw, even, odd, sems,
):
    core = me[0] % 2
    copies = [
        pltpu.make_async_copy(to_partner, normed.at[1 - core], sems.at[0]),
        pltpu.make_async_copy(to_cross, normed.at[core], sems.at[1]),
    ]
    for copy in copies:
        copy.start()
    for copy in copies:
        copy.wait()
    lane = lax.broadcasted_iota(jnp.int32, (512, 128), 1)
    alive = [normed[half, 512:528, :].astype(F32)[0:1] for half in range(2)]
    tops = []
    for half in range(2):
        rows = normed[half, 0:512, :]
        found = jnp.dot(rows, qkv[0], preferred_element_type=F32) * SCALE
        for head in range(8):
            pair = found[:, 128 * (head // 2) : 128 * (head // 2) + 128]
            keep = lane < 64 if head % 2 == 0 else lane >= 64
            query[head, half] = jnp.where(keep, pair, 0.0).astype(BF16)
        tops.append(
            keys_values(
                rows, qkv[1], wv_t[...], alive[half], keys.at[half], values.at[half], raw.at[half]
            )
        )
    row = lax.broadcasted_iota(jnp.int32, (128, 128), 0)
    col = lax.broadcasted_iota(jnp.int32, (128, 128), 1)
    eye = row == col

    small = jnp.maximum(tops[0], tops[1]) < 1e12
    stats[0] = 0.0

    @pl.when(small)
    def plain():
        def score(head, into, unit):
            for half in (unit // 2,):
                for tile in (unit % 2,):
                    into[2 * half + tile] = lax.dot_general(
                        keys[half, head // 2],
                        query[head, half, 256 * tile : 256 * tile + 256, :],
                        NT,
                        preferred_element_type=F32,
                    )

        def attend(head, scores, unit):
            good = None
            for half in (unit // 2,):
                for tile in (unit % 2,):
                    lanes = slice(256 * tile, 256 * tile + 256)
                    parts, own = [], []
                    for chunk in range(4):
                        weights = jnp.exp2(
                            scores[2 * half + tile, 128 * chunk : 128 * chunk + 128, :]
                        )
                        if chunk // 2 == tile:
                            first = 128 * (chunk % 2)
                            block = weights[:, first : first + 128]
                            own.append(
                                jnp.sum(jnp.where(eye, block, 0.0), axis=0, keepdims=True)
                            )
                        parts.append(weights.astype(BF16))
                    out = jnp.dot(
                        values[half, head],
                        jnp.concatenate(parts, axis=0),
                        preferred_element_type=F32,
                    )
                    extra = jnp.concatenate(own, axis=1) * (1.0 - alive[half][:, lanes])
                    out = out + extra * raw[half, head, :, lanes].astype(F32)
                    state[head, half, :, lanes] = out[0:72]
                    peak[head, half, :, lanes] = jnp.zeros((8, 256), F32)
                    good = in_range(out[64:72])
            return good

        for unit in range(4):
            score(0, even, unit)

        def per_two(i, good):
            for unit in range(4):
                score(2 * i + 1, odd, unit)
                good = good * attend(2 * i, even, unit)
            for unit in range(4):
                score(jnp.minimum(2 * i + 2, 7), even, unit)
                good = good * attend(2 * i + 1, odd, unit)
            return good

        stats[0] = jnp.min(lax.fori_loop(0, 4, per_two, jnp.ones((8, 256), F32)))

    @pl.when(stats[0] < 0.5)
    def general():
        def per_head(head, carry):
            for half in range(2):
                biases = [
                    jnp.where(occ[8 * half + b] > 0, 0.0, NEG).astype(F32) for b in range(8)
                ]
                for tile in range(2):
                    lanes = slice(256 * tile, 256 * tile + 256)
                    scores = lax.dot_general(
                        keys[half, head // 2],
                        query[head, half, lanes, :],
                        NT,
                        preferred_element_type=F32,
                    )
                    selves = []
                    for k in range(2):
                        first = 256 * tile + 128 * k
                        block = scores[first : first + 128, 128 * k : 128 * k + 128]
                        selves.append(column_max(jnp.where(eye, block, NEG)))
                    dead = alive[half][:, lanes] < 0.5
                    own = jnp.where(dead, jnp.concatenate(selves, axis=1), NEG)
                    top = jnp.maximum(block_max(scores, biases), own)
                    out = jnp.dot(
                        values[half, head],
                        shifted_weights(scores, top, biases),
                        preferred_element_type=F32,
                    )
                    extra = jnp.where(dead, jnp.exp2(own - top), 0.0)
                    out = out + extra * raw[half, head, :, lanes].astype(F32)
                    state[head, half, :, lanes] = out[0:72]
                    peak[head, half, :, lanes] = jnp.broadcast_to(top, (8, 256))
            return carry

        lax.fori_loop(0, 8, per_head, 0)


def own_attention(occ, me, to_partner, to_cross, qkv, wv_t):
    return pl.pallas_call(
        own_kernel,
        name="own_attention",
        out_shape=(
            jax.ShapeDtypeStruct((8, 2, 512, 128), BF16),
            jax.ShapeDtypeStruct((8, 2, 72, 512), F32),
            jax.ShapeDtypeStruct((8, 2, 8, 512), F32),
            jax.ShapeDtypeStruct((8,), F32),
        ),
        in_specs=smem(2) + anyspace(2) + vmem(2),
        out_specs=tuple(vmem(3) + smem(1)),
        scratch_shapes=[
            VM((2, 528, 512), BF16),
            VM((2, 4, 512, 128), BF16),
            VM((2, 8, 80, 512), BF16),
            VM((2, 8, 80, 512), BF16),
            VM((4, 512, 256), F32),
            VM((4, 512, 256), F32),
            pltpu.SemaphoreType.DMA((2,)),
        ],
        compiler_params=PACKED,
        cost_estimate=cost(6 << 30, 8 << 20, 1 << 22),
    )(occ, me, to_partner, to_cross, qkv, wv_t)


def side_kernel(
    me, stats, remote, query, state, peak, qkv, wv_t, wo_t, latent_t, proj_t, pooled, *rest
):
    last = len(rest) == 8
    if last:
        other, out, keys, values, attended, even, odd, fast = rest
        half = me[0] % 2
    else:
        out, keys, values, attended, even, odd, fast = rest
        half = 1 - me[0] % 2
    flags = remote[512:528, :].astype(F32)
    value_peak = keys_values(
        remote[0:512, :], qkv[1], wv_t[...], flags[0:1], keys, values, None
    )
    fast[0] = 0.0

    def finish(head, lanes, total):
        result = total[0:64] / total[64:65]
        attended[pl.ds(pl.multiple_of(head * 64, 64), 64), lanes] = result.astype(BF16)

    @pl.when((value_peak < 1e12) & (stats[0] > 0.5))
    def plain():
        def score(pair, into, unit):
            into[unit] = lax.dot_general(
                keys[pair],
                query[2 * pair + unit // 2, half, 256 * (unit % 2) : 256 * (unit % 2) + 256, :],
                NT,
                preferred_element_type=F32,
            )

        def attend(pair, scores, unit):
            lanes = slice(256 * (unit % 2), 256 * (unit % 2) + 256)
            head = 2 * pair + unit // 2
            parts = [
                jnp.exp2(scores[unit, 128 * chunk : 128 * chunk + 128, :]).astype(BF16)
                for chunk in range(4)
            ]
            total = jnp.dot(
                values[head], jnp.concatenate(parts, axis=0), preferred_element_type=F32
            )
            total = total[0:72] + state[head, half, :, lanes]
            finish(head, lanes, total)
            return in_range(total[64:72])

        for unit in range(4):
            score(0, even, unit)

        def per_two(i, good):
            for unit in range(4):
                score(2 * i + 1, odd, unit)
                good = good * attend(2 * i, even, unit)
            for unit in range(4):
                score(jnp.minimum(2 * i + 2, 3), even, unit)
                good = good * attend(2 * i + 1, odd, unit)
            return good

        fast[0] = jnp.min(lax.fori_loop(0, 2, per_two, jnp.ones((8, 256), F32)))

    @pl.when(fast[0] < 0.5)
    def general():
        biases = [jnp.where(flags[8 + b : 9 + b, 0:256] > 0.5, 0.0, NEG) for b in range(8)]

        def per_head(head, carry):
            for tile in range(2):
                lanes = slice(256 * tile, 256 * tile + 256)
                scores = lax.dot_general(
                    keys[head // 2], query[head, half, lanes, :], NT, preferred_element_type=F32
                )
                before = peak[head, half, 0:1, lanes]
                top = jnp.maximum(block_max(scores, biases), before)
                total = jnp.dot(
                    values[head], shifted_weights(scores, top, biases), preferred_element_type=F32
                )
                finish(
                    head, lanes, total[0:72] + state[head, half, :, lanes] * jnp.exp2(before - top)
                )
            return carry

        lax.fori_loop(0, 8, per_head, 0)

    place = pl.ds(pl.multiple_of(half * 512, 512), 512)
    mixing = jnp.dot(wo_t[...], attended[...], preferred_element_type=F32)
    lifted = lax.dot_general(proj_t[...], pooled[place, :], NT, preferred_element_type=F32)
    result = ((latent_t[:, place].astype(F32) + lifted) + mixing).astype(BF16)
    if last:
        out[:, place] = result
        out[:, pl.ds(pl.multiple_of((1 - half) * 512, 512), 512)] = other[...]
    else:
        out[...] = result


def side_attention(me, stats, remote, *shared, other):
    last = other is not None
    return pl.pallas_call(
        side_kernel,
        name="last_attention" if last else "side_attention",
        out_shape=jax.ShapeDtypeStruct((512, 1024 if last else 512), BF16),
        in_specs=smem(2) + vmem(len(shared) + 1 + last),
        out_specs=vmem(1)[0],
        scratch_shapes=[
            VM((4, 512, 128), BF16),
            VM((8, 80, 512), BF16),
            VM((512, 512), BF16),
            VM((4, 512, 256), F32),
            VM((4, 512, 256), F32),
            pltpu.SMEM((1,), F32),
        ],
        compiler_params=PACKED,
        cost_estimate=cost(4 << 30, 6 << 20, 1 << 21),
    )(me, stats, remote, *shared, *([other] if last else []))


def pool_tables():
    pool = np.zeros((64, 64), np.float32)
    pick = np.zeros((64, 256), np.float32)
    for token in range(64):
        p = (token // 32) * 2 + token // 4 % 2
        q = (token // 16 % 2) * 2 + token // 2 % 2
        r = (token // 8 % 2) * 2 + token % 2
        for x in (2 * p, 2 * p + 1):
            for y in (2 * q, 2 * q + 1):
                pool[token, 8 * x + y] = 0.125
        pick[token, 64 * r : 64 * r + 64] = 1.0
    return jnp.asarray(pool, BF16), jnp.asarray(pick, F32)


def moved(array, by):
    size = lax.axis_size(AXES)
    pairs = [(i, i + by) for i in range(size) if 0 <= i + by < size]
    return lax.ppermute(array, AXES, pairs)


def swapped(array):
    size = lax.axis_size(AXES)
    return lax.ppermute(array, AXES, [(i, i ^ 1) for i in range(size)])


def crossed(array):
    size = lax.axis_size(AXES)
    pairs = [(i, (i - 1) % size if i % 2 == 0 else (i + 1) % size) for i in range(size)]
    return lax.ppermute(array, AXES, pairs)


def local(
    features, occupancy, neighbours, conv_weight, conv_bias, latent, token_proj, norm_gain,
    qkv_weight, out_weight,
):
    me = lax.axis_index(AXES)
    core = me % 2
    me_ref = me.astype(jnp.int32).reshape(1)
    faces = prep(occupancy, features)
    back = moved(faces, 2)
    ahead = moved(faces, -2)
    partner = swapped(faces)
    conv_weight, _ = lax.optimization_barrier((conv_weight, faces))
    source, band, band_z, wv_t, wo_t, latent_t, proj_t = weights(
        neighbours, me_ref, conv_weight, qkv_weight, out_weight, latent, token_proj
    )
    bias = jnp.tile(conv_bias, 8)[None, :]
    xb, acc = inner(occupancy, features, band)
    back, ahead, acc, band_z = lax.optimization_barrier((back, ahead, acc, band_z))
    relay = swapped(jnp.where(core == 1, back, ahead))
    blocks, pooled, to_partner, to_cross = outer(
        source, occupancy, me_ref, (faces, back, ahead, partner, relay), xb, acc, band, band_z,
        bias, latent, token_proj, norm_gain[None, :],
    )
    from_cross = crossed(to_cross)
    from_partner = swapped(to_partner)
    query, state, peak, stats = own_attention(
        occupancy, me_ref, to_partner, to_cross, qkv_weight, wv_t
    )
    conv_out = restore(blocks)
    shared = (query, state, peak, qkv_weight, wv_t, wo_t, latent_t, proj_t, pooled)
    first = side_attention(me_ref, stats, from_partner, *shared, other=None)
    tokens_out = side_attention(me_ref, stats, from_cross, *shared, other=first)
    return (conv_out, tokens_out)


def solution(mesh):
    return jax.shard_map(
        local,
        mesh=mesh,
        in_specs=(
            P(AXES, None, None),
            P(AXES),
            P(AXES, None),
            P(),
            P(),
            P(AXES, None),
            P(),
            P(),
            P(),
            P(),
        ),
        out_specs=(P(AXES, None, None), P(None, AXES)),
        check_vma=False,
    )
```

```python
import math

import jax
import jax.numpy as jnp
import numpy as np
from jax import lax
from jax.experimental import pallas as pl
from jax.experimental.pallas import tpu as pltpu
from jax.sharding import PartitionSpec as P

HD = 64
WIN = 1024
REACH = 2
AXES = ("space", "chan")
NEG = -1e30
TILES = 88
F32 = jnp.float32
BF16 = jnp.bfloat16
VM = pltpu.VMEM
NT = (((1,), (1,)), ((), ()))
SCALE = HD ** (-0.5) * math.log2(math.e)
LIMIT = pltpu.CompilerParams(vmem_limit_bytes=20 << 20)
WHOLE = pltpu.CompilerParams(vmem_limit_bytes=63 << 20)
PACKED = pltpu.CompilerParams(
    vmem_limit_bytes=20 << 20
)


def vmem(count):
    return [pl.BlockSpec(memory_space=pltpu.VMEM)] * count


def smem(count):
    return [pl.BlockSpec(memory_space=pltpu.SMEM)] * count


def anyspace(count):
    return [pl.BlockSpec(memory_space=pl.ANY)] * count


def cost(flops, moved, trans=0):
    return pl.CostEstimate(flops=flops, bytes_accessed=moved, transcendentals=trans)


def swap_blocks(four):
    lane = lax.broadcasted_iota(jnp.int32, four[0].shape, 1)
    low = lane < 64
    even = (lane // 32) % 2 == 0
    half = []
    for a, b in ((0, 2), (1, 3)):
        half.append(jnp.where(low, four[a], pltpu.roll(four[b], 64, 1)))
        half.append(jnp.where(low, pltpu.roll(four[a], 64, 1), four[b]))
    a0, a2, a1, a3 = half
    return [
        jnp.where(even, a0, pltpu.roll(a1, 32, 1)),
        jnp.where(even, pltpu.roll(a0, 96, 1), a1),
        jnp.where(even, a2, pltpu.roll(a3, 32, 1)),
        jnp.where(even, pltpu.roll(a2, 96, 1), a3),
    ]


def lanes_of(half):
    return slice(128 * half, 128 * half + 128)


def picker(voxel_of, count):
    row = lax.broadcasted_iota(jnp.int32, (count, 512), 0)
    col = lax.broadcasted_iota(jnp.int32, (count, 512), 1)
    return jnp.where(voxel_of(row) == col, 1.0, 0.0).astype(BF16)


def rim_table():
    table = np.zeros((384, 512), np.float32)
    for row in range(256):
        z, face, i = row // 32, row // 8 % 4, row % 8
        end = 7 * (1 - face % 2)
        table[row, (64 * end + 8 * i if face < 2 else 64 * i + 8 * end) + z] = 1.0
    for row in range(128):
        table[256 + row, row % 64 * 8 + row // 64 * 7] = 1.0
    return jnp.asarray(table, BF16)


def prep_kernel(occ, feat, table, faces, masked, picks, sems):
    copies = [
        pltpu.make_async_copy(
            feat.at[pl.ds(8 * two, 8)], masked.at[pl.ds(8 * two, 8)], sems.at[two]
        )
        for two in range(2)
    ]
    load = pltpu.make_async_copy(table, picks, sems.at[2])
    copies[0].start()
    load.start()
    copies[1].start()
    for two in range(2):
        copies[two].wait()
        if two == 0:
            load.wait()
        rows = []
        for b in range(8 * two, 8 * two + 8):
            rows.append((masked[b].astype(F32) * occ[b].astype(F32)).astype(BF16))
        rows = jnp.concatenate(rows, axis=0)
        found = lax.dot_general(picks[...], rows, NT, preferred_element_type=F32)
        for g in (2 * two, 2 * two + 1):
            for face in range(2):
                sheet = found[256 + 64 * face : 320 + 64 * face, lanes_of(g % 2)]
                for x in range(1, 4):
                    tile = jnp.concatenate(
                        [sheet[8 * x : 8 * x + 8], sheet[8 * x + 24 : 8 * x + 32]], axis=1
                    )
                    faces[64 + (2 * g + face) * 3 + x - 1] = tile.astype(BF16)
            for half in range(2):
                four = [
                    found[32 * z : 32 * z + 32, lanes_of(g % 2)]
                    for z in range(4 * half, 4 * half + 4)
                ]
                for j, block in enumerate(swap_blocks(four)):
                    for face in range(4):
                        faces[4 * (4 * g + j) + face, :, lanes_of(half)] = block[
                            8 * face : 8 * face + 8
                        ].astype(BF16)


def prep(occ, feat):
    return pl.pallas_call(
        prep_kernel,
        name="prep",
        out_shape=jax.ShapeDtypeStruct((TILES, 8, 256), BF16),
        in_specs=smem(1) + [pl.BlockSpec(memory_space=pltpu.HBM)] * 2,
        out_specs=vmem(1)[0],
        scratch_shapes=[
            VM((16, 32, 512), BF16),
            VM((384, 512), BF16),
            pltpu.SemaphoreType.DMA((3,)),
        ],
        compiler_params=WHOLE,
        cost_estimate=cost(1 << 28, 2 << 20),
    )(occ, feat, rim_table())


def choose_kernel(me, back, ahead, out, sems):
    core = me[0] % 2
    for which, ref in ((1, back), (0, ahead)):

        @pl.when(core == which)
        def send(ref=ref):
            copy = pltpu.make_async_copy(ref, out, sems.at[0])
            copy.start()
            copy.wait()


def choose(me, back, ahead):
    return pl.pallas_call(
        choose_kernel,
        name="choose",
        out_shape=jax.ShapeDtypeStruct(back.shape, BF16),
        in_specs=smem(1) + anyspace(2),
        out_specs=anyspace(1)[0],
        scratch_shapes=[pltpu.SemaphoreType.DMA((1,))],
        compiler_params=LIMIT,
        cost_estimate=cost(1 << 10, 1 << 20),
    )(me, back, ahead)


def shifted_rows(tile, step):
    if step == 0:
        return tile
    row = lax.broadcasted_iota(jnp.int32, tile.shape, 0) % 8
    if step < 0:
        moved = pltpu.roll(tile, 1, 0)
        return jnp.where(row == 0, 0.0, moved)
    moved = pltpu.roll(tile, tile.shape[0] - 1, 0)
    return jnp.where(row == 7, 0.0, moved)


def joined(pair, *at):
    return jnp.concatenate([pair[(0, *at)], pair[(1, *at)]], axis=1)


def write_patches(lhs, brick, tiles):
    zero = jnp.zeros((8, 256), F32)
    rows = pl.ds(pl.multiple_of(brick * 64, 64), 64)
    for dy in (-1, 0, 1):
        moved = [shifted_rows(t, dy) for t in tiles]
        for dx in (-1, 0, 1):
            picked = [moved[x + dx] if 0 <= x + dx < 8 else zero for x in range(8)]
            tap = (dx + 1) * 3 + dy + 1
            lhs[rows, 256 * tap : 256 * tap + 256] = jnp.concatenate(picked, axis=0).astype(BF16)


def turn(eye, array):
    return lax.dot_general(eye, array, NT, preferred_element_type=F32).astype(BF16)


def weights_kernel(
    neighbours, me, conv, conv_bias, qkv, out_weight, latent, token_proj,
    source, bias, band, band_z, wv_t, wo_t, latent_t, proj_t, wide, table,
):
    core = me[0] % 2
    for away, slot in enumerate((1, 4 - core, 0, 3 + core, 2)):
        table[away] = slot

    def per_brick(b, carry):
        for face in range(6):
            peer = neighbours[face, b]
            safe = jnp.maximum(peer, 0)
            away = jnp.clip(safe // 16 - me[0], -REACH, REACH)
            start = table[away + REACH] * TILES
            brick = safe % 16
            source[b * 16 + face] = jnp.where(peer >= 0, start + brick * 4, 5 * TILES)
            if face >= 4:
                sheet = start + 64 + (brick // 4 * 2 + (5 - face)) * 3
                source[b * 16 + face + 2] = jnp.where(peer >= 0, sheet, 5 * TILES)
                source[b * 16 + face + 4] = brick % 4
        return carry

    lax.fori_loop(0, 16, per_brick, 0)
    row = lax.broadcasted_iota(jnp.int32, (32, 256), 0)
    col = lax.broadcasted_iota(jnp.int32, (32, 256), 1) % 32
    column = jnp.where(row == col, conv_bias[...], 0.0)
    bias[...] = jnp.sum(column, axis=0, keepdims=True)
    spread = jnp.where(row == col, 1.0, 0.0).astype(BF16)
    for tap in range(27):
        wide[32 * tap : 32 * tap + 32, :] = jnp.dot(
            conv[tap].astype(F32).T.astype(BF16), spread, preferred_element_type=F32
        )
    block = lax.broadcasted_iota(jnp.int32, (32, 256), 1) // 32

    def per_tap(t, carry):
        base = [
            wide[pl.ds(pl.multiple_of((t * 3 + k) * 32, 32), 32), :] for k in range(3)
        ]
        for z in range(8):
            value = jnp.where(block == z, base[1], 0.0)
            value = jnp.where(block == z + 1, base[0], value)
            value = jnp.where(block == z - 1, base[2], value)
            band[pl.ds(pl.multiple_of(t * 256 + 32 * z, 32), 32), :] = value.astype(BF16)
        return carry

    lax.fori_loop(0, 9, per_tap, 0)
    for dy in range(3):
        for face, k in ((0, 0), (1, 2)):
            value = jnp.zeros((32, 256), F32)
            for dx in range(3):
                start = ((dx * 3 + dy) * 3 + k) * 32
                value = jnp.where(block == 2 * dx + face, wide[start : start + 32, :], value)
            for j in range(4):
                start = dy * 256 + 128 * face + 32 * j
                band_z[start : start + 32, :] = value.astype(BF16)
    row = lax.broadcasted_iota(jnp.int32, (512, 512), 0)
    col = lax.broadcasted_iota(jnp.int32, (512, 512), 1)
    eye = jnp.where(row == col, 1.0, 0.0).astype(BF16)
    wv_t[...] = turn(eye, qkv[2])
    wo_t[...] = turn(eye, out_weight[...])
    latent_t[...] = turn(eye, latent[...])
    proj_t[...] = turn(
        eye, jnp.concatenate([token_proj[...], jnp.zeros((96, 512), BF16)], axis=0)
    )


def weights(neighbours, me, conv_weight, conv_bias, qkv, out_weight, latent, token_proj):
    return pl.pallas_call(
        weights_kernel,
        name="weights",
        out_shape=(
            jax.ShapeDtypeStruct((256,), jnp.int32),
            jax.ShapeDtypeStruct((1, 256), F32),
            jax.ShapeDtypeStruct((2304, 256), BF16),
            jax.ShapeDtypeStruct((768, 256), BF16),
            jax.ShapeDtypeStruct((512, 512), BF16),
            jax.ShapeDtypeStruct((512, 512), BF16),
            jax.ShapeDtypeStruct((512, 1024), BF16),
            jax.ShapeDtypeStruct((512, 128), BF16),
        ),
        in_specs=smem(2) + vmem(6),
        out_specs=tuple(smem(1) + vmem(7)),
        scratch_shapes=[VM((864, 256), F32), pltpu.SMEM((8,), jnp.int32)],
        compiler_params=LIMIT,
        cost_estimate=cost(1 << 31, 8 << 20),
    )(neighbours, me, conv_weight, conv_bias, qkv, out_weight, latent, token_proj)


def inner_kernel(occ, feat, band, xb, acc, masked, lhs):
    for b in range(16):
        rows = feat[b].astype(F32) * occ[b].astype(F32)
        masked[32 * b : 32 * b + 32, :] = rows.astype(BF16)
    order = picker(lambda row: row % 64 * 8 + row // 64, 512)
    for two in range(2):
        found = lax.dot_general(
            order, masked[256 * two : 256 * two + 256, :], NT, preferred_element_type=F32
        )
        for g in (2 * two, 2 * two + 1):
            for half in range(2):
                four = [
                    found[64 * z : 64 * z + 64, lanes_of(g % 2)]
                    for z in range(4 * half, 4 * half + 4)
                ]
                for j, block in enumerate(swap_blocks(four)):
                    xb[half, 4 * g + j] = block

    def per_brick(b, carry):
        write_patches(lhs, b, [joined(xb, b, slice(8 * x, 8 * x + 8)) for x in range(8)])
        return carry

    lax.fori_loop(0, 16, per_brick, 0)

    def per_rows(i, carry):
        rows = pl.ds(pl.multiple_of(i * 512, 512), 512)
        acc[rows, :] = jnp.dot(lhs[rows, :], band[...], preferred_element_type=F32)
        return carry

    lax.fori_loop(0, 2, per_rows, 0)


def inner(occ, feat, band):
    return pl.pallas_call(
        inner_kernel,
        name="inner",
        out_shape=(
            jax.ShapeDtypeStruct((2, 16, 64, 128), F32),
            jax.ShapeDtypeStruct((1024, 256), F32),
        ),
        in_specs=smem(1) + vmem(2),
        out_specs=tuple(vmem(2)),
        scratch_shapes=[VM((512, 512), BF16), VM((1024, 2304), BF16)],
        compiler_params=LIMIT,
        cost_estimate=cost(2 * 1024 * 2304 * 256, 4 << 20),
    )(occ, feat, band)


def outer_kernel(
    source, occ, me, own, back, ahead, partner, relay, xb, acc, band, band_z, bias, pool, pick,
    latent, proj, gain,
    blocks, pooled, to_partner, to_cross,
    store, lhs, flat, edges, sums, halves, sems,
):
    copies = [
        pltpu.make_async_copy(ref, store.at[pl.ds(slot * TILES, TILES)], sems.at[slot])
        for slot, ref in enumerate((own, back, ahead, partner, relay))
    ]
    for copy in copies:
        copy.start()
    core = me[0] % 2
    store[5 * TILES : 5 * TILES + 8] = jnp.zeros((8, 8, 256), BF16)
    for copy in copies:
        copy.wait()
    lane = lax.broadcasted_iota(jnp.int32, (8, 256), 1) % 128 // 32

    def gather(b, carry):
        for face in range(4):
            tile = store[source[b * 16 + face] + face].astype(F32)
            flat[face, pl.ds(pl.multiple_of(b * 8, 8), 8), :] = tile
        pair = []
        for face in range(2):
            edge = source[b * 16 + 4 + face]
            sheet = source[b * 16 + 6 + face]
            mask = lane == source[b * 16 + 8 + face]
            part = lanes_of(1 - face)
            rim = lane[:, :128] == (3 if face == 0 else 0)
            first = jnp.where(rim, store[edge + 1].astype(F32)[:, part], 0.0)
            final = jnp.where(rim, store[edge].astype(F32)[:, part], 0.0)
            mids = [jnp.where(mask, store[sheet + k].astype(F32), 0.0) for k in range(3)]
            pair.append(
                [first] + [m[:, :128] for m in mids] + [m[:, 128:] for m in mids] + [final]
            )
        tiles = [jnp.concatenate([pair[0][x], pair[1][x]], axis=1) for x in range(8)]
        rows = pl.ds(pl.multiple_of(b * 64, 64), 64)
        for dy in (-1, 0, 1):
            moved = [shifted_rows(t, dy) for t in tiles]
            start = 256 * (dy + 1)
            lhs[rows, start : start + 256] = jnp.concatenate(moved, axis=0).astype(BF16)
        return carry

    lax.fori_loop(0, 16, gather, 0)
    for face in range(4):
        sheet = flat[face]
        side = 0 if face % 2 == 0 else 2
        total = None
        for step in (-1, 0, 1):
            tap = side * 3 + step + 1 if face < 2 else (step + 1) * 3 + side
            part = jnp.dot(
                shifted_rows(sheet, step).astype(BF16),
                band[256 * tap : 256 * tap + 256, :],
                preferred_element_type=F32,
            )
            total = part if total is None else total + part
        edges[face] = total
    sums[...] = jnp.dot(lhs[...], band_z[...], preferred_element_type=F32)
    row = lax.broadcasted_iota(jnp.int32, (8, 256), 0)
    one = lax.broadcasted_iota(jnp.int32, (8, 128), 1)

    def finish(b, alive):
        start = pl.multiple_of(b * 64, 64)
        sheet_rows = pl.ds(pl.multiple_of(b * 8, 8), 8)
        y_low, y_high = edges[2, sheet_rows, :], edges[3, sheet_rows, :]
        done = []
        for x in range(8):
            tile_rows = pl.ds(start + 8 * x, 8)
            rim = pltpu.roll(sums[tile_rows, 0:128], 64, 1)
            if x > 0:
                rim = rim + sums[pl.ds(start + 8 * x - 8, 8), 0:128]
            if x < 7:
                rim = rim + sums[pl.ds(start + 8 * x + 8, 8), 128:256]
            rim = jnp.concatenate(
                [
                    jnp.where(one < 32, rim, 0.0),
                    jnp.where(one >= 96, pltpu.roll(rim, 64, 1), 0.0),
                ],
                axis=1,
            )
            total = acc[tile_rows, :] + rim
            total = total + jnp.where(row == 0, y_low[x : x + 1, :], 0.0)
            total = total + jnp.where(row == 7, y_high[x : x + 1, :], 0.0)
            if x == 0:
                total = total + edges[0, sheet_rows, :]
            if x == 7:
                total = total + edges[1, sheet_rows, :]
            value = total + bias[...]
            kept = joined(xb, b, slice(8 * x, 8 * x + 8))
            done.append(alive * (kept + value / (1.0 + jnp.exp(-value))))
        block = jnp.concatenate(done, axis=0).astype(BF16)
        for half in range(2):
            blocks[half, b] = block[:, lanes_of(half)].astype(F32)
        cells = jnp.dot(pool[...], block, preferred_element_type=F32) * pick[...]
        cells = cells[:, :128] + cells[:, 128:]
        cells = cells + pltpu.roll(cells, 64, 1)
        cells = cells + pltpu.roll(cells, 32, 1)
        pooled[pl.ds(start, 64), :] = cells.astype(BF16)

    def finish_four(i, carry):
        for k in range(4):
            finish(4 * i + k, occ[4 * i + k].astype(F32))
        return carry

    lax.fori_loop(0, 4, finish_four, 0)

    def norm(i, carry):
        rows = pl.ds(pl.multiple_of(i * 256, 256), 256)
        lifted = jnp.dot(pooled[rows, 0:32], proj[...], preferred_element_type=F32)
        mixed = latent[rows, :].astype(F32) + lifted
        scale = lax.rsqrt(jnp.mean(mixed * mixed, axis=-1, keepdims=True) + 1e-06)
        halves[i // 2, pl.ds(pl.multiple_of(i % 2 * 256, 256), 256), :] = (
            mixed * scale * gain[...]
        ).astype(BF16)
        return carry

    lax.fori_loop(0, 4, norm, 0)
    flag_row = lax.broadcasted_iota(jnp.int32, (16, 512), 0)
    flag_lane = lax.broadcasted_iota(jnp.int32, (16, 512), 1) // 64
    for half in range(2):
        flags = jnp.zeros((16, 512), F32)
        for b in range(8):
            here = (flag_row == 8 + b) | ((flag_row == 0) & (flag_lane == b))
            flags = jnp.where(here, occ[8 * half + b].astype(F32), flags)
        halves[half, 512:528, :] = flags.astype(BF16)
    out = [
        pltpu.make_async_copy(halves.at[1 - core], to_partner, sems.at[5]),
        pltpu.make_async_copy(halves.at[core], to_cross, sems.at[6]),
    ]
    for copy in out:
        copy.start()
    for copy in out:
        copy.wait()


def outer(source, occ, me, stores, xb, acc, band, band_z, bias, latent, proj, gain):
    return pl.pallas_call(
        outer_kernel,
        name="outer",
        out_shape=(
            jax.ShapeDtypeStruct((2, 16, 64, 128), F32),
            jax.ShapeDtypeStruct((1024, 128), BF16),
            jax.ShapeDtypeStruct((528, 512), BF16),
            jax.ShapeDtypeStruct((528, 512), BF16),
        ),
        in_specs=smem(3) + anyspace(5) + vmem(10),
        out_specs=tuple(vmem(2) + anyspace(2)),
        scratch_shapes=[
            VM((5 * TILES + 8, 8, 256), BF16),
            VM((1024, 768), BF16),
            VM((4, 128, 256), F32),
            VM((4, 128, 256), F32),
            VM((1024, 256), F32),
            VM((2, 528, 512), BF16),
            pltpu.SemaphoreType.DMA((7,)),
        ],
        compiler_params=LIMIT,
        cost_estimate=cost(2 * 1024 * 2304 * 256, 8 << 20, 1 << 18),
    )(source, occ, me, *stores, xb, acc, band, band_z, bias, *pool_tables(), latent, proj, gain)


def restore_kernel(blocks, out, turned):
    row = lax.broadcasted_iota(jnp.int32, (128, 128), 0)
    col = lax.broadcasted_iota(jnp.int32, (128, 128), 1)
    eye = jnp.where(row == col, 1.0, 0.0).astype(BF16)
    for g in range(4):
        for half in range(2):
            four = [blocks[half, 4 * g + j] for j in range(4)]
            for k, sheet in enumerate(swap_blocks(four)):
                turned[g, pl.ds(4 * half + k, 64, stride=8), :] = sheet
    for g in range(4):
        rows = turn(eye, turned[g].astype(BF16))
        for j in range(4):
            out[4 * g + j] = rows[32 * j : 32 * j + 32]


def restore(blocks):
    return pl.pallas_call(
        restore_kernel,
        name="restore",
        out_shape=jax.ShapeDtypeStruct((16, 32, 512), BF16),
        in_specs=vmem(1),
        out_specs=vmem(1)[0],
        scratch_shapes=[VM((4, 512, 128), F32)],
        compiler_params=LIMIT,
        cost_estimate=cost(1 << 20, 2 << 20),
    )(blocks)


def column_max(part):
    return jnp.max(part, axis=0, keepdims=True)


def in_range(total):
    return jnp.where((total > 2.0**-60) & (total < 2.0**60), 1.0, 0.0)


def block_max(scores, biases):
    top = None
    for b in range(8):
        part = scores[64 * b : 64 * b + 8]
        for k in range(1, 8):
            part = jnp.maximum(part, scores[64 * b + 8 * k : 64 * b + 8 * k + 8])
        part = part + biases[b]
        top = part if top is None else jnp.maximum(top, part)
    return column_max(top)


def shifted_weights(scores, top, biases):
    parts = [
        jnp.exp2(scores[64 * b : 64 * b + 64] - (top - biases[b])).astype(BF16) for b in range(8)
    ]
    return jnp.concatenate(parts, axis=0)


def keys_values(rows, wk, wv_t, alive, keys, values, raw):
    found = jnp.dot(rows, wk, preferred_element_type=F32)
    for pair in range(4):
        keys[pair] = found[:, 128 * pair : 128 * pair + 128].astype(BF16)
    found = lax.dot_general(wv_t, rows, NT, preferred_element_type=F32)
    ones = jnp.ones((16, 512), F32)
    for head in range(8):
        block = found[64 * head : 64 * head + 64]
        if raw is not None:
            raw[head, 0:64, :] = block.astype(BF16)
            raw[head, 64:80, :] = ones.astype(BF16)
        values[head, 0:64, :] = (block * alive).astype(BF16)
        values[head, 64:80, :] = (ones * alive).astype(BF16)
    return jnp.max(jnp.abs(found))


def own_kernel(
    occ, me, to_partner, to_cross, qkv, wv_t, query, state, peak, stats,
    normed, keys, values, raw, even, odd, sems,
):
    core = me[0] % 2
    copies = [
        pltpu.make_async_copy(to_partner, normed.at[1 - core], sems.at[0]),
        pltpu.make_async_copy(to_cross, normed.at[core], sems.at[1]),
    ]
    for copy in copies:
        copy.start()
    for copy in copies:
        copy.wait()
    lane = lax.broadcasted_iota(jnp.int32, (512, 128), 1)
    alive = [normed[half, 512:528, :].astype(F32)[0:1] for half in range(2)]
    tops = []
    for half in range(2):
        rows = normed[half, 0:512, :]
        found = jnp.dot(rows, qkv[0], preferred_element_type=F32) * SCALE
        for head in range(8):
            pair = found[:, 128 * (head // 2) : 128 * (head // 2) + 128]
            keep = lane < 64 if head % 2 == 0 else lane >= 64
            query[head, half] = jnp.where(keep, pair, 0.0).astype(BF16)
        tops.append(
            keys_values(
                rows, qkv[1], wv_t[...], alive[half], keys.at[half], values.at[half], raw.at[half]
            )
        )
    row = lax.broadcasted_iota(jnp.int32, (128, 128), 0)
    col = lax.broadcasted_iota(jnp.int32, (128, 128), 1)
    eye = row == col

    small = jnp.maximum(tops[0], tops[1]) < 1e12
    stats[0] = 0.0

    @pl.when(small)
    def plain():
        def score(head, into, unit):
            for half in (unit // 2,):
                for tile in (unit % 2,):
                    into[2 * half + tile] = lax.dot_general(
                        keys[half, head // 2],
                        query[head, half, 256 * tile : 256 * tile + 256, :],
                        NT,
                        preferred_element_type=F32,
                    )

        def attend(head, scores, unit):
            good = None
            for half in (unit // 2,):
                for tile in (unit % 2,):
                    lanes = slice(256 * tile, 256 * tile + 256)
                    parts, own = [], []
                    for chunk in range(4):
                        weights = jnp.exp2(
                            scores[2 * half + tile, 128 * chunk : 128 * chunk + 128, :]
                        )
                        if chunk // 2 == tile:
                            first = 128 * (chunk % 2)
                            block = weights[:, first : first + 128]
                            own.append(
                                jnp.sum(jnp.where(eye, block, 0.0), axis=0, keepdims=True)
                            )
                        parts.append(weights.astype(BF16))
                    out = jnp.dot(
                        values[half, head],
                        jnp.concatenate(parts, axis=0),
                        preferred_element_type=F32,
                    )
                    extra = jnp.concatenate(own, axis=1) * (1.0 - alive[half][:, lanes])
                    out = out + extra * raw[half, head, :, lanes].astype(F32)
                    state[head, half, :, lanes] = out[0:72]
                    peak[head, half, :, lanes] = jnp.zeros((8, 256), F32)
                    good = in_range(out[64:72])
            return good

        for unit in range(4):
            score(0, even, unit)

        def per_two(i, good):
            for unit in range(4):
                score(2 * i + 1, odd, unit)
                good = good * attend(2 * i, even, unit)
            for unit in range(4):
                score(jnp.minimum(2 * i + 2, 7), even, unit)
                good = good * attend(2 * i + 1, odd, unit)
            return good

        stats[0] = jnp.min(lax.fori_loop(0, 4, per_two, jnp.ones((8, 256), F32)))

    @pl.when(stats[0] < 0.5)
    def general():
        def per_head(head, carry):
            for half in range(2):
                biases = [
                    jnp.where(occ[8 * half + b] > 0, 0.0, NEG).astype(F32) for b in range(8)
                ]
                for tile in range(2):
                    lanes = slice(256 * tile, 256 * tile + 256)
                    scores = lax.dot_general(
                        keys[half, head // 2],
                        query[head, half, lanes, :],
                        NT,
                        preferred_element_type=F32,
                    )
                    selves = []
                    for k in range(2):
                        first = 256 * tile + 128 * k
                        block = scores[first : first + 128, 128 * k : 128 * k + 128]
                        selves.append(column_max(jnp.where(eye, block, NEG)))
                    dead = alive[half][:, lanes] < 0.5
                    own = jnp.where(dead, jnp.concatenate(selves, axis=1), NEG)
                    top = jnp.maximum(block_max(scores, biases), own)
                    out = jnp.dot(
                        values[half, head],
                        shifted_weights(scores, top, biases),
                        preferred_element_type=F32,
                    )
                    extra = jnp.where(dead, jnp.exp2(own - top), 0.0)
                    out = out + extra * raw[half, head, :, lanes].astype(F32)
                    state[head, half, :, lanes] = out[0:72]
                    peak[head, half, :, lanes] = jnp.broadcast_to(top, (8, 256))
            return carry

        lax.fori_loop(0, 8, per_head, 0)


def own_attention(occ, me, to_partner, to_cross, qkv, wv_t):
    return pl.pallas_call(
        own_kernel,
        name="own_attention",
        out_shape=(
            jax.ShapeDtypeStruct((8, 2, 512, 128), BF16),
            jax.ShapeDtypeStruct((8, 2, 72, 512), F32),
            jax.ShapeDtypeStruct((8, 2, 8, 512), F32),
            jax.ShapeDtypeStruct((8,), F32),
        ),
        in_specs=smem(2) + anyspace(2) + vmem(2),
        out_specs=tuple(vmem(3) + smem(1)),
        scratch_shapes=[
            VM((2, 528, 512), BF16),
            VM((2, 4, 512, 128), BF16),
            VM((2, 8, 80, 512), BF16),
            VM((2, 8, 80, 512), BF16),
            VM((4, 512, 256), F32),
            VM((4, 512, 256), F32),
            pltpu.SemaphoreType.DMA((2,)),
        ],
        compiler_params=PACKED,
        cost_estimate=cost(6 << 30, 8 << 20, 1 << 22),
    )(occ, me, to_partner, to_cross, qkv, wv_t)


def side_kernel(
    me, stats, remote, query, state, peak, qkv, wv_t, wo_t, latent_t, proj_t, pooled, *rest
):
    last = len(rest) == 8
    if last:
        other, out, keys, values, attended, even, odd, fast = rest
        half = me[0] % 2
    else:
        out, keys, values, attended, even, odd, fast = rest
        half = 1 - me[0] % 2
    flags = remote[512:528, :].astype(F32)
    value_peak = keys_values(
        remote[0:512, :], qkv[1], wv_t[...], flags[0:1], keys, values, None
    )
    fast[0] = 0.0

    def finish(head, lanes, total):
        result = total[0:64] / total[64:65]
        attended[pl.ds(pl.multiple_of(head * 64, 64), 64), lanes] = result.astype(BF16)

    @pl.when((value_peak < 1e12) & (stats[0] > 0.5))
    def plain():
        def score(pair, into, unit):
            into[unit] = lax.dot_general(
                keys[pair],
                query[2 * pair + unit // 2, half, 256 * (unit % 2) : 256 * (unit % 2) + 256, :],
                NT,
                preferred_element_type=F32,
            )

        def attend(pair, scores, unit):
            lanes = slice(256 * (unit % 2), 256 * (unit % 2) + 256)
            head = 2 * pair + unit // 2
            parts = [
                jnp.exp2(scores[unit, 128 * chunk : 128 * chunk + 128, :]).astype(BF16)
                for chunk in range(4)
            ]
            total = jnp.dot(
                values[head], jnp.concatenate(parts, axis=0), preferred_element_type=F32
            )
            total = total[0:72] + state[head, half, :, lanes]
            finish(head, lanes, total)
            return in_range(total[64:72])

        for unit in range(4):
            score(0, even, unit)

        def per_two(i, good):
            for unit in range(4):
                score(2 * i + 1, odd, unit)
                good = good * attend(2 * i, even, unit)
            for unit in range(4):
                score(jnp.minimum(2 * i + 2, 3), even, unit)
                good = good * attend(2 * i + 1, odd, unit)
            return good

        fast[0] = jnp.min(lax.fori_loop(0, 2, per_two, jnp.ones((8, 256), F32)))

    @pl.when(fast[0] < 0.5)
    def general():
        biases = [jnp.where(flags[8 + b : 9 + b, 0:256] > 0.5, 0.0, NEG) for b in range(8)]

        def per_head(head, carry):
            for tile in range(2):
                lanes = slice(256 * tile, 256 * tile + 256)
                scores = lax.dot_general(
                    keys[head // 2], query[head, half, lanes, :], NT, preferred_element_type=F32
                )
                before = peak[head, half, 0:1, lanes]
                top = jnp.maximum(block_max(scores, biases), before)
                total = jnp.dot(
                    values[head], shifted_weights(scores, top, biases), preferred_element_type=F32
                )
                finish(
                    head, lanes, total[0:72] + state[head, half, :, lanes] * jnp.exp2(before - top)
                )
            return carry

        lax.fori_loop(0, 8, per_head, 0)

    place = pl.ds(pl.multiple_of(half * 512, 512), 512)
    mixing = jnp.dot(wo_t[...], attended[...], preferred_element_type=F32)
    lifted = lax.dot_general(proj_t[...], pooled[place, :], NT, preferred_element_type=F32)
    result = ((latent_t[:, place].astype(F32) + lifted) + mixing).astype(BF16)
    if last:
        out[:, place] = result
        out[:, pl.ds(pl.multiple_of((1 - half) * 512, 512), 512)] = other[...]
    else:
        out[...] = result


def side_attention(me, stats, remote, *shared, other):
    last = other is not None
    return pl.pallas_call(
        side_kernel,
        name="last_attention" if last else "side_attention",
        out_shape=jax.ShapeDtypeStruct((512, 1024 if last else 512), BF16),
        in_specs=smem(2) + vmem(len(shared) + 1 + last),
        out_specs=vmem(1)[0],
        scratch_shapes=[
            VM((4, 512, 128), BF16),
            VM((8, 80, 512), BF16),
            VM((512, 512), BF16),
            VM((4, 512, 256), F32),
            VM((4, 512, 256), F32),
            pltpu.SMEM((1,), F32),
        ],
        compiler_params=PACKED,
        cost_estimate=cost(4 << 30, 6 << 20, 1 << 21),
    )(me, stats, remote, *shared, *([other] if last else []))


def pool_tables():
    pool = np.zeros((64, 64), np.float32)
    pick = np.zeros((64, 256), np.float32)
    for token in range(64):
        p = (token // 32) * 2 + token // 4 % 2
        q = (token // 16 % 2) * 2 + token // 2 % 2
        r = (token // 8 % 2) * 2 + token % 2
        for x in (2 * p, 2 * p + 1):
            for y in (2 * q, 2 * q + 1):
                pool[token, 8 * x + y] = 0.125
        pick[token, 64 * r : 64 * r + 64] = 1.0
    return jnp.asarray(pool, BF16), jnp.asarray(pick, F32)


def moved(array, by):
    size = lax.axis_size(AXES)
    pairs = [(i, i + by) for i in range(size) if 0 <= i + by < size]
    return lax.ppermute(array, AXES, pairs)


def swapped(array):
    size = lax.axis_size(AXES)
    return lax.ppermute(array, AXES, [(i, i ^ 1) for i in range(size)])


def crossed(array):
    size = lax.axis_size(AXES)
    pairs = [(i, (i - 1) % size if i % 2 == 0 else (i + 1) % size) for i in range(size)]
    return lax.ppermute(array, AXES, pairs)


def local(
    features, occupancy, neighbours, conv_weight, conv_bias, latent, token_proj, norm_gain,
    qkv_weight, out_weight,
):
    me = lax.axis_index(AXES)
    me_ref = me.astype(jnp.int32).reshape(1)
    faces = prep(occupancy, features)
    back = moved(faces, 2)
    ahead = moved(faces, -2)
    partner = swapped(faces)
    conv_weight, _ = lax.optimization_barrier((conv_weight, faces))
    source, bias, band, band_z, wv_t, wo_t, latent_t, proj_t = weights(
        neighbours.T, me_ref, conv_weight, conv_bias[:, None], qkv_weight, out_weight, latent,
        token_proj,
    )
    xb, acc = inner(occupancy, features, band)
    back, ahead, acc, band_z = lax.optimization_barrier((back, ahead, acc, band_z))
    relay = swapped(choose(me_ref, back, ahead))
    blocks, pooled, to_partner, to_cross = outer(
        source, occupancy, me_ref, (faces, back, ahead, partner, relay), xb, acc, band, band_z,
        bias, latent, token_proj, norm_gain[None, :],
    )
    from_cross = crossed(to_cross)
    from_partner = swapped(to_partner)
    query, state, peak, stats = own_attention(
        occupancy, me_ref, to_partner, to_cross, qkv_weight, wv_t
    )
    conv_out = restore(blocks)
    shared = (query, state, peak, qkv_weight, wv_t, wo_t, latent_t, proj_t, pooled)
    first = side_attention(me_ref, stats, from_partner, *shared, other=None)
    tokens_out = side_attention(me_ref, stats, from_cross, *shared, other=first)
    return (conv_out, tokens_out)


def solution(mesh):
    return jax.shard_map(
        local,
        mesh=mesh,
        in_specs=(
            P(AXES, None, None),
            P(AXES),
            P(AXES, None),
            P(),
            P(),
            P(AXES, None),
            P(),
            P(),
            P(),
            P(),
        ),
        out_specs=(P(AXES, None, None), P(None, AXES)),
        check_vma=False,
    )
```

```python
import math

import jax
import jax.numpy as jnp
import numpy as np
from jax import lax
from jax.experimental import pallas as pl
from jax.experimental.pallas import tpu as pltpu
from jax.sharding import PartitionSpec as P

HD = 64
WIN = 1024
REACH = 2
AXES = ("space", "chan")
NEG = -1e30
TILES = 88
F32 = jnp.float32
BF16 = jnp.bfloat16
VM = pltpu.VMEM
NT = (((1,), (1,)), ((), ()))
SCALE = HD ** (-0.5) * math.log2(math.e)
LIMIT = pltpu.CompilerParams(vmem_limit_bytes=20 << 20)
WHOLE = pltpu.CompilerParams(vmem_limit_bytes=63 << 20)
PACKED = pltpu.CompilerParams(
    vmem_limit_bytes=20 << 20
)


def vmem(count):
    return [pl.BlockSpec(memory_space=pltpu.VMEM)] * count


def smem(count):
    return [pl.BlockSpec(memory_space=pltpu.SMEM)] * count


def anyspace(count):
    return [pl.BlockSpec(memory_space=pl.ANY)] * count


def cost(flops, moved, trans=0):
    return pl.CostEstimate(flops=flops, bytes_accessed=moved, transcendentals=trans)


def swap_blocks(four):
    lane = lax.broadcasted_iota(jnp.int32, four[0].shape, 1)
    low = lane < 64
    even = (lane // 32) % 2 == 0
    half = []
    for a, b in ((0, 2), (1, 3)):
        half.append(jnp.where(low, four[a], pltpu.roll(four[b], 64, 1)))
        half.append(jnp.where(low, pltpu.roll(four[a], 64, 1), four[b]))
    a0, a2, a1, a3 = half
    return [
        jnp.where(even, a0, pltpu.roll(a1, 32, 1)),
        jnp.where(even, pltpu.roll(a0, 96, 1), a1),
        jnp.where(even, a2, pltpu.roll(a3, 32, 1)),
        jnp.where(even, pltpu.roll(a2, 96, 1), a3),
    ]


def lanes_of(half):
    return slice(128 * half, 128 * half + 128)


def picker(voxel_of, count):
    row = lax.broadcasted_iota(jnp.int32, (count, 512), 0)
    col = lax.broadcasted_iota(jnp.int32, (count, 512), 1)
    return jnp.where(voxel_of(row) == col, 1.0, 0.0).astype(BF16)


def pick_rows(first, stride):
    row = lax.broadcasted_iota(jnp.int32, (8, 512), 0)
    col = lax.broadcasted_iota(jnp.int32, (8, 512), 1)
    return jnp.where(row * stride + first == col, 1.0, 0.0)


def rim_rows():
    rows = []
    for z in range(8):
        for first, stride in ((448, 8), (0, 8), (56, 64), (0, 64)):
            rows.append(pick_rows(first + z, stride))
    for z in (0, 7):
        for x in range(8):
            rows.append(pick_rows(64 * x + z, 8))
    return jnp.concatenate(rows, axis=0).astype(BF16)


def alive_rows(rows, alive):
    return jnp.where(alive > 0, rows, jnp.zeros_like(rows))


def prep_kernel(occ, feat, faces, masked, picks, sems):
    copies = [
        pltpu.make_async_copy(
            feat.at[pl.ds(8 * two, 8)], masked.at[pl.ds(8 * two, 8)], sems.at[two]
        )
        for two in range(2)
    ]
    for copy in copies:
        copy.start()
    picks[...] = rim_rows()
    for two in range(2):
        copies[two].wait()
        rows = []
        for b in range(8 * two, 8 * two + 8):
            rows.append(alive_rows(masked[b], occ[b]))
        rows = jnp.concatenate(rows, axis=0)
        found = lax.dot_general(picks[...], rows, NT, preferred_element_type=F32).astype(BF16)
        for g in (2 * two, 2 * two + 1):
            for face in range(2):
                sheet = found[256 + 64 * face : 320 + 64 * face, lanes_of(g % 2)]
                for x in range(1, 4):
                    tile = jnp.concatenate(
                        [sheet[8 * x : 8 * x + 8], sheet[8 * x + 24 : 8 * x + 32]], axis=1
                    )
                    faces[64 + (2 * g + face) * 3 + x - 1] = tile
            for half in range(2):
                four = [
                    found[32 * z : 32 * z + 32, lanes_of(g % 2)]
                    for z in range(4 * half, 4 * half + 4)
                ]
                for j, block in enumerate(swap_blocks(four)):
                    for face in range(4):
                        faces[4 * (4 * g + j) + face, :, lanes_of(half)] = block[
                            8 * face : 8 * face + 8
                        ]


def prep(occ, feat):
    return pl.pallas_call(
        prep_kernel,
        name="prep",
        out_shape=jax.ShapeDtypeStruct((TILES, 8, 256), BF16),
        in_specs=smem(1) + [pl.BlockSpec(memory_space=pltpu.HBM)],
        out_specs=vmem(1)[0],
        scratch_shapes=[
            VM((16, 32, 512), BF16),
            VM((384, 512), BF16),
            pltpu.SemaphoreType.DMA((2,)),
        ],
        compiler_params=WHOLE,
        cost_estimate=cost(1 << 28, 2 << 20),
    )(occ, feat)


def choose_kernel(me, back, ahead, out, sems):
    core = me[0] % 2
    for which, ref in ((1, back), (0, ahead)):

        @pl.when(core == which)
        def send(ref=ref):
            copy = pltpu.make_async_copy(ref, out, sems.at[0])
            copy.start()
            copy.wait()


def choose(me, back, ahead):
    return pl.pallas_call(
        choose_kernel,
        name="choose",
        out_shape=jax.ShapeDtypeStruct(back.shape, BF16),
        in_specs=smem(1) + anyspace(2),
        out_specs=anyspace(1)[0],
        scratch_shapes=[pltpu.SemaphoreType.DMA((1,))],
        compiler_params=LIMIT,
        cost_estimate=cost(1 << 10, 1 << 20),
    )(me, back, ahead)


def shifted_rows(tile, step):
    if step == 0:
        return tile
    row = lax.broadcasted_iota(jnp.int32, tile.shape, 0) % 8
    if step < 0:
        moved = pltpu.roll(tile, 1, 0)
        return jnp.where(row == 0, 0.0, moved)
    moved = pltpu.roll(tile, tile.shape[0] - 1, 0)
    return jnp.where(row == 7, 0.0, moved)


def joined(pair, *at):
    return jnp.concatenate([pair[(0, *at)], pair[(1, *at)]], axis=1)


def write_patches(lhs, brick, tiles):
    zero = jnp.zeros((8, 256), F32)
    rows = pl.ds(pl.multiple_of(brick * 64, 64), 64)
    for dy in (-1, 0, 1):
        moved = [shifted_rows(t, dy) for t in tiles]
        for dx in (-1, 0, 1):
            picked = [moved[x + dx] if 0 <= x + dx < 8 else zero for x in range(8)]
            tap = (dx + 1) * 3 + dy + 1
            lhs[rows, 256 * tap : 256 * tap + 256] = jnp.concatenate(picked, axis=0).astype(BF16)


def turn(eye, array):
    return lax.dot_general(eye, array, NT, preferred_element_type=F32).astype(BF16)


def weights_kernel(
    conv, qkv, out_weight, latent, band, band_z, wv_t, wo_t, latent_t, wide
):
    row = lax.broadcasted_iota(jnp.int32, (32, 256), 0)
    col = lax.broadcasted_iota(jnp.int32, (32, 256), 1) % 32
    spread = jnp.where(row == col, 1.0, 0.0).astype(BF16)
    for tap in range(27):
        wide[32 * tap : 32 * tap + 32, :] = jnp.dot(
            conv[tap].astype(F32).T.astype(BF16), spread, preferred_element_type=F32
        )
    block = lax.broadcasted_iota(jnp.int32, (32, 256), 1) // 32

    def per_tap(t, carry):
        base = [
            wide[pl.ds(pl.multiple_of((t * 3 + k) * 32, 32), 32), :] for k in range(3)
        ]
        for z in range(8):
            value = jnp.where(block == z, base[1], 0.0)
            value = jnp.where(block == z + 1, base[0], value)
            value = jnp.where(block == z - 1, base[2], value)
            band[pl.ds(pl.multiple_of(t * 256 + 32 * z, 32), 32), :] = value.astype(BF16)
        return carry

    lax.fori_loop(0, 9, per_tap, 0)
    for dy in range(3):
        for face, k in ((0, 0), (1, 2)):
            value = jnp.zeros((32, 256), F32)
            for dx in range(3):
                start = ((dx * 3 + dy) * 3 + k) * 32
                value = jnp.where(block == 2 * dx + face, wide[start : start + 32, :], value)
            for j in range(4):
                start = dy * 256 + 128 * face + 32 * j
                band_z[start : start + 32, :] = value.astype(BF16)
    row = lax.broadcasted_iota(jnp.int32, (512, 512), 0)
    col = lax.broadcasted_iota(jnp.int32, (512, 512), 1)
    eye = jnp.where(row == col, 1.0, 0.0).astype(BF16)
    wv_t[...] = turn(eye, qkv[2])
    wo_t[...] = turn(eye, out_weight[...])
    latent_t[...] = turn(eye, latent[...])


def weights(conv_weight, qkv, out_weight, latent):
    return pl.pallas_call(
        weights_kernel,
        name="weights",
        out_shape=(
            jax.ShapeDtypeStruct((2304, 256), BF16),
            jax.ShapeDtypeStruct((768, 256), BF16),
            jax.ShapeDtypeStruct((512, 512), BF16),
            jax.ShapeDtypeStruct((512, 512), BF16),
            jax.ShapeDtypeStruct((512, 1024), BF16),
        ),
        in_specs=vmem(4),
        out_specs=tuple(vmem(5)),
        scratch_shapes=[VM((864, 256), F32)],
        compiler_params=LIMIT,
        cost_estimate=cost(1 << 31, 8 << 20),
    )(conv_weight, qkv, out_weight, latent)


def spread_kernel(occ, feat, xb, masked):
    for b in range(16):
        masked[32 * b : 32 * b + 32, :] = alive_rows(feat[b], occ[b])
    order = [pick_rows(64 * x + z, 8) for z in range(8) for x in range(8)]
    order = jnp.concatenate(order, axis=0).astype(BF16)
    for two in range(2):
        found = lax.dot_general(
            order, masked[256 * two : 256 * two + 256, :], NT, preferred_element_type=F32
        ).astype(BF16)
        for g in (2 * two, 2 * two + 1):
            for half in range(2):
                four = [
                    found[64 * z : 64 * z + 64, lanes_of(g % 2)]
                    for z in range(4 * half, 4 * half + 4)
                ]
                for j, block in enumerate(swap_blocks(four)):
                    xb[half, 4 * g + j] = block.astype(F32)


def spread(occ, feat):
    return pl.pallas_call(
        spread_kernel,
        name="spread",
        out_shape=jax.ShapeDtypeStruct((2, 16, 64, 128), F32),
        in_specs=smem(1) + vmem(1),
        out_specs=vmem(1)[0],
        scratch_shapes=[VM((512, 512), BF16)],
        compiler_params=LIMIT,
        cost_estimate=cost(1 << 28, 2 << 20),
    )(occ, feat)


def inner_kernel(neighbours, me, xb, band, acc, source, lhs, table):
    core = me[0] % 2
    for away, slot in enumerate((1, 4 - core, 0, 3 + core, 2)):
        table[away] = slot

    def look_up(b, carry):
        for face in range(6):
            peer = neighbours[face, b]
            safe = jnp.maximum(peer, 0)
            away = jnp.clip(safe // 16 - me[0], -REACH, REACH)
            start = table[away + REACH] * TILES
            brick = safe % 16
            source[b * 16 + face] = jnp.where(peer >= 0, start + brick * 4, 5 * TILES)
            if face >= 4:
                sheet = start + 64 + (brick // 4 * 2 + (5 - face)) * 3
                source[b * 16 + face + 2] = jnp.where(peer >= 0, sheet, 5 * TILES)
                source[b * 16 + face + 4] = brick % 4
        return carry

    lax.fori_loop(0, 16, look_up, 0)
    def per_brick(b, carry):
        write_patches(lhs, b, [joined(xb, b, slice(8 * x, 8 * x + 8)) for x in range(8)])
        return carry

    lax.fori_loop(0, 16, per_brick, 0)

    def per_rows(i, carry):
        rows = pl.ds(pl.multiple_of(i * 512, 512), 512)
        acc[rows, :] = jnp.dot(lhs[rows, :], band[...], preferred_element_type=F32)
        return carry

    lax.fori_loop(0, 2, per_rows, 0)


def inner(neighbours, me, xb, band):
    return pl.pallas_call(
        inner_kernel,
        name="inner",
        out_shape=(
            jax.ShapeDtypeStruct((1024, 256), F32),
            jax.ShapeDtypeStruct((256,), jnp.int32),
        ),
        in_specs=smem(2) + vmem(2),
        out_specs=tuple(vmem(1) + smem(1)),
        scratch_shapes=[VM((1024, 2304), BF16), pltpu.SMEM((8,), jnp.int32)],
        compiler_params=LIMIT,
        cost_estimate=cost(2 * 1024 * 2304 * 256, 4 << 20),
    )(neighbours, me, xb, band)


def outer_kernel(
    source, occ, me, own, back, ahead, partner, relay, xb, acc, band, band_z, bias, pool, pick,
    latent, proj, gain,
    blocks, pooled, to_partner, to_cross,
    store, lhs, flat, edges, sums, halves, sems,
):
    copies = [
        pltpu.make_async_copy(ref, store.at[pl.ds(slot * TILES, TILES)], sems.at[slot])
        for slot, ref in enumerate((own, back, ahead, partner, relay))
    ]
    for copy in copies:
        copy.start()
    core = me[0] % 2
    store[5 * TILES : 5 * TILES + 8] = jnp.zeros((8, 8, 256), BF16)
    for copy in copies:
        copy.wait()
    lane = lax.broadcasted_iota(jnp.int32, (8, 256), 1) % 128 // 32

    def gather(b, carry):
        for face in range(4):
            tile = store[source[b * 16 + face] + face].astype(F32)
            flat[face, pl.ds(pl.multiple_of(b * 8, 8), 8), :] = tile
        pair = []
        for face in range(2):
            edge = source[b * 16 + 4 + face]
            sheet = source[b * 16 + 6 + face]
            mask = lane == source[b * 16 + 8 + face]
            part = lanes_of(1 - face)
            rim = lane[:, :128] == (3 if face == 0 else 0)
            first = jnp.where(rim, store[edge + 1].astype(F32)[:, part], 0.0)
            final = jnp.where(rim, store[edge].astype(F32)[:, part], 0.0)
            mids = [jnp.where(mask, store[sheet + k].astype(F32), 0.0) for k in range(3)]
            pair.append(
                [first] + [m[:, :128] for m in mids] + [m[:, 128:] for m in mids] + [final]
            )
        tiles = [jnp.concatenate([pair[0][x], pair[1][x]], axis=1) for x in range(8)]
        rows = pl.ds(pl.multiple_of(b * 64, 64), 64)
        for dy in (-1, 0, 1):
            moved = [shifted_rows(t, dy) for t in tiles]
            start = 256 * (dy + 1)
            lhs[rows, start : start + 256] = jnp.concatenate(moved, axis=0).astype(BF16)
        return carry

    lax.fori_loop(0, 16, gather, 0)
    for face in range(4):
        sheet = flat[face]
        side = 0 if face % 2 == 0 else 2
        total = None
        for step in (-1, 0, 1):
            tap = side * 3 + step + 1 if face < 2 else (step + 1) * 3 + side
            part = jnp.dot(
                shifted_rows(sheet, step).astype(BF16),
                band[256 * tap : 256 * tap + 256, :],
                preferred_element_type=F32,
            )
            total = part if total is None else total + part
        edges[face] = total
    sums[...] = jnp.dot(lhs[...], band_z[...], preferred_element_type=F32)
    row = lax.broadcasted_iota(jnp.int32, (8, 256), 0)
    shift = jnp.concatenate([bias[...]] * 8, axis=1)
    one = lax.broadcasted_iota(jnp.int32, (8, 128), 1)

    def finish(b, alive):
        start = pl.multiple_of(b * 64, 64)
        sheet_rows = pl.ds(pl.multiple_of(b * 8, 8), 8)
        y_low, y_high = edges[2, sheet_rows, :], edges[3, sheet_rows, :]
        done = []
        for x in range(8):
            tile_rows = pl.ds(start + 8 * x, 8)
            rim = pltpu.roll(sums[tile_rows, 0:128], 64, 1)
            if x > 0:
                rim = rim + sums[pl.ds(start + 8 * x - 8, 8), 0:128]
            if x < 7:
                rim = rim + sums[pl.ds(start + 8 * x + 8, 8), 128:256]
            rim = jnp.concatenate(
                [
                    jnp.where(one < 32, rim, 0.0),
                    jnp.where(one >= 96, pltpu.roll(rim, 64, 1), 0.0),
                ],
                axis=1,
            )
            total = acc[tile_rows, :] + rim
            total = total + jnp.where(row == 0, y_low[x : x + 1, :], 0.0)
            total = total + jnp.where(row == 7, y_high[x : x + 1, :], 0.0)
            if x == 0:
                total = total + edges[0, sheet_rows, :]
            if x == 7:
                total = total + edges[1, sheet_rows, :]
            value = total + shift
            kept = joined(xb, b, slice(8 * x, 8 * x + 8))
            value = 0.5 * value
            done.append(alive * (kept + (value + value * jnp.tanh(value))))
        block = jnp.concatenate(done, axis=0).astype(BF16)
        for half in range(2):
            blocks[half, b] = block[:, lanes_of(half)]
        cells = jnp.dot(pool[...], block, preferred_element_type=F32) * pick[...]
        cells = cells[:, :128] + cells[:, 128:]
        cells = cells + pltpu.roll(cells, 64, 1)
        cells = cells + pltpu.roll(cells, 32, 1)
        pooled[pl.ds(start, 64), :] = cells.astype(BF16)

    def finish_four(i, carry):
        for k in range(4):
            finish(4 * i + k, occ[4 * i + k].astype(F32))
        return carry

    lax.fori_loop(0, 4, finish_four, 0)

    def norm(i, carry):
        rows = pl.ds(pl.multiple_of(i * 256, 256), 256)
        lifted = jnp.dot(pooled[rows, 0:32], proj[...], preferred_element_type=F32)
        mixed = latent[rows, :].astype(F32) + lifted
        scale = lax.rsqrt(jnp.mean(mixed * mixed, axis=-1, keepdims=True) + 1e-06)
        halves[i // 2, pl.ds(pl.multiple_of(i % 2 * 256, 256), 256), :] = (
            mixed * scale * gain[...]
        ).astype(BF16)
        return carry

    lax.fori_loop(0, 4, norm, 0)
    flag_row = lax.broadcasted_iota(jnp.int32, (16, 512), 0)
    flag_lane = lax.broadcasted_iota(jnp.int32, (16, 512), 1) // 64
    for half in range(2):
        flags = jnp.zeros((16, 512), F32)
        for b in range(8):
            here = (flag_row == 8 + b) | ((flag_row == 0) & (flag_lane == b))
            flags = jnp.where(here, occ[8 * half + b].astype(F32), flags)
        halves[half, 512:528, :] = flags.astype(BF16)
    out = [
        pltpu.make_async_copy(halves.at[1 - core], to_partner, sems.at[5]),
        pltpu.make_async_copy(halves.at[core], to_cross, sems.at[6]),
    ]
    for copy in out:
        copy.start()
    for copy in out:
        copy.wait()


def outer(source, occ, me, stores, xb, acc, band, band_z, bias, latent, proj, gain):
    return pl.pallas_call(
        outer_kernel,
        name="outer",
        out_shape=(
            jax.ShapeDtypeStruct((2, 16, 64, 128), BF16),
            jax.ShapeDtypeStruct((1024, 128), BF16),
            jax.ShapeDtypeStruct((528, 512), BF16),
            jax.ShapeDtypeStruct((528, 512), BF16),
        ),
        in_specs=smem(3) + anyspace(5) + vmem(10),
        out_specs=tuple(vmem(2) + anyspace(2)),
        scratch_shapes=[
            VM((5 * TILES + 8, 8, 256), BF16),
            VM((1024, 768), BF16),
            VM((4, 128, 256), F32),
            VM((4, 128, 256), F32),
            VM((1024, 256), F32),
            VM((2, 528, 512), BF16),
            pltpu.SemaphoreType.DMA((7,)),
        ],
        compiler_params=LIMIT,
        cost_estimate=cost(2 * 1024 * 2304 * 256, 8 << 20, 1 << 18),
    )(source, occ, me, *stores, xb, acc, band, band_z, bias, *pool_tables(), latent, proj, gain)


def restore_kernel(blocks, out, turned):
    row = lax.broadcasted_iota(jnp.int32, (128, 128), 0)
    col = lax.broadcasted_iota(jnp.int32, (128, 128), 1)
    eye = jnp.where(row == col, 1.0, 0.0).astype(BF16)
    for g in range(4):
        for half in range(2):
            four = [blocks[half, 4 * g + j] for j in range(4)]
            for k, sheet in enumerate(swap_blocks(four)):
                turned[g, pl.ds(4 * half + k, 64, stride=8), :] = sheet.astype(F32)
    for g in range(4):
        rows = turn(eye, turned[g].astype(BF16))
        for j in range(4):
            out[4 * g + j] = rows[32 * j : 32 * j + 32]


def restore(blocks):
    return pl.pallas_call(
        restore_kernel,
        name="restore",
        out_shape=jax.ShapeDtypeStruct((16, 32, 512), BF16),
        in_specs=vmem(1),
        out_specs=vmem(1)[0],
        scratch_shapes=[VM((4, 512, 128), F32)],
        compiler_params=LIMIT,
        cost_estimate=cost(1 << 20, 2 << 20),
    )(blocks)


def column_max(part):
    return jnp.max(part, axis=0, keepdims=True)


def in_range(total):
    return jnp.where((total > 2.0**-60) & (total < 2.0**60), 1.0, 0.0)


def block_max(scores, biases):
    top = None
    for b in range(8):
        part = scores[64 * b : 64 * b + 8]
        for k in range(1, 8):
            part = jnp.maximum(part, scores[64 * b + 8 * k : 64 * b + 8 * k + 8])
        part = part + biases[b]
        top = part if top is None else jnp.maximum(top, part)
    return column_max(top)


def shifted_weights(scores, top, biases):
    parts = [
        jnp.exp2(scores[64 * b : 64 * b + 64] - (top - biases[b])).astype(BF16) for b in range(8)
    ]
    return jnp.concatenate(parts, axis=0)


def keys_values(rows, wk, wv_t, alive, keys, values, raw):
    found = jnp.dot(rows, wk, preferred_element_type=F32)
    for pair in range(4):
        keys[pair] = found[:, 128 * pair : 128 * pair + 128].astype(BF16)
    found = lax.dot_general(wv_t, rows, NT, preferred_element_type=F32)
    ones = jnp.ones((16, 512), F32)
    for head in range(8):
        block = found[64 * head : 64 * head + 64]
        if raw is not None:
            raw[head, 0:64, :] = block.astype(BF16)
            raw[head, 64:80, :] = ones.astype(BF16)
        values[head, 0:64, :] = (block * alive).astype(BF16)
        values[head, 64:80, :] = (ones * alive).astype(BF16)
    return jnp.max(jnp.abs(found))


def own_kernel(
    occ, me, to_partner, to_cross, qkv, wv_t, query, state, peak, stats,
    normed, keys, values, raw, even, odd, sems,
):
    core = me[0] % 2
    copies = [
        pltpu.make_async_copy(to_partner, normed.at[1 - core], sems.at[0]),
        pltpu.make_async_copy(to_cross, normed.at[core], sems.at[1]),
    ]
    for copy in copies:
        copy.start()
    for copy in copies:
        copy.wait()
    lane = lax.broadcasted_iota(jnp.int32, (512, 128), 1)
    alive = [normed[half, 512:528, :].astype(F32)[0:1] for half in range(2)]
    tops = []
    for half in range(2):
        rows = normed[half, 0:512, :]
        found = jnp.dot(rows, qkv[0], preferred_element_type=F32) * SCALE
        for head in range(8):
            pair = found[:, 128 * (head // 2) : 128 * (head // 2) + 128]
            keep = lane < 64 if head % 2 == 0 else lane >= 64
            query[head, half] = jnp.where(keep, pair, 0.0).astype(BF16)
        tops.append(
            keys_values(
                rows, qkv[1], wv_t[...], alive[half], keys.at[half], values.at[half], raw.at[half]
            )
        )
    row = lax.broadcasted_iota(jnp.int32, (128, 128), 0)
    col = lax.broadcasted_iota(jnp.int32, (128, 128), 1)
    eye = row == col

    small = jnp.maximum(tops[0], tops[1]) < 1e12
    stats[0] = 0.0

    @pl.when(small)
    def plain():
        def score(head, into, unit):
            for half in (unit // 2,):
                for tile in (unit % 2,):
                    into[2 * half + tile] = lax.dot_general(
                        keys[half, head // 2],
                        query[head, half, 256 * tile : 256 * tile + 256, :],
                        NT,
                        preferred_element_type=F32,
                    )

        def attend(head, scores, unit):
            good = None
            for half in (unit // 2,):
                for tile in (unit % 2,):
                    lanes = slice(256 * tile, 256 * tile + 256)
                    parts, own = [], []
                    for chunk in range(4):
                        weights = jnp.exp2(
                            scores[2 * half + tile, 128 * chunk : 128 * chunk + 128, :]
                        )
                        if chunk // 2 == tile:
                            first = 128 * (chunk % 2)
                            block = weights[:, first : first + 128]
                            own.append(
                                jnp.sum(jnp.where(eye, block, 0.0), axis=0, keepdims=True)
                            )
                        parts.append(weights.astype(BF16))
                    out = jnp.dot(
                        values[half, head],
                        jnp.concatenate(parts, axis=0),
                        preferred_element_type=F32,
                    )
                    extra = jnp.concatenate(own, axis=1) * (1.0 - alive[half][:, lanes])
                    out = out + extra * raw[half, head, :, lanes].astype(F32)
                    state[head, half, :, lanes] = out[0:72]
                    peak[head, half, :, lanes] = jnp.zeros((8, 256), F32)
                    good = in_range(out[64:72])
            return good

        for unit in range(4):
            score(0, even, unit)

        def per_two(i, good):
            for unit in range(4):
                score(2 * i + 1, odd, unit)
                good = good * attend(2 * i, even, unit)
            for unit in range(4):
                score(jnp.minimum(2 * i + 2, 7), even, unit)
                good = good * attend(2 * i + 1, odd, unit)
            return good

        stats[0] = jnp.min(lax.fori_loop(0, 4, per_two, jnp.ones((8, 256), F32)))

    @pl.when(stats[0] < 0.5)
    def general():
        def per_head(head, carry):
            for half in range(2):
                biases = [
                    jnp.where(occ[8 * half + b] > 0, 0.0, NEG).astype(F32) for b in range(8)
                ]
                for tile in range(2):
                    lanes = slice(256 * tile, 256 * tile + 256)
                    scores = lax.dot_general(
                        keys[half, head // 2],
                        query[head, half, lanes, :],
                        NT,
                        preferred_element_type=F32,
                    )
                    selves = []
                    for k in range(2):
                        first = 256 * tile + 128 * k
                        block = scores[first : first + 128, 128 * k : 128 * k + 128]
                        selves.append(column_max(jnp.where(eye, block, NEG)))
                    dead = alive[half][:, lanes] < 0.5
                    own = jnp.where(dead, jnp.concatenate(selves, axis=1), NEG)
                    top = jnp.maximum(block_max(scores, biases), own)
                    out = jnp.dot(
                        values[half, head],
                        shifted_weights(scores, top, biases),
                        preferred_element_type=F32,
                    )
                    extra = jnp.where(dead, jnp.exp2(own - top), 0.0)
                    out = out + extra * raw[half, head, :, lanes].astype(F32)
                    state[head, half, :, lanes] = out[0:72]
                    peak[head, half, :, lanes] = jnp.broadcast_to(top, (8, 256))
            return carry

        lax.fori_loop(0, 8, per_head, 0)


def own_attention(occ, me, to_partner, to_cross, qkv, wv_t):
    return pl.pallas_call(
        own_kernel,
        name="own_attention",
        out_shape=(
            jax.ShapeDtypeStruct((8, 2, 512, 128), BF16),
            jax.ShapeDtypeStruct((8, 2, 72, 512), F32),
            jax.ShapeDtypeStruct((8, 2, 8, 512), F32),
            jax.ShapeDtypeStruct((8,), F32),
        ),
        in_specs=smem(2) + anyspace(2) + vmem(2),
        out_specs=tuple(vmem(3) + smem(1)),
        scratch_shapes=[
            VM((2, 528, 512), BF16),
            VM((2, 4, 512, 128), BF16),
            VM((2, 8, 80, 512), BF16),
            VM((2, 8, 80, 512), BF16),
            VM((4, 512, 256), F32),
            VM((4, 512, 256), F32),
            pltpu.SemaphoreType.DMA((2,)),
        ],
        compiler_params=PACKED,
        cost_estimate=cost(6 << 30, 8 << 20, 1 << 22),
    )(occ, me, to_partner, to_cross, qkv, wv_t)


def side_kernel(
    me, stats, remote, query, state, peak, qkv, wv_t, wo_t, latent_t, proj, pooled, *rest
):
    last = len(rest) == 10
    out, keys, values, attended, even, odd, fast, result, sems = rest[-9:]
    half = me[0] % 2 if last else 1 - me[0] % 2
    flags = remote[512:528, :].astype(F32)
    value_peak = keys_values(
        remote[0:512, :], qkv[1], wv_t[...], flags[0:1], keys, values, None
    )
    fast[0] = 0.0

    def finish(head, lanes, total):
        result = total[0:64] / total[64:65]
        attended[pl.ds(pl.multiple_of(head * 64, 64), 64), lanes] = result.astype(BF16)

    @pl.when((value_peak < 1e12) & (stats[0] > 0.5))
    def plain():
        def score(pair, into, unit):
            into[unit] = lax.dot_general(
                keys[pair],
                query[2 * pair + unit // 2, half, 256 * (unit % 2) : 256 * (unit % 2) + 256, :],
                NT,
                preferred_element_type=F32,
            )

        def attend(pair, scores, unit):
            lanes = slice(256 * (unit % 2), 256 * (unit % 2) + 256)
            head = 2 * pair + unit // 2
            parts = [
                jnp.exp2(scores[unit, 128 * chunk : 128 * chunk + 128, :]).astype(BF16)
                for chunk in range(4)
            ]
            total = jnp.dot(
                values[head], jnp.concatenate(parts, axis=0), preferred_element_type=F32
            )
            total = total[0:72] + state[head, half, :, lanes]
            finish(head, lanes, total)
            return in_range(total[64:72])

        for unit in range(4):
            score(0, even, unit)

        def per_two(i, good):
            for unit in range(4):
                score(2 * i + 1, odd, unit)
                good = good * attend(2 * i, even, unit)
            for unit in range(4):
                score(jnp.minimum(2 * i + 2, 3), even, unit)
                good = good * attend(2 * i + 1, odd, unit)
            return good

        fast[0] = jnp.min(lax.fori_loop(0, 2, per_two, jnp.ones((8, 256), F32)))

    @pl.when(fast[0] < 0.5)
    def general():
        biases = [jnp.where(flags[8 + b : 9 + b, 0:256] > 0.5, 0.0, NEG) for b in range(8)]

        def per_head(head, carry):
            for tile in range(2):
                lanes = slice(256 * tile, 256 * tile + 256)
                scores = lax.dot_general(
                    keys[head // 2], query[head, half, lanes, :], NT, preferred_element_type=F32
                )
                before = peak[head, half, 0:1, lanes]
                top = jnp.maximum(block_max(scores, biases), before)
                total = jnp.dot(
                    values[head], shifted_weights(scores, top, biases), preferred_element_type=F32
                )
                finish(
                    head, lanes, total[0:72] + state[head, half, :, lanes] * jnp.exp2(before - top)
                )
            return carry

        lax.fori_loop(0, 8, per_head, 0)

    place = pl.ds(pl.multiple_of(half * 512, 512), 512)
    proj_t = proj[...].astype(F32).T.astype(BF16)
    copies = []
    for i in range(2):
        rows = slice(256 * i, 256 * i + 256)
        mixing = jnp.dot(wo_t[rows, :], attended[...], preferred_element_type=F32)
        lifted = lax.dot_general(
            proj_t[rows], pooled[place, 0:32], NT, preferred_element_type=F32
        )
        result[rows, :] = ((latent_t[rows, place].astype(F32) + lifted) + mixing).astype(BF16)
        copies.append(pltpu.make_async_copy(result.at[rows], out.at[rows, place], sems.at[i]))
        copies[-1].start()
    for copy in copies:
        copy.wait()


def side_attention(me, stats, remote, *shared, other):
    last = other is not None
    return pl.pallas_call(
        side_kernel,
        name="last_attention" if last else "side_attention",
        out_shape=jax.ShapeDtypeStruct((512, 1024), BF16),
        in_specs=smem(2) + vmem(len(shared) + 1) + [pl.BlockSpec(memory_space=pltpu.HBM)] * last,
        out_specs=pl.BlockSpec(memory_space=pltpu.HBM),
        input_output_aliases={len(shared) + 3: 0} if last else {},
        scratch_shapes=[
            VM((4, 512, 128), BF16),
            VM((8, 80, 512), BF16),
            VM((512, 512), BF16),
            VM((4, 512, 256), F32),
            VM((4, 512, 256), F32),
            pltpu.SMEM((1,), F32),
            VM((512, 512), BF16),
            pltpu.SemaphoreType.DMA((2,)),
        ],
        compiler_params=PACKED,
        cost_estimate=cost(4 << 30, 6 << 20, 1 << 21),
    )(me, stats, remote, *shared, *([other] if last else []))


def pool_tables():
    pool = np.zeros((64, 64), np.float32)
    pick = np.zeros((64, 256), np.float32)
    for token in range(64):
        p = (token // 32) * 2 + token // 4 % 2
        q = (token // 16 % 2) * 2 + token // 2 % 2
        r = (token // 8 % 2) * 2 + token % 2
        for x in (2 * p, 2 * p + 1):
            for y in (2 * q, 2 * q + 1):
                pool[token, 8 * x + y] = 0.125
        pick[token, 64 * r : 64 * r + 64] = 1.0
    return jnp.asarray(pool, BF16), jnp.asarray(pick, F32)


def moved(array, by):
    size = lax.axis_size(AXES)
    pairs = [(i, i + by) for i in range(size) if 0 <= i + by < size]
    return lax.ppermute(array, AXES, pairs)


def swapped(array):
    size = lax.axis_size(AXES)
    return lax.ppermute(array, AXES, [(i, i ^ 1) for i in range(size)])


def crossed(array):
    size = lax.axis_size(AXES)
    pairs = [(i, (i - 1) % size if i % 2 == 0 else (i + 1) % size) for i in range(size)]
    return lax.ppermute(array, AXES, pairs)


def local(
    features, occupancy, neighbours, conv_weight, conv_bias, latent, token_proj, norm_gain,
    qkv_weight, out_weight,
):
    me = lax.axis_index(AXES)
    me_ref = me.astype(jnp.int32).reshape(1)
    faces = prep(occupancy, features)
    back = moved(faces, 2)
    ahead = moved(faces, -2)
    partner = swapped(faces)
    later, _ = lax.optimization_barrier((features, faces))
    xb = spread(occupancy, later)
    conv_weight, _ = lax.optimization_barrier((conv_weight, xb))
    band, band_z, wv_t, wo_t, latent_t = weights(conv_weight, qkv_weight, out_weight, latent)
    acc, source = inner(neighbours.T, me_ref, xb, band)
    back, ahead, acc, band_z = lax.optimization_barrier((back, ahead, acc, band_z))
    relay = swapped(choose(me_ref, back, ahead))
    blocks, pooled, to_partner, to_cross = outer(
        source, occupancy, me_ref, (faces, back, ahead, partner, relay), xb, acc, band, band_z,
        conv_bias[None, :], latent, token_proj, norm_gain[None, :],
    )
    from_cross = crossed(to_cross)
    from_partner = swapped(to_partner)
    query, state, peak, stats = own_attention(
        occupancy, me_ref, to_partner, to_cross, qkv_weight, wv_t
    )
    conv_out = restore(blocks)
    shared = (query, state, peak, qkv_weight, wv_t, wo_t, latent_t, token_proj, pooled)
    first = side_attention(me_ref, stats, from_partner, *shared, other=None)
    tokens_out = side_attention(me_ref, stats, from_cross, *shared, other=first)
    return (conv_out, tokens_out)


def solution(mesh):
    return jax.shard_map(
        local,
        mesh=mesh,
        in_specs=(
            P(AXES, None, None),
            P(AXES),
            P(AXES, None),
            P(),
            P(),
            P(AXES, None),
            P(),
            P(),
            P(),
            P(),
        ),
        out_specs=(P(AXES, None, None), P(None, AXES)),
        check_vma=False,
    )
```

```python
import math

import jax
import jax.numpy as jnp
import numpy as np
from jax import lax
from jax.experimental import pallas as pl
from jax.experimental.pallas import tpu as pltpu
from jax.sharding import PartitionSpec as P


HD = 64
REACH = 2
AXES = ("space", "chan")
NEG = -1e30
TILES = 88
F32 = jnp.float32
SMALL = pl.CostEstimate(flops=1 << 20, bytes_accessed=1 << 16, transcendentals=0)
BF16 = jnp.bfloat16
VM = pltpu.VMEM
NT = (((1,), (1,)), ((), ()))
SCALE = HD ** (-0.5) * math.log2(math.e)
LIMIT = pltpu.CompilerParams(vmem_limit_bytes=20 << 20)
WHOLE = pltpu.CompilerParams(vmem_limit_bytes=63 << 20)
PACKED = pltpu.CompilerParams(vmem_limit_bytes=20 << 20)


def vmem(count):
    return [pl.BlockSpec(memory_space=pltpu.VMEM)] * count


def smem(count):
    return [pl.BlockSpec(memory_space=pltpu.SMEM)] * count


def anyspace(count):
    return [pl.BlockSpec(memory_space=pl.ANY)] * count


def cost(flops, moved, trans=0):
    return pl.CostEstimate(flops=flops, bytes_accessed=moved, transcendentals=trans)


def swap_blocks(four):
    lane = lax.broadcasted_iota(jnp.int32, four[0].shape, 1)
    low = lane < 64
    even = (lane // 32) % 2 == 0
    half = []
    for a, b in ((0, 2), (1, 3)):
        half.append(jnp.where(low, four[a], pltpu.roll(four[b], 64, 1)))
        half.append(jnp.where(low, pltpu.roll(four[a], 64, 1), four[b]))
    a0, a2, a1, a3 = half
    return [
        jnp.where(even, a0, pltpu.roll(a1, 32, 1)),
        jnp.where(even, pltpu.roll(a0, 96, 1), a1),
        jnp.where(even, a2, pltpu.roll(a3, 32, 1)),
        jnp.where(even, pltpu.roll(a2, 96, 1), a3),
    ]


def lanes_of(half):
    return slice(128 * half, 128 * half + 128)


def pick_rows(first, stride):
    row = lax.broadcasted_iota(jnp.int32, (8, 512), 0)
    col = lax.broadcasted_iota(jnp.int32, (8, 512), 1)
    return jnp.where(row * stride + first == col, 1.0, 0.0)


def rim_rows():
    rows = []
    for z in range(8):
        for first, stride in ((448, 8), (0, 8), (56, 64), (0, 64)):
            rows.append(pick_rows(first + z, stride))
    for z in (0, 7):
        for x in range(8):
            rows.append(pick_rows(64 * x + z, 8))
    return jnp.concatenate(rows, axis=0).astype(BF16)


def alive_rows(rows, alive):
    return jnp.where(alive > 0, rows, jnp.zeros_like(rows))


def prep_kernel(alive, feat, out, occ, faces, masked, picks, sems):
    copies = [
        pltpu.make_async_copy(
            feat.at[pl.ds(8 * two, 8)], masked.at[pl.ds(8 * two, 8)], sems.at[two]
        )
        for two in range(2)
    ]
    flags = pltpu.make_async_copy(alive, occ, sems.at[2])
    flags.start()
    for copy in copies:
        copy.start()
    picks[...] = rim_rows()
    flags.wait()
    sends = []
    for two in range(2):
        copies[two].wait()
        rows = []
        for b in range(8 * two, 8 * two + 8):
            rows.append(alive_rows(masked[b], occ[b]))
        rows = jnp.concatenate(rows, axis=0)
        found = lax.dot_general(picks[...], rows, NT, preferred_element_type=F32).astype(BF16)
        for g in (2 * two, 2 * two + 1):
            for face in range(2):
                sheet = found[256 + 64 * face : 320 + 64 * face, lanes_of(g % 2)]
                for x in range(1, 4):
                    tile = jnp.concatenate(
                        [sheet[8 * x : 8 * x + 8], sheet[8 * x + 24 : 8 * x + 32]], axis=1
                    )
                    faces[64 + (2 * g + face) * 3 + x - 1] = tile
            for half in range(2):
                four = [
                    found[32 * z : 32 * z + 32, lanes_of(g % 2)]
                    for z in range(4 * half, 4 * half + 4)
                ]
                for j, block in enumerate(swap_blocks(four)):
                    for face in range(4):
                        faces[4 * (4 * g + j) + face, :, lanes_of(half)] = block[
                            8 * face : 8 * face + 8
                        ]
        for part, (start, count) in enumerate(((32 * two, 32), (64 + 12 * two, 12))):
            tiles = pl.ds(start, count)
            sends.append(
                pltpu.make_async_copy(faces.at[tiles], out.at[tiles], sems.at[3 + 2 * two + part])
            )
            sends[-1].start()
    for copy in sends:
        copy.wait()


def prep(occ, feat):
    return pl.pallas_call(
        prep_kernel,
        name="prep",
        out_shape=jax.ShapeDtypeStruct((TILES, 8, 256), BF16),
        in_specs=[pl.BlockSpec(memory_space=pltpu.HBM)] * 2,
        out_specs=pl.BlockSpec(memory_space=pltpu.HBM),
        scratch_shapes=[
            pltpu.SMEM((16,), jnp.int32),
            VM((TILES, 8, 256), BF16),
            VM((16, 32, 512), BF16),
            VM((384, 512), BF16),
            pltpu.SemaphoreType.DMA((7,)),
        ],
        compiler_params=WHOLE,
        cost_estimate=cost(1 << 28, 2 << 20),
    )(occ, feat)


def shifted_rows(tile, step):
    if step == 0:
        return tile
    row = lax.broadcasted_iota(jnp.int32, tile.shape, 0) % 8
    if step < 0:
        moved = pltpu.roll(tile, 1, 0)
        return jnp.where(row == 0, 0.0, moved)
    moved = pltpu.roll(tile, tile.shape[0] - 1, 0)
    return jnp.where(row == 7, 0.0, moved)


def joined(pair, *at):
    return jnp.concatenate([pair[(0, *at)], pair[(1, *at)]], axis=1)


def write_patches(lhs, brick, tiles):
    zero = jnp.zeros((8, 256), F32)
    rows = pl.ds(pl.multiple_of(brick * 64, 64), 64)
    for dy in (-1, 0, 1):
        moved = [shifted_rows(t, dy) for t in tiles]
        for dx in (-1, 0, 1):
            picked = [moved[x + dx] if 0 <= x + dx < 8 else zero for x in range(8)]
            tap = (dx + 1) * 3 + dy + 1
            lhs[rows, 256 * tap : 256 * tap + 256] = jnp.concatenate(picked, axis=0).astype(BF16)


def turn(eye, array):
    return lax.dot_general(eye, array, NT, preferred_element_type=F32).astype(BF16)


def turns_kernel(qkv, out_weight, latent, wv_t, wo_t, latent_t, *rest):
    before, after, sems = rest[:3], rest[3:6], rest[6]
    loads = [
        pltpu.make_async_copy(ref, to, sems.at[i])
        for i, (ref, to) in enumerate(zip((qkv.at[2], out_weight, latent), before))
    ]
    for copy in loads:
        copy.start()
    row = lax.broadcasted_iota(jnp.int32, (512, 512), 0)
    col = lax.broadcasted_iota(jnp.int32, (512, 512), 1)
    eye = jnp.where(row == col, 1.0, 0.0).astype(BF16)
    sends = []
    for i, out in enumerate((wv_t, wo_t, latent_t)):
        loads[i].wait()
        after[i][...] = turn(eye, before[i][...])
        sends.append(pltpu.make_async_copy(after[i], out, sems.at[3 + i]))
        sends[-1].start()
    for copy in sends:
        copy.wait()


def turns(qkv, out_weight, latent):
    shapes = ((512, 512), (512, 512), (512, 1024))
    return pl.pallas_call(
        turns_kernel,
        name="turns",
        out_shape=tuple(jax.ShapeDtypeStruct(shape, BF16) for shape in shapes),
        in_specs=[pl.BlockSpec(memory_space=pltpu.HBM)] * 3,
        out_specs=tuple([pl.BlockSpec(memory_space=pltpu.HBM)] * 3),
        scratch_shapes=[VM(shape, BF16) for shape in ((512, 512), (512, 512), (1024, 512), *shapes)]
        + [pltpu.SemaphoreType.DMA((6,))],
        compiler_params=WHOLE,
        cost_estimate=SMALL,
    )(qkv, out_weight, latent)


def bands_kernel(conv, band, band_z, wide):
    row = lax.broadcasted_iota(jnp.int32, (32, 256), 0)
    col = lax.broadcasted_iota(jnp.int32, (32, 256), 1) % 32
    spread = jnp.where(row == col, 1.0, 0.0).astype(BF16)
    for tap in range(27):
        wide[32 * tap : 32 * tap + 32, :] = jnp.dot(
            conv[tap].astype(F32).T.astype(BF16), spread, preferred_element_type=F32
        )
    block = lax.broadcasted_iota(jnp.int32, (32, 256), 1) // 32

    def per_tap(t, carry):
        base = [
            wide[pl.ds(pl.multiple_of((t * 3 + k) * 32, 32), 32), :] for k in range(3)
        ]
        for z in range(8):
            value = jnp.where(block == z, base[1], 0.0)
            value = jnp.where(block == z + 1, base[0], value)
            value = jnp.where(block == z - 1, base[2], value)
            band[pl.ds(pl.multiple_of(t * 256 + 32 * z, 32), 32), :] = value.astype(BF16)
        return carry

    lax.fori_loop(0, 9, per_tap, 0)
    for dy in range(3):
        for face, k in ((0, 0), (1, 2)):
            value = jnp.zeros((32, 256), F32)
            for dx in range(3):
                start = ((dx * 3 + dy) * 3 + k) * 32
                value = jnp.where(block == 2 * dx + face, wide[start : start + 32, :], value)
            for j in range(4):
                start = dy * 256 + 128 * face + 32 * j
                band_z[start : start + 32, :] = value.astype(BF16)


def bands(conv_weight):
    return pl.pallas_call(
        bands_kernel,
        name="bands",
        out_shape=(
            jax.ShapeDtypeStruct((2304, 256), BF16),
            jax.ShapeDtypeStruct((768, 256), BF16),
        ),
        in_specs=vmem(1),
        out_specs=tuple(vmem(2)),
        scratch_shapes=[VM((864, 256), F32)],
        compiler_params=LIMIT,
        cost_estimate=SMALL,
    )(conv_weight)


def spread_kernel(occ, feat, xb, masked):
    for b in range(16):
        masked[32 * b : 32 * b + 32, :] = alive_rows(feat[b], occ[b])
    order = [pick_rows(64 * x + z, 8) for z in range(8) for x in range(8)]
    order = jnp.concatenate(order, axis=0).astype(BF16)
    for two in range(2):
        found = lax.dot_general(
            order, masked[256 * two : 256 * two + 256, :], NT, preferred_element_type=F32
        ).astype(BF16)
        for g in (2 * two, 2 * two + 1):
            for half in range(2):
                four = [
                    found[64 * z : 64 * z + 64, lanes_of(g % 2)]
                    for z in range(4 * half, 4 * half + 4)
                ]
                for j, block in enumerate(swap_blocks(four)):
                    xb[half, 4 * g + j] = block.astype(F32)


def spread(occ, feat):
    return pl.pallas_call(
        spread_kernel,
        name="spread",
        out_shape=jax.ShapeDtypeStruct((2, 16, 64, 128), F32),
        in_specs=smem(1) + vmem(1),
        out_specs=vmem(1)[0],
        scratch_shapes=[VM((512, 512), BF16)],
        compiler_params=LIMIT,
        cost_estimate=SMALL,
    )(occ, feat)


def inner_kernel(neighbours, me, xb, band, acc, source, lhs, table):
    core = me[0] % 2
    for away, slot in enumerate((2 + 2 * core, 1 + 2 * core, 0, 3 - 2 * core, 4 - 2 * core)):
        table[away] = slot

    def look_up(b, carry):
        for face in range(6):
            peer = neighbours[face, b]
            safe = jnp.maximum(peer, 0)
            away = jnp.clip(safe // 16 - me[0], -REACH, REACH)
            start = table[away + REACH] * TILES
            brick = safe % 16
            source[b * 16 + face] = jnp.where(peer >= 0, start + brick * 4, 5 * TILES)
            if face >= 4:
                sheet = start + 64 + (brick // 4 * 2 + (5 - face)) * 3
                source[b * 16 + face + 2] = jnp.where(peer >= 0, sheet, 5 * TILES)
                source[b * 16 + face + 4] = brick % 4
        return carry

    lax.fori_loop(0, 16, look_up, 0)

    def per_brick(b, carry):
        write_patches(lhs, b, [joined(xb, b, slice(8 * x, 8 * x + 8)) for x in range(8)])
        return carry

    lax.fori_loop(0, 16, per_brick, 0)

    def per_rows(i, carry):
        rows = pl.ds(pl.multiple_of(i * 512, 512), 512)
        acc[rows, :] = jnp.dot(lhs[rows, :], band[...], preferred_element_type=F32)
        return carry

    lax.fori_loop(0, 2, per_rows, 0)


def inner(neighbours, me, xb, band):
    return pl.pallas_call(
        inner_kernel,
        name="inner",
        out_shape=(
            jax.ShapeDtypeStruct((1024, 256), F32),
            jax.ShapeDtypeStruct((256,), jnp.int32),
        ),
        in_specs=smem(2) + vmem(2),
        out_specs=tuple(vmem(1) + smem(1)),
        scratch_shapes=[VM((1024, 2304), BF16), pltpu.SMEM((8,), jnp.int32)],
        compiler_params=LIMIT,
        cost_estimate=SMALL,
    )(neighbours, me, xb, band)


def outer_kernel(
    source, occ, me, own, near, far, partner, relay, xb, acc, band, band_z, bias, pool, pick,
    latent, proj, gain,
    blocks, pooled, to_partner, to_cross,
    store, lhs, flat, edges, sums, halves, sems,
):
    copies = [
        pltpu.make_async_copy(ref, store.at[pl.ds(slot * TILES, TILES)], sems.at[slot])
        for slot, ref in enumerate((own, near, far, partner, relay))
    ]
    for copy in copies:
        copy.start()
    core = me[0] % 2
    store[5 * TILES : 5 * TILES + 8] = jnp.zeros((8, 8, 256), BF16)
    for copy in copies:
        copy.wait()
    lane = lax.broadcasted_iota(jnp.int32, (8, 256), 1) % 128 // 32

    def gather(b, carry):
        for face in range(4):
            tile = store[source[b * 16 + face] + face].astype(F32)
            flat[face, pl.ds(pl.multiple_of(b * 8, 8), 8), :] = tile
        pair = []
        for face in range(2):
            edge = source[b * 16 + 4 + face]
            sheet = source[b * 16 + 6 + face]
            mask = lane == source[b * 16 + 8 + face]
            part = lanes_of(1 - face)
            rim = lane[:, :128] == (3 if face == 0 else 0)
            first = jnp.where(rim, store[edge + 1].astype(F32)[:, part], 0.0)
            final = jnp.where(rim, store[edge].astype(F32)[:, part], 0.0)
            mids = [jnp.where(mask, store[sheet + k].astype(F32), 0.0) for k in range(3)]
            pair.append(
                [first] + [m[:, :128] for m in mids] + [m[:, 128:] for m in mids] + [final]
            )
        tiles = [jnp.concatenate([pair[0][x], pair[1][x]], axis=1) for x in range(8)]
        rows = pl.ds(pl.multiple_of(b * 64, 64), 64)
        for dy in (-1, 0, 1):
            moved = [shifted_rows(t, dy) for t in tiles]
            start = 256 * (dy + 1)
            lhs[rows, start : start + 256] = jnp.concatenate(moved, axis=0).astype(BF16)
        return carry

    lax.fori_loop(0, 16, gather, 0)
    for face in range(4):
        sheet = flat[face]
        side = 0 if face % 2 == 0 else 2
        total = None
        for step in (-1, 0, 1):
            tap = side * 3 + step + 1 if face < 2 else (step + 1) * 3 + side
            part = jnp.dot(
                shifted_rows(sheet, step).astype(BF16),
                band[256 * tap : 256 * tap + 256, :],
                preferred_element_type=F32,
            )
            total = part if total is None else total + part
        edges[face] = total
    sums[...] = jnp.dot(lhs[...], band_z[...], preferred_element_type=F32)
    row = lax.broadcasted_iota(jnp.int32, (8, 256), 0)
    shift = jnp.concatenate([bias[...]] * 8, axis=1)
    one = lax.broadcasted_iota(jnp.int32, (8, 128), 1)

    def finish(b, alive):
        start = pl.multiple_of(b * 64, 64)
        sheet_rows = pl.ds(pl.multiple_of(b * 8, 8), 8)
        y_low, y_high = edges[2, sheet_rows, :], edges[3, sheet_rows, :]
        done = []
        for x in range(8):
            tile_rows = pl.ds(start + 8 * x, 8)
            rim = pltpu.roll(sums[tile_rows, 0:128], 64, 1)
            if x > 0:
                rim = rim + sums[pl.ds(start + 8 * x - 8, 8), 0:128]
            if x < 7:
                rim = rim + sums[pl.ds(start + 8 * x + 8, 8), 128:256]
            rim = jnp.concatenate(
                [
                    jnp.where(one < 32, rim, 0.0),
                    jnp.where(one >= 96, pltpu.roll(rim, 64, 1), 0.0),
                ],
                axis=1,
            )
            total = acc[tile_rows, :] + rim
            total = total + jnp.where(row == 0, y_low[x : x + 1, :], 0.0)
            total = total + jnp.where(row == 7, y_high[x : x + 1, :], 0.0)
            if x == 0:
                total = total + edges[0, sheet_rows, :]
            if x == 7:
                total = total + edges[1, sheet_rows, :]
            value = total + shift
            kept = joined(xb, b, slice(8 * x, 8 * x + 8))
            value = 0.5 * value
            done.append(alive * (kept + (value + value * jnp.tanh(value))))
        block = jnp.concatenate(done, axis=0).astype(BF16)
        for half in range(2):
            blocks[half, b] = block[:, lanes_of(half)]
        cells = jnp.dot(pool[...], block, preferred_element_type=F32) * pick[...]
        cells = cells[:, :128] + cells[:, 128:]
        cells = cells + pltpu.roll(cells, 64, 1)
        cells = cells + pltpu.roll(cells, 32, 1)
        pooled[pl.ds(start, 64), :] = cells.astype(BF16)

    def finish_four(i, carry):
        for k in range(4):
            finish(4 * i + k, occ[4 * i + k].astype(F32))
        return carry

    lax.fori_loop(0, 4, finish_four, 0)

    def norm(i, carry):
        rows = pl.ds(pl.multiple_of(i * 256, 256), 256)
        lifted = jnp.dot(pooled[rows, 0:32], proj[...], preferred_element_type=F32)
        mixed = latent[rows, :].astype(F32) + lifted
        scale = lax.rsqrt(jnp.mean(mixed * mixed, axis=-1, keepdims=True) + 1e-06)
        halves[i // 2, pl.ds(pl.multiple_of(i % 2 * 256, 256), 256), :] = (
            mixed * scale * gain[...]
        ).astype(BF16)
        return carry

    lax.fori_loop(0, 4, norm, 0)
    flag_row = lax.broadcasted_iota(jnp.int32, (16, 512), 0)
    flag_lane = lax.broadcasted_iota(jnp.int32, (16, 512), 1) // 64
    for half in range(2):
        flags = jnp.zeros((16, 512), F32)
        for b in range(8):
            here = (flag_row == 8 + b) | ((flag_row == 0) & (flag_lane == b))
            flags = jnp.where(here, occ[8 * half + b].astype(F32), flags)
        halves[half, 512:528, :] = flags.astype(BF16)
    out = [
        pltpu.make_async_copy(halves.at[1 - core], to_partner, sems.at[5]),
        pltpu.make_async_copy(halves.at[core], to_cross, sems.at[6]),
    ]
    for copy in out:
        copy.start()
    for copy in out:
        copy.wait()


def outer(source, occ, me, stores, xb, acc, band, band_z, bias, latent, proj, gain):
    return pl.pallas_call(
        outer_kernel,
        name="outer",
        out_shape=(
            jax.ShapeDtypeStruct((2, 16, 64, 128), BF16),
            jax.ShapeDtypeStruct((1024, 128), BF16),
            jax.ShapeDtypeStruct((528, 512), BF16),
            jax.ShapeDtypeStruct((528, 512), BF16),
        ),
        in_specs=smem(3) + anyspace(5) + vmem(10),
        out_specs=tuple(vmem(2) + anyspace(2)),
        scratch_shapes=[
            VM((5 * TILES + 8, 8, 256), BF16),
            VM((1024, 768), BF16),
            VM((4, 128, 256), F32),
            VM((4, 128, 256), F32),
            VM((1024, 256), F32),
            VM((2, 528, 512), BF16),
            pltpu.SemaphoreType.DMA((7,)),
        ],
        compiler_params=LIMIT,
        cost_estimate=cost(2 * 1024 * 2304 * 256, 8 << 20, 1 << 18),
    )(source, occ, me, *stores, xb, acc, band, band_z, bias, *pool_tables(), latent, proj, gain)


def restore_kernel(blocks, out, turned):
    row = lax.broadcasted_iota(jnp.int32, (128, 128), 0)
    col = lax.broadcasted_iota(jnp.int32, (128, 128), 1)
    eye = jnp.where(row == col, 1.0, 0.0).astype(BF16)
    for g in range(4):
        for half in range(2):
            four = [blocks[half, 4 * g + j] for j in range(4)]
            for k, sheet in enumerate(swap_blocks(four)):
                turned[g, pl.ds(4 * half + k, 64, stride=8), :] = sheet.astype(F32)
    for g in range(4):
        rows = turn(eye, turned[g].astype(BF16))
        for j in range(4):
            out[4 * g + j] = rows[32 * j : 32 * j + 32]


def restore(blocks):
    return pl.pallas_call(
        restore_kernel,
        name="restore",
        out_shape=jax.ShapeDtypeStruct((16, 32, 512), BF16),
        in_specs=vmem(1),
        out_specs=vmem(1)[0],
        scratch_shapes=[VM((4, 512, 128), F32)],
        compiler_params=LIMIT,
        cost_estimate=cost(1 << 20, 2 << 20),
    )(blocks)


def column_max(part):
    return jnp.max(part, axis=0, keepdims=True)


def in_range(total):
    return jnp.where((total > 2.0**-60) & (total < 2.0**60), 1.0, 0.0)


def block_max(scores, biases):
    top = None
    for b in range(8):
        part = scores[64 * b : 64 * b + 8]
        for k in range(1, 8):
            part = jnp.maximum(part, scores[64 * b + 8 * k : 64 * b + 8 * k + 8])
        part = part + biases[b]
        top = part if top is None else jnp.maximum(top, part)
    return column_max(top)


def shifted_weights(scores, top, biases):
    parts = [
        jnp.exp2(scores[64 * b : 64 * b + 64] - (top - biases[b])).astype(BF16) for b in range(8)
    ]
    return jnp.concatenate(parts, axis=0)


def keys_values(rows, wk, wv_t, alive, keys, values, raw):
    found = jnp.dot(rows, wk, preferred_element_type=F32)
    for pair in range(4):
        keys[pair] = found[:, 128 * pair : 128 * pair + 128].astype(BF16)
    found = lax.dot_general(wv_t, rows, NT, preferred_element_type=F32)
    ones = jnp.ones((16, 512), F32)
    for head in range(8):
        block = found[64 * head : 64 * head + 64]
        if raw is not None:
            raw[head, 0:64, :] = block.astype(BF16)
            raw[head, 64:80, :] = ones.astype(BF16)
        values[head, 0:64, :] = (block * alive).astype(BF16)
        values[head, 64:80, :] = (ones * alive).astype(BF16)
    return jnp.max(jnp.abs(found))


def project_kernel(
    me, to_partner, to_cross, qkv, wv_t, query, keys, values, raw, alive, small, normed, sems
):
    core = me[0] % 2
    copies = [
        pltpu.make_async_copy(to_partner, normed.at[1 - core], sems.at[0]),
        pltpu.make_async_copy(to_cross, normed.at[core], sems.at[1]),
    ]
    for copy in copies:
        copy.start()
    for copy in copies:
        copy.wait()
    lane = lax.broadcasted_iota(jnp.int32, (512, 128), 1)
    tops = []
    for half in range(2):
        flags = normed[half, 512:528, :].astype(F32)[0:1]
        alive[half] = jnp.broadcast_to(flags, (8, 512))
        rows = normed[half, 0:512, :]
        found = jnp.dot(rows, qkv[0], preferred_element_type=F32) * SCALE
        for head in range(8):
            pair = found[:, 128 * (head // 2) : 128 * (head // 2) + 128]
            keep = lane < 64 if head % 2 == 0 else lane >= 64
            query[head, half] = jnp.where(keep, pair, 0.0).astype(BF16)
        tops.append(
            keys_values(
                rows, qkv[1], wv_t[...], flags, keys.at[half], values.at[half], raw.at[half]
            )
        )
    small[0] = (jnp.maximum(tops[0], tops[1]) < 1e12).astype(F32)


def project(me, to_partner, to_cross, qkv, wv_t):
    return pl.pallas_call(
        project_kernel,
        name="project",
        out_shape=(
            jax.ShapeDtypeStruct((8, 2, 512, 128), BF16),
            jax.ShapeDtypeStruct((2, 4, 512, 128), BF16),
            jax.ShapeDtypeStruct((2, 8, 80, 512), BF16),
            jax.ShapeDtypeStruct((2, 8, 80, 512), BF16),
            jax.ShapeDtypeStruct((2, 8, 512), F32),
            jax.ShapeDtypeStruct((8,), F32),
        ),
        in_specs=smem(1) + anyspace(2) + vmem(2),
        out_specs=tuple(vmem(5) + smem(1)),
        scratch_shapes=[VM((2, 528, 512), BF16), pltpu.SemaphoreType.DMA((2,))],
        compiler_params=PACKED,
        cost_estimate=cost(3 << 30, 6 << 20),
    )(me, to_partner, to_cross, qkv, wv_t)


def own_kernel(
    occ, small, query, keys, values, raw, alive_rows, state, peak, stats, even, odd
):
    alive = [alive_rows[half, 0:1, :] for half in range(2)]
    row = lax.broadcasted_iota(jnp.int32, (128, 128), 0)
    col = lax.broadcasted_iota(jnp.int32, (128, 128), 1)
    eye = row == col

    stats[0] = 0.0

    @pl.when(small[0] > 0.5)
    def plain():
        def score(head, into, unit):
            for half in (unit // 2,):
                for tile in (unit % 2,):
                    into[2 * half + tile] = lax.dot_general(
                        keys[half, head // 2],
                        query[head, half, 256 * tile : 256 * tile + 256, :],
                        NT,
                        preferred_element_type=F32,
                    )

        def attend(head, scores, unit):
            good = None
            for half in (unit // 2,):
                for tile in (unit % 2,):
                    lanes = slice(256 * tile, 256 * tile + 256)
                    parts, own = [], []
                    for chunk in range(4):
                        weights = jnp.exp2(
                            scores[2 * half + tile, 128 * chunk : 128 * chunk + 128, :]
                        )
                        if chunk // 2 == tile:
                            first = 128 * (chunk % 2)
                            block = weights[:, first : first + 128]
                            own.append(
                                jnp.sum(jnp.where(eye, block, 0.0), axis=0, keepdims=True)
                            )
                        parts.append(weights.astype(BF16))
                    out = jnp.dot(
                        values[half, head],
                        jnp.concatenate(parts, axis=0),
                        preferred_element_type=F32,
                    )
                    extra = jnp.concatenate(own, axis=1) * (1.0 - alive[half][:, lanes])
                    out = out + extra * raw[half, head, :, lanes].astype(F32)
                    state[head, half, :, lanes] = out[0:72]
                    peak[head, half, :, lanes] = jnp.zeros((8, 256), F32)
                    good = in_range(out[64:72])
            return good

        for unit in range(4):
            score(0, even, unit)

        def per_two(i, good):
            for unit in range(4):
                score(2 * i + 1, odd, unit)
                good = good * attend(2 * i, even, unit)
            for unit in range(4):
                score(jnp.minimum(2 * i + 2, 7), even, unit)
                good = good * attend(2 * i + 1, odd, unit)
            return good

        stats[0] = jnp.min(lax.fori_loop(0, 4, per_two, jnp.ones((8, 256), F32)))

    @pl.when(stats[0] < 0.5)
    def general():
        def per_head(head, carry):
            for half in range(2):
                biases = [
                    jnp.where(occ[8 * half + b] > 0, 0.0, NEG).astype(F32) for b in range(8)
                ]
                for tile in range(2):
                    lanes = slice(256 * tile, 256 * tile + 256)
                    scores = lax.dot_general(
                        keys[half, head // 2],
                        query[head, half, lanes, :],
                        NT,
                        preferred_element_type=F32,
                    )
                    selves = []
                    for k in range(2):
                        first = 256 * tile + 128 * k
                        block = scores[first : first + 128, 128 * k : 128 * k + 128]
                        selves.append(column_max(jnp.where(eye, block, NEG)))
                    dead = alive[half][:, lanes] < 0.5
                    own = jnp.where(dead, jnp.concatenate(selves, axis=1), NEG)
                    top = jnp.maximum(block_max(scores, biases), own)
                    out = jnp.dot(
                        values[half, head],
                        shifted_weights(scores, top, biases),
                        preferred_element_type=F32,
                    )
                    extra = jnp.where(dead, jnp.exp2(own - top), 0.0)
                    out = out + extra * raw[half, head, :, lanes].astype(F32)
                    state[head, half, :, lanes] = out[0:72]
                    peak[head, half, :, lanes] = jnp.broadcast_to(top, (8, 256))
            return carry

        lax.fori_loop(0, 8, per_head, 0)


def own_attention(occ, small, *operands):
    return pl.pallas_call(
        own_kernel,
        name="own_attention",
        out_shape=(
            jax.ShapeDtypeStruct((8, 2, 72, 512), F32),
            jax.ShapeDtypeStruct((8, 2, 8, 512), F32),
            jax.ShapeDtypeStruct((8,), F32),
        ),
        in_specs=smem(2) + vmem(5),
        out_specs=tuple(vmem(2) + smem(1)),
        scratch_shapes=[VM((4, 512, 256), F32), VM((4, 512, 256), F32)],
        compiler_params=PACKED,
        cost_estimate=cost(3 << 30, 8 << 20, 1 << 22),
    )(occ, small, *operands)


def side_kernel(
    me, stats, remote, query, state, peak, qkv, wv_t, wo_t, latent_t, proj, pooled, *rest
):
    last = len(rest) == 10
    if last:
        other, out, keys, values, attended, even, odd, fast, result, sems = rest
        half = me[0] % 2
        place = pl.ds(pl.multiple_of((1 - half) * 512, 512), 512)
        send = pltpu.make_async_copy(other, out.at[:, place], sems.at[2])
        send.start()
    else:
        out, keys, values, attended, even, odd, fast = rest
        half = 1 - me[0] % 2
    flags = remote[512:528, :].astype(F32)
    value_peak = keys_values(
        remote[0:512, :], qkv[1], wv_t[...], flags[0:1], keys, values, None
    )
    fast[0] = 0.0

    def finish(head, lanes, total):
        result = total[0:64] / total[64:65]
        attended[pl.ds(pl.multiple_of(head * 64, 64), 64), lanes] = result.astype(BF16)

    @pl.when((value_peak < 1e12) & (stats[0] > 0.5))
    def plain():
        def score(pair, into, unit):
            into[unit] = lax.dot_general(
                keys[pair],
                query[2 * pair + unit // 2, half, 256 * (unit % 2) : 256 * (unit % 2) + 256, :],
                NT,
                preferred_element_type=F32,
            )

        def attend(pair, scores, unit):
            lanes = slice(256 * (unit % 2), 256 * (unit % 2) + 256)
            head = 2 * pair + unit // 2
            parts = [
                jnp.exp2(scores[unit, 128 * chunk : 128 * chunk + 128, :]).astype(BF16)
                for chunk in range(4)
            ]
            total = jnp.dot(
                values[head], jnp.concatenate(parts, axis=0), preferred_element_type=F32
            )
            total = total[0:72] + state[head, half, :, lanes]
            finish(head, lanes, total)
            return in_range(total[64:72])

        for unit in range(4):
            score(0, even, unit)

        def per_two(i, good):
            for unit in range(4):
                score(2 * i + 1, odd, unit)
                good = good * attend(2 * i, even, unit)
            for unit in range(4):
                score(jnp.minimum(2 * i + 2, 3), even, unit)
                good = good * attend(2 * i + 1, odd, unit)
            return good

        fast[0] = jnp.min(lax.fori_loop(0, 2, per_two, jnp.ones((8, 256), F32)))

    @pl.when(fast[0] < 0.5)
    def general():
        biases = [jnp.where(flags[8 + b : 9 + b, 0:256] > 0.5, 0.0, NEG) for b in range(8)]

        def per_head(head, carry):
            for tile in range(2):
                lanes = slice(256 * tile, 256 * tile + 256)
                scores = lax.dot_general(
                    keys[head // 2], query[head, half, lanes, :], NT, preferred_element_type=F32
                )
                before = peak[head, half, 0:1, lanes]
                top = jnp.maximum(block_max(scores, biases), before)
                total = jnp.dot(
                    values[head], shifted_weights(scores, top, biases), preferred_element_type=F32
                )
                finish(
                    head, lanes, total[0:72] + state[head, half, :, lanes] * jnp.exp2(before - top)
                )
            return carry

        lax.fori_loop(0, 8, per_head, 0)

    place = pl.ds(pl.multiple_of(half * 512, 512), 512)
    proj_t = proj[...].astype(F32).T.astype(BF16)
    copies = []
    for i in range(2):
        rows = slice(256 * i, 256 * i + 256)
        mixing = jnp.dot(wo_t[rows, :], attended[...], preferred_element_type=F32)
        lifted = lax.dot_general(
            proj_t[rows], pooled[place, 0:32], NT, preferred_element_type=F32
        )
        block = ((latent_t[rows, place].astype(F32) + lifted) + mixing).astype(BF16)
        if last:
            result[rows, :] = block
            copies.append(pltpu.make_async_copy(result.at[rows], out.at[rows, place], sems.at[i]))
            copies[-1].start()
        else:
            out[rows, :] = block
    if last:
        copies.append(send)
    for copy in copies:
        copy.wait()


def side_attention(me, stats, remote, *shared, other):
    last = other is not None
    return pl.pallas_call(
        side_kernel,
        name="last_attention" if last else "side_attention",
        out_shape=jax.ShapeDtypeStruct((512, 1024 if last else 512), BF16),
        in_specs=smem(2) + vmem(len(shared) + 1 + last),
        out_specs=pl.BlockSpec(memory_space=pltpu.HBM) if last else vmem(1)[0],
        scratch_shapes=[
            VM((4, 512, 128), BF16),
            VM((8, 80, 512), BF16),
            VM((512, 512), BF16),
            VM((4, 512, 256), F32),
            VM((4, 512, 256), F32),
            pltpu.SMEM((1,), F32),
        ]
        + ([VM((512, 512), BF16), pltpu.SemaphoreType.DMA((3,))] if last else []),
        compiler_params=PACKED,
        cost_estimate=cost(4 << 30, 6 << 20, 1 << 21),
    )(me, stats, remote, *shared, *([other] if last else []))


def pool_tables():
    pool = np.zeros((64, 64), np.float32)
    pick = np.zeros((64, 256), np.float32)
    for token in range(64):
        p = (token // 32) * 2 + token // 4 % 2
        q = (token // 16 % 2) * 2 + token // 2 % 2
        r = (token // 8 % 2) * 2 + token % 2
        for x in (2 * p, 2 * p + 1):
            for y in (2 * q, 2 * q + 1):
                pool[token, 8 * x + y] = 0.125
        pick[token, 64 * r : 64 * r + 64] = 1.0
    return jnp.asarray(pool, BF16), jnp.asarray(pick, F32)


def swapped(array):
    size = lax.axis_size(AXES)
    return lax.ppermute(array, AXES, [(i, i ^ 1) for i in range(size)])


def crossed(array, wrap):
    size = lax.axis_size(AXES)
    pairs = [(i, i - 1 if i % 2 == 0 else i + 1) for i in range(size)]
    pairs = [(i, j % size) for i, j in pairs if wrap or 0 <= j < size]
    return lax.ppermute(array, AXES, pairs)


def local(
    features, occupancy, neighbours, conv_weight, conv_bias, latent, token_proj, norm_gain,
    qkv_weight, out_weight,
):
    me = lax.axis_index(AXES)
    me_ref = me.astype(jnp.int32).reshape(1)
    faces = prep(occupancy, features)
    near = crossed(faces, False)
    partner = swapped(faces)
    far = crossed(partner, False)
    later, _ = lax.optimization_barrier((latent, partner))
    wv_t, wo_t, latent_t = turns(qkv_weight, out_weight, later)
    conv_weight, _ = lax.optimization_barrier((conv_weight, wo_t))
    band, band_z = bands(conv_weight)
    later, _ = lax.optimization_barrier((features, band_z))
    xb = spread(occupancy, later)
    near, xb = lax.optimization_barrier((near, xb))
    relay = swapped(near)
    acc, source = inner(neighbours.T, me_ref, xb, band)
    far, acc = lax.optimization_barrier((far, acc))
    blocks, pooled, to_partner, to_cross = outer(
        source, occupancy, me_ref, (faces, near, far, partner, relay), xb, acc, band, band_z,
        conv_bias[None, :], latent, token_proj, norm_gain[None, :],
    )
    from_partner = swapped(to_partner)
    query, keys, values, raw, alive, small = project(
        me_ref, to_partner, to_cross, qkv_weight, wv_t
    )
    to_cross, small = lax.optimization_barrier((to_cross, small))
    from_cross = crossed(to_cross, True)
    state, peak, stats = own_attention(occupancy, small, query, keys, values, raw, alive)
    conv_out = restore(blocks)
    shared = (query, state, peak, qkv_weight, wv_t, wo_t, latent_t, token_proj, pooled)
    first = side_attention(me_ref, stats, from_partner, *shared, other=None)
    tokens_out = side_attention(me_ref, stats, from_cross, *shared, other=first)
    return (conv_out, tokens_out)


def solution(mesh):
    return jax.shard_map(
        local,
        mesh=mesh,
        in_specs=(
            P(AXES, None, None),
            P(AXES),
            P(AXES, None),
            P(),
            P(),
            P(AXES, None),
            P(),
            P(),
            P(),
            P(),
        ),
        out_specs=(P(AXES, None, None), P(None, AXES)),
        check_vma=False,
    )
```

```python
import math

import jax
import jax.numpy as jnp
import numpy as np
from jax import lax
from jax.experimental import pallas as pl
from jax.experimental.pallas import tpu as pltpu
from jax.sharding import PartitionSpec as P


HD = 64
REACH = 2
AXES = ("space", "chan")
NEG = -1e30
TILES = 88
F32 = jnp.float32
SMALL = pl.CostEstimate(flops=1 << 20, bytes_accessed=1 << 16, transcendentals=0)
BF16 = jnp.bfloat16
VM = pltpu.VMEM
NT = (((1,), (1,)), ((), ()))
SCALE = HD ** (-0.5) * math.log2(math.e)
LIMIT = pltpu.CompilerParams(vmem_limit_bytes=20 << 20)
WHOLE = pltpu.CompilerParams(vmem_limit_bytes=63 << 20)
PACKED = pltpu.CompilerParams(vmem_limit_bytes=20 << 20)


def vmem(count):
    return [pl.BlockSpec(memory_space=pltpu.VMEM)] * count


def smem(count):
    return [pl.BlockSpec(memory_space=pltpu.SMEM)] * count


def anyspace(count):
    return [pl.BlockSpec(memory_space=pl.ANY)] * count


def cost(flops, moved, trans=0):
    return pl.CostEstimate(flops=flops, bytes_accessed=moved, transcendentals=trans)


def swap_blocks(four):
    lane = lax.broadcasted_iota(jnp.int32, four[0].shape, 1)
    low = lane < 64
    even = (lane // 32) % 2 == 0
    half = []
    for a, b in ((0, 2), (1, 3)):
        half.append(jnp.where(low, four[a], pltpu.roll(four[b], 64, 1)))
        half.append(jnp.where(low, pltpu.roll(four[a], 64, 1), four[b]))
    a0, a2, a1, a3 = half
    return [
        jnp.where(even, a0, pltpu.roll(a1, 32, 1)),
        jnp.where(even, pltpu.roll(a0, 96, 1), a1),
        jnp.where(even, a2, pltpu.roll(a3, 32, 1)),
        jnp.where(even, pltpu.roll(a2, 96, 1), a3),
    ]


def lanes_of(half):
    return slice(128 * half, 128 * half + 128)


def pick_rows(first, stride):
    row = lax.broadcasted_iota(jnp.int32, (8, 512), 0)
    col = lax.broadcasted_iota(jnp.int32, (8, 512), 1)
    return jnp.where(row * stride + first == col, 1.0, 0.0)


def rim_rows():
    rows = []
    for z in range(8):
        for first, stride in ((448, 8), (0, 8), (56, 64), (0, 64)):
            rows.append(pick_rows(first + z, stride))
    for z in (0, 7):
        for x in range(8):
            rows.append(pick_rows(64 * x + z, 8))
    return jnp.concatenate(rows, axis=0).astype(BF16)


def alive_rows(rows, alive):
    return jnp.where(alive > 0, rows, jnp.zeros_like(rows))


def prep_kernel(alive, feat, out, occ, faces, masked, picks, sems):
    copies = [
        pltpu.make_async_copy(
            feat.at[pl.ds(8 * two, 8)], masked.at[pl.ds(8 * two, 8)], sems.at[two]
        )
        for two in range(2)
    ]
    flags = pltpu.make_async_copy(alive, occ, sems.at[2])
    flags.start()
    for copy in copies:
        copy.start()
    picks[...] = rim_rows()
    flags.wait()
    sends = []
    for two in range(2):
        copies[two].wait()
        rows = []
        for b in range(8 * two, 8 * two + 8):
            rows.append(alive_rows(masked[b], occ[b]))
        rows = jnp.concatenate(rows, axis=0)
        found = lax.dot_general(picks[...], rows, NT, preferred_element_type=F32).astype(BF16)
        for g in (2 * two, 2 * two + 1):
            for face in range(2):
                sheet = found[256 + 64 * face : 320 + 64 * face, lanes_of(g % 2)]
                for x in range(1, 4):
                    tile = jnp.concatenate(
                        [sheet[8 * x : 8 * x + 8], sheet[8 * x + 24 : 8 * x + 32]], axis=1
                    )
                    faces[64 + (2 * g + face) * 3 + x - 1] = tile
            for half in range(2):
                four = [
                    found[32 * z : 32 * z + 32, lanes_of(g % 2)]
                    for z in range(4 * half, 4 * half + 4)
                ]
                for j, block in enumerate(swap_blocks(four)):
                    for face in range(4):
                        faces[4 * (4 * g + j) + face, :, lanes_of(half)] = block[
                            8 * face : 8 * face + 8
                        ]
        for part, (start, count) in enumerate(((32 * two, 32), (64 + 12 * two, 12))):
            tiles = pl.ds(start, count)
            sends.append(
                pltpu.make_async_copy(faces.at[tiles], out.at[tiles], sems.at[3 + 2 * two + part])
            )
            sends[-1].start()
    for copy in sends:
        copy.wait()


def prep(occ, feat):
    return pl.pallas_call(
        prep_kernel,
        name="prep",
        out_shape=jax.ShapeDtypeStruct((TILES, 8, 256), BF16),
        in_specs=[pl.BlockSpec(memory_space=pltpu.HBM)] * 2,
        out_specs=pl.BlockSpec(memory_space=pltpu.HBM),
        scratch_shapes=[
            pltpu.SMEM((16,), jnp.int32),
            VM((TILES, 8, 256), BF16),
            VM((16, 32, 512), BF16),
            VM((384, 512), BF16),
            pltpu.SemaphoreType.DMA((7,)),
        ],
        compiler_params=WHOLE,
        cost_estimate=cost(1 << 28, 2 << 20),
    )(occ, feat)


def shifted_rows(tile, step):
    if step == 0:
        return tile
    row = lax.broadcasted_iota(jnp.int32, tile.shape, 0) % 8
    if step < 0:
        moved = pltpu.roll(tile, 1, 0)
        return jnp.where(row == 0, 0.0, moved)
    moved = pltpu.roll(tile, tile.shape[0] - 1, 0)
    return jnp.where(row == 7, 0.0, moved)


def joined(pair, *at):
    return jnp.concatenate([pair[(0, *at)], pair[(1, *at)]], axis=1)


def write_patches(lhs, brick, tiles):
    zero = jnp.zeros((8, 256), F32)
    rows = pl.ds(pl.multiple_of(brick * 64, 64), 64)
    for dy in (-1, 0, 1):
        moved = [shifted_rows(t, dy) for t in tiles]
        for dx in (-1, 0, 1):
            picked = [moved[x + dx] if 0 <= x + dx < 8 else zero for x in range(8)]
            tap = (dx + 1) * 3 + dy + 1
            lhs[rows, 256 * tap : 256 * tap + 256] = jnp.concatenate(picked, axis=0).astype(BF16)


def turn(eye, array):
    return lax.dot_general(eye, array, NT, preferred_element_type=F32).astype(BF16)


def turns_kernel(qkv, out_weight, latent, wv_t, wo_t, latent_t, *rest):
    before, after, sems = rest[:3], rest[3:6], rest[6]
    loads = [
        pltpu.make_async_copy(ref, to, sems.at[i])
        for i, (ref, to) in enumerate(zip((qkv.at[2], out_weight, latent), before))
    ]
    for copy in loads:
        copy.start()
    row = lax.broadcasted_iota(jnp.int32, (512, 512), 0)
    col = lax.broadcasted_iota(jnp.int32, (512, 512), 1)
    eye = jnp.where(row == col, 1.0, 0.0).astype(BF16)
    sends = []
    for i, out in enumerate((wv_t, wo_t, latent_t)):
        loads[i].wait()
        after[i][...] = turn(eye, before[i][...])
        sends.append(pltpu.make_async_copy(after[i], out, sems.at[3 + i]))
        sends[-1].start()
    for copy in sends:
        copy.wait()


def turns(qkv, out_weight, latent):
    shapes = ((512, 512), (512, 512), (512, 1024))
    return pl.pallas_call(
        turns_kernel,
        name="turns",
        out_shape=tuple(jax.ShapeDtypeStruct(shape, BF16) for shape in shapes),
        in_specs=[pl.BlockSpec(memory_space=pltpu.HBM)] * 3,
        out_specs=tuple([pl.BlockSpec(memory_space=pltpu.HBM)] * 3),
        scratch_shapes=[VM(shape, BF16) for shape in ((512, 512), (512, 512), (1024, 512), *shapes)]
        + [pltpu.SemaphoreType.DMA((6,))],
        compiler_params=WHOLE,
        cost_estimate=SMALL,
    )(qkv, out_weight, latent)


def bands_kernel(conv, band, band_z, wide):
    row = lax.broadcasted_iota(jnp.int32, (32, 256), 0)
    col = lax.broadcasted_iota(jnp.int32, (32, 256), 1) % 32
    spread = jnp.where(row == col, 1.0, 0.0).astype(BF16)
    for tap in range(27):
        wide[32 * tap : 32 * tap + 32, :] = jnp.dot(
            conv[tap].astype(F32).T.astype(BF16), spread, preferred_element_type=F32
        )
    block = lax.broadcasted_iota(jnp.int32, (32, 256), 1) // 32

    def per_tap(t, carry):
        base = [
            wide[pl.ds(pl.multiple_of((t * 3 + k) * 32, 32), 32), :] for k in range(3)
        ]
        for z in range(8):
            value = jnp.where(block == z, base[1], 0.0)
            value = jnp.where(block == z + 1, base[0], value)
            value = jnp.where(block == z - 1, base[2], value)
            band[pl.ds(pl.multiple_of(t * 256 + 32 * z, 32), 32), :] = value.astype(BF16)
        return carry

    lax.fori_loop(0, 9, per_tap, 0)
    for dy in range(3):
        for face, k in ((0, 0), (1, 2)):
            value = jnp.zeros((32, 256), F32)
            for dx in range(3):
                start = ((dx * 3 + dy) * 3 + k) * 32
                value = jnp.where(block == 2 * dx + face, wide[start : start + 32, :], value)
            for j in range(4):
                start = dy * 256 + 128 * face + 32 * j
                band_z[start : start + 32, :] = value.astype(BF16)


def bands(conv_weight):
    return pl.pallas_call(
        bands_kernel,
        name="bands",
        out_shape=(
            jax.ShapeDtypeStruct((2304, 256), BF16),
            jax.ShapeDtypeStruct((768, 256), BF16),
        ),
        in_specs=vmem(1),
        out_specs=tuple(vmem(2)),
        scratch_shapes=[VM((864, 256), F32)],
        compiler_params=LIMIT,
        cost_estimate=SMALL,
    )(conv_weight)


def spread_kernel(occ, feat, xb, masked):
    for b in range(16):
        masked[32 * b : 32 * b + 32, :] = alive_rows(feat[b], occ[b])
    order = [pick_rows(64 * x + z, 8) for z in range(8) for x in range(8)]
    order = jnp.concatenate(order, axis=0).astype(BF16)
    for two in range(2):
        found = lax.dot_general(
            order, masked[256 * two : 256 * two + 256, :], NT, preferred_element_type=F32
        ).astype(BF16)
        for g in (2 * two, 2 * two + 1):
            for half in range(2):
                four = [
                    found[64 * z : 64 * z + 64, lanes_of(g % 2)]
                    for z in range(4 * half, 4 * half + 4)
                ]
                for j, block in enumerate(swap_blocks(four)):
                    xb[half, 4 * g + j] = block.astype(F32)


def spread(occ, feat):
    return pl.pallas_call(
        spread_kernel,
        name="spread",
        out_shape=jax.ShapeDtypeStruct((2, 16, 64, 128), F32),
        in_specs=smem(1) + vmem(1),
        out_specs=vmem(1)[0],
        scratch_shapes=[VM((512, 512), BF16)],
        compiler_params=LIMIT,
        cost_estimate=SMALL,
    )(occ, feat)


def inner_kernel(neighbours, me, xb, band, acc, source, lhs, table):
    core = me[0] % 2
    for away, slot in enumerate((2 + 2 * core, 1 + 2 * core, 0, 3 - 2 * core, 4 - 2 * core)):
        table[away] = slot

    def look_up(b, carry):
        for face in range(6):
            peer = neighbours[face, b]
            safe = jnp.maximum(peer, 0)
            away = jnp.clip(safe // 16 - me[0], -REACH, REACH)
            start = table[away + REACH] * TILES
            brick = safe % 16
            source[b * 16 + face] = jnp.where(peer >= 0, start + brick * 4, 5 * TILES)
            if face >= 4:
                sheet = start + 64 + (brick // 4 * 2 + (5 - face)) * 3
                source[b * 16 + face + 2] = jnp.where(peer >= 0, sheet, 5 * TILES)
                source[b * 16 + face + 4] = brick % 4
        return carry

    lax.fori_loop(0, 16, look_up, 0)

    def per_brick(b, carry):
        write_patches(lhs, b, [joined(xb, b, slice(8 * x, 8 * x + 8)) for x in range(8)])
        return carry

    lax.fori_loop(0, 16, per_brick, 0)

    def per_rows(i, carry):
        rows = pl.ds(pl.multiple_of(i * 512, 512), 512)
        acc[rows, :] = jnp.dot(lhs[rows, :], band[...], preferred_element_type=F32)
        return carry

    lax.fori_loop(0, 2, per_rows, 0)


def inner(neighbours, me, xb, band):
    return pl.pallas_call(
        inner_kernel,
        name="inner",
        out_shape=(
            jax.ShapeDtypeStruct((1024, 256), F32),
            jax.ShapeDtypeStruct((256,), jnp.int32),
        ),
        in_specs=smem(2) + vmem(2),
        out_specs=tuple(vmem(1) + smem(1)),
        scratch_shapes=[VM((1024, 2304), BF16), pltpu.SMEM((8,), jnp.int32)],
        compiler_params=LIMIT,
        cost_estimate=SMALL,
    )(neighbours, me, xb, band)


def outer_kernel(
    source, occ, me, own, near, far, partner, relay, xb, acc, band, band_z, bias, pool, pick,
    latent, proj, gain,
    blocks, pooled, to_partner, to_cross,
    store, lhs, flat, edges, sums, halves, sems,
):
    copies = [
        pltpu.make_async_copy(ref, store.at[pl.ds(slot * TILES, TILES)], sems.at[slot])
        for slot, ref in enumerate((own, near, far, partner, relay))
    ]
    for copy in copies:
        copy.start()
    core = me[0] % 2
    store[5 * TILES : 5 * TILES + 8] = jnp.zeros((8, 8, 256), BF16)
    for copy in copies:
        copy.wait()
    lane = lax.broadcasted_iota(jnp.int32, (8, 256), 1) % 128 // 32

    def gather(b, carry):
        for face in range(4):
            tile = store[source[b * 16 + face] + face].astype(F32)
            flat[face, pl.ds(pl.multiple_of(b * 8, 8), 8), :] = tile
        pair = []
        for face in range(2):
            edge = source[b * 16 + 4 + face]
            sheet = source[b * 16 + 6 + face]
            mask = lane == source[b * 16 + 8 + face]
            part = lanes_of(1 - face)
            rim = lane[:, :128] == (3 if face == 0 else 0)
            first = jnp.where(rim, store[edge + 1].astype(F32)[:, part], 0.0)
            final = jnp.where(rim, store[edge].astype(F32)[:, part], 0.0)
            mids = [jnp.where(mask, store[sheet + k].astype(F32), 0.0) for k in range(3)]
            pair.append(
                [first] + [m[:, :128] for m in mids] + [m[:, 128:] for m in mids] + [final]
            )
        tiles = [jnp.concatenate([pair[0][x], pair[1][x]], axis=1) for x in range(8)]
        rows = pl.ds(pl.multiple_of(b * 64, 64), 64)
        for dy in (-1, 0, 1):
            moved = [shifted_rows(t, dy) for t in tiles]
            start = 256 * (dy + 1)
            lhs[rows, start : start + 256] = jnp.concatenate(moved, axis=0).astype(BF16)
        return carry

    lax.fori_loop(0, 16, gather, 0)
    for face in range(4):
        sheet = flat[face]
        side = 0 if face % 2 == 0 else 2
        total = None
        for step in (-1, 0, 1):
            tap = side * 3 + step + 1 if face < 2 else (step + 1) * 3 + side
            part = jnp.dot(
                shifted_rows(sheet, step).astype(BF16),
                band[256 * tap : 256 * tap + 256, :],
                preferred_element_type=F32,
            )
            total = part if total is None else total + part
        edges[face] = total
    sums[...] = jnp.dot(lhs[...], band_z[...], preferred_element_type=F32)
    row = lax.broadcasted_iota(jnp.int32, (8, 256), 0)
    shift = jnp.concatenate([bias[...]] * 8, axis=1)
    one = lax.broadcasted_iota(jnp.int32, (8, 128), 1)

    def finish(b, alive):
        start = pl.multiple_of(b * 64, 64)
        sheet_rows = pl.ds(pl.multiple_of(b * 8, 8), 8)
        y_low, y_high = edges[2, sheet_rows, :], edges[3, sheet_rows, :]
        done = []
        for x in range(8):
            tile_rows = pl.ds(start + 8 * x, 8)
            rim = pltpu.roll(sums[tile_rows, 0:128], 64, 1)
            if x > 0:
                rim = rim + sums[pl.ds(start + 8 * x - 8, 8), 0:128]
            if x < 7:
                rim = rim + sums[pl.ds(start + 8 * x + 8, 8), 128:256]
            rim = jnp.concatenate(
                [
                    jnp.where(one < 32, rim, 0.0),
                    jnp.where(one >= 96, pltpu.roll(rim, 64, 1), 0.0),
                ],
                axis=1,
            )
            total = acc[tile_rows, :] + rim
            total = total + jnp.where(row == 0, y_low[x : x + 1, :], 0.0)
            total = total + jnp.where(row == 7, y_high[x : x + 1, :], 0.0)
            if x == 0:
                total = total + edges[0, sheet_rows, :]
            if x == 7:
                total = total + edges[1, sheet_rows, :]
            value = total + shift
            kept = joined(xb, b, slice(8 * x, 8 * x + 8))
            value = 0.5 * value
            done.append(alive * (kept + (value + value * jnp.tanh(value))))
        block = jnp.concatenate(done, axis=0).astype(BF16)
        for half in range(2):
            blocks[half, b] = block[:, lanes_of(half)]
        cells = jnp.dot(pool[...], block, preferred_element_type=F32) * pick[...]
        cells = cells[:, :128] + cells[:, 128:]
        cells = cells + pltpu.roll(cells, 64, 1)
        cells = cells + pltpu.roll(cells, 32, 1)
        pooled[pl.ds(start, 64), :] = cells.astype(BF16)

    def finish_four(i, carry):
        for k in range(4):
            finish(4 * i + k, occ[4 * i + k].astype(F32))
        return carry

    lax.fori_loop(0, 4, finish_four, 0)

    def norm(i, carry):
        rows = pl.ds(pl.multiple_of(i * 256, 256), 256)
        lifted = jnp.dot(pooled[rows, 0:32], proj[...], preferred_element_type=F32)
        mixed = latent[rows, :].astype(F32) + lifted
        scale = lax.rsqrt(jnp.mean(mixed * mixed, axis=-1, keepdims=True) + 1e-06)
        halves[i // 2, pl.ds(pl.multiple_of(i % 2 * 256, 256), 256), :] = (
            mixed * scale * gain[...]
        ).astype(BF16)
        return carry

    lax.fori_loop(0, 4, norm, 0)
    flag_row = lax.broadcasted_iota(jnp.int32, (16, 512), 0)
    flag_lane = lax.broadcasted_iota(jnp.int32, (16, 512), 1) // 64
    for half in range(2):
        flags = jnp.zeros((16, 512), F32)
        for b in range(8):
            here = (flag_row == 8 + b) | ((flag_row == 0) & (flag_lane == b))
            flags = jnp.where(here, occ[8 * half + b].astype(F32), flags)
        halves[half, 512:528, :] = flags.astype(BF16)
    out = [
        pltpu.make_async_copy(halves.at[1 - core], to_partner, sems.at[5]),
        pltpu.make_async_copy(halves.at[core], to_cross, sems.at[6]),
    ]
    for copy in out:
        copy.start()
    for copy in out:
        copy.wait()


def outer(source, occ, me, stores, xb, acc, band, band_z, bias, latent, proj, gain):
    return pl.pallas_call(
        outer_kernel,
        name="outer",
        out_shape=(
            jax.ShapeDtypeStruct((2, 16, 64, 128), BF16),
            jax.ShapeDtypeStruct((1024, 128), BF16),
            jax.ShapeDtypeStruct((528, 512), BF16),
            jax.ShapeDtypeStruct((528, 512), BF16),
        ),
        in_specs=smem(3) + anyspace(5) + vmem(10),
        out_specs=tuple(vmem(2) + anyspace(2)),
        scratch_shapes=[
            VM((5 * TILES + 8, 8, 256), BF16),
            VM((1024, 768), BF16),
            VM((4, 128, 256), F32),
            VM((4, 128, 256), F32),
            VM((1024, 256), F32),
            VM((2, 528, 512), BF16),
            pltpu.SemaphoreType.DMA((7,)),
        ],
        compiler_params=PACKED,
        cost_estimate=cost(2 * 1024 * 2304 * 256, 8 << 20, 1 << 18),
    )(source, occ, me, *stores, xb, acc, band, band_z, bias, *pool_tables(), latent, proj, gain)


def restore_kernel(blocks, out, turned):
    row = lax.broadcasted_iota(jnp.int32, (128, 128), 0)
    col = lax.broadcasted_iota(jnp.int32, (128, 128), 1)
    eye = jnp.where(row == col, 1.0, 0.0).astype(BF16)
    for g in range(4):
        for half in range(2):
            four = [blocks[half, 4 * g + j] for j in range(4)]
            for k, sheet in enumerate(swap_blocks(four)):
                turned[g, pl.ds(4 * half + k, 64, stride=8), :] = sheet.astype(F32)
    for g in range(4):
        rows = turn(eye, turned[g].astype(BF16))
        for j in range(4):
            out[4 * g + j] = rows[32 * j : 32 * j + 32]


def restore(blocks):
    return pl.pallas_call(
        restore_kernel,
        name="restore",
        out_shape=jax.ShapeDtypeStruct((16, 32, 512), BF16),
        in_specs=vmem(1),
        out_specs=vmem(1)[0],
        scratch_shapes=[VM((4, 512, 128), F32)],
        compiler_params=LIMIT,
        cost_estimate=cost(1 << 20, 2 << 20),
    )(blocks)


def column_max(part):
    return jnp.max(part, axis=0, keepdims=True)


def in_range(total):
    return jnp.where((total > 2.0**-60) & (total < 2.0**60), 1.0, 0.0)


def block_max(scores, biases):
    top = None
    for b in range(8):
        part = scores[64 * b : 64 * b + 8]
        for k in range(1, 8):
            part = jnp.maximum(part, scores[64 * b + 8 * k : 64 * b + 8 * k + 8])
        part = part + biases[b]
        top = part if top is None else jnp.maximum(top, part)
    return column_max(top)


def shifted_weights(scores, top, biases):
    parts = [
        jnp.exp2(scores[64 * b : 64 * b + 64] - (top - biases[b])).astype(BF16) for b in range(8)
    ]
    return jnp.concatenate(parts, axis=0)


def keys_values(rows, wk, wv_t, alive, keys, values, raw):
    found = jnp.dot(rows, wk, preferred_element_type=F32)
    for pair in range(4):
        keys[pair] = found[:, 128 * pair : 128 * pair + 128].astype(BF16)
    found = lax.dot_general(wv_t, rows, NT, preferred_element_type=F32)
    ones = jnp.ones((16, 512), F32)
    for head in range(8):
        block = found[64 * head : 64 * head + 64]
        if raw is not None:
            raw[head, 0:64, :] = block.astype(BF16)
            raw[head, 64:80, :] = ones.astype(BF16)
        values[head, 0:64, :] = (block * alive).astype(BF16)
        values[head, 64:80, :] = (ones * alive).astype(BF16)
    return jnp.max(jnp.abs(found))


def own_kernel(
    occ, me, to_partner, to_cross, qkv, wv_t, query, state, peak, stats,
    normed, keys, values, raw, even, odd, sems,
):
    core = me[0] % 2
    copies = [
        pltpu.make_async_copy(to_partner, normed.at[1 - core], sems.at[0]),
        pltpu.make_async_copy(to_cross, normed.at[core], sems.at[1]),
    ]
    for copy in copies:
        copy.start()
    for copy in copies:
        copy.wait()
    lane = lax.broadcasted_iota(jnp.int32, (512, 128), 1)
    alive = [normed[half, 512:528, :].astype(F32)[0:1] for half in range(2)]
    tops = []
    for half in range(2):
        rows = normed[half, 0:512, :]
        found = jnp.dot(rows, qkv[0], preferred_element_type=F32) * SCALE
        for head in range(8):
            pair = found[:, 128 * (head // 2) : 128 * (head // 2) + 128]
            keep = lane < 64 if head % 2 == 0 else lane >= 64
            query[head, half] = jnp.where(keep, pair, 0.0).astype(BF16)
        tops.append(
            keys_values(
                rows, qkv[1], wv_t[...], alive[half], keys.at[half], values.at[half], raw.at[half]
            )
        )
    row = lax.broadcasted_iota(jnp.int32, (128, 128), 0)
    col = lax.broadcasted_iota(jnp.int32, (128, 128), 1)
    eye = row == col

    small = jnp.maximum(tops[0], tops[1]) < 1e12
    stats[0] = 0.0

    @pl.when(small)
    def plain():
        def score(head, into, unit):
            for half in (unit // 2,):
                for tile in (unit % 2,):
                    into[2 * half + tile] = lax.dot_general(
                        keys[half, head // 2],
                        query[head, half, 256 * tile : 256 * tile + 256, :],
                        NT,
                        preferred_element_type=F32,
                    )

        def attend(head, scores, unit):
            good = None
            for half in (unit // 2,):
                for tile in (unit % 2,):
                    lanes = slice(256 * tile, 256 * tile + 256)
                    parts, own = [], []
                    for chunk in range(4):
                        weights = jnp.exp2(
                            scores[2 * half + tile, 128 * chunk : 128 * chunk + 128, :]
                        )
                        if chunk // 2 == tile:
                            first = 128 * (chunk % 2)
                            block = weights[:, first : first + 128]
                            own.append(
                                jnp.sum(jnp.where(eye, block, 0.0), axis=0, keepdims=True)
                            )
                        parts.append(weights.astype(BF16))
                    out = jnp.dot(
                        values[half, head],
                        jnp.concatenate(parts, axis=0),
                        preferred_element_type=F32,
                    )
                    extra = jnp.concatenate(own, axis=1) * (1.0 - alive[half][:, lanes])
                    out = out + extra * raw[half, head, :, lanes].astype(F32)
                    state[head, half, :, lanes] = out[0:72]
                    peak[head, half, :, lanes] = jnp.zeros((8, 256), F32)
                    good = in_range(out[64:72])
            return good

        for unit in range(4):
            score(0, even, unit)

        def per_two(i, good):
            for unit in range(4):
                score(2 * i + 1, odd, unit)
                good = good * attend(2 * i, even, unit)
            for unit in range(4):
                score(jnp.minimum(2 * i + 2, 7), even, unit)
                good = good * attend(2 * i + 1, odd, unit)
            return good

        stats[0] = jnp.min(lax.fori_loop(0, 4, per_two, jnp.ones((8, 256), F32)))

    @pl.when(stats[0] < 0.5)
    def general():
        def per_head(head, carry):
            for half in range(2):
                biases = [
                    jnp.where(occ[8 * half + b] > 0, 0.0, NEG).astype(F32) for b in range(8)
                ]
                for tile in range(2):
                    lanes = slice(256 * tile, 256 * tile + 256)
                    scores = lax.dot_general(
                        keys[half, head // 2],
                        query[head, half, lanes, :],
                        NT,
                        preferred_element_type=F32,
                    )
                    selves = []
                    for k in range(2):
                        first = 256 * tile + 128 * k
                        block = scores[first : first + 128, 128 * k : 128 * k + 128]
                        selves.append(column_max(jnp.where(eye, block, NEG)))
                    dead = alive[half][:, lanes] < 0.5
                    own = jnp.where(dead, jnp.concatenate(selves, axis=1), NEG)
                    top = jnp.maximum(block_max(scores, biases), own)
                    out = jnp.dot(
                        values[half, head],
                        shifted_weights(scores, top, biases),
                        preferred_element_type=F32,
                    )
                    extra = jnp.where(dead, jnp.exp2(own - top), 0.0)
                    out = out + extra * raw[half, head, :, lanes].astype(F32)
                    state[head, half, :, lanes] = out[0:72]
                    peak[head, half, :, lanes] = jnp.broadcast_to(top, (8, 256))
            return carry

        lax.fori_loop(0, 8, per_head, 0)


def own_attention(occ, me, to_partner, to_cross, qkv, wv_t):
    return pl.pallas_call(
        own_kernel,
        name="own_attention",
        out_shape=(
            jax.ShapeDtypeStruct((8, 2, 512, 128), BF16),
            jax.ShapeDtypeStruct((8, 2, 72, 512), F32),
            jax.ShapeDtypeStruct((8, 2, 8, 512), F32),
            jax.ShapeDtypeStruct((8,), F32),
        ),
        in_specs=smem(2) + anyspace(2) + vmem(2),
        out_specs=tuple(vmem(3) + smem(1)),
        scratch_shapes=[
            VM((2, 528, 512), BF16),
            VM((2, 4, 512, 128), BF16),
            VM((2, 8, 80, 512), BF16),
            VM((2, 8, 80, 512), BF16),
            VM((4, 512, 256), F32),
            VM((4, 512, 256), F32),
            pltpu.SemaphoreType.DMA((2,)),
        ],
        compiler_params=PACKED,
        cost_estimate=cost(6 << 30, 8 << 20, 1 << 22),
    )(occ, me, to_partner, to_cross, qkv, wv_t)


def side_kernel(
    me, stats, remote, query, state, peak, qkv, wv_t, wo_t, latent_t, proj, pooled, *rest
):
    last = len(rest) == 10
    if last:
        other, out, keys, values, attended, even, odd, fast, result, sems = rest
        half = me[0] % 2
        place = pl.ds(pl.multiple_of((1 - half) * 512, 512), 512)
        send = pltpu.make_async_copy(other, out.at[:, place], sems.at[2])
        send.start()
    else:
        out, keys, values, attended, even, odd, fast = rest
        half = 1 - me[0] % 2
    flags = remote[512:528, :].astype(F32)
    value_peak = keys_values(
        remote[0:512, :], qkv[1], wv_t[...], flags[0:1], keys, values, None
    )
    fast[0] = 0.0

    def finish(head, lanes, total):
        result = total[0:64] / total[64:65]
        attended[pl.ds(pl.multiple_of(head * 64, 64), 64), lanes] = result.astype(BF16)

    @pl.when((value_peak < 1e12) & (stats[0] > 0.5))
    def plain():
        def score(pair, into, unit):
            into[unit] = lax.dot_general(
                keys[pair],
                query[2 * pair + unit // 2, half, 256 * (unit % 2) : 256 * (unit % 2) + 256, :],
                NT,
                preferred_element_type=F32,
            )

        def attend(pair, scores, unit):
            lanes = slice(256 * (unit % 2), 256 * (unit % 2) + 256)
            head = 2 * pair + unit // 2
            parts = [
                jnp.exp2(scores[unit, 128 * chunk : 128 * chunk + 128, :]).astype(BF16)
                for chunk in range(4)
            ]
            total = jnp.dot(
                values[head], jnp.concatenate(parts, axis=0), preferred_element_type=F32
            )
            total = total[0:72] + state[head, half, :, lanes]
            finish(head, lanes, total)
            return in_range(total[64:72])

        for unit in range(4):
            score(0, even, unit)

        def per_two(i, good):
            for unit in range(4):
                score(2 * i + 1, odd, unit)
                good = good * attend(2 * i, even, unit)
            for unit in range(4):
                score(jnp.minimum(2 * i + 2, 3), even, unit)
                good = good * attend(2 * i + 1, odd, unit)
            return good

        fast[0] = jnp.min(lax.fori_loop(0, 2, per_two, jnp.ones((8, 256), F32)))

    @pl.when(fast[0] < 0.5)
    def general():
        biases = [jnp.where(flags[8 + b : 9 + b, 0:256] > 0.5, 0.0, NEG) for b in range(8)]

        def per_head(head, carry):
            for tile in range(2):
                lanes = slice(256 * tile, 256 * tile + 256)
                scores = lax.dot_general(
                    keys[head // 2], query[head, half, lanes, :], NT, preferred_element_type=F32
                )
                before = peak[head, half, 0:1, lanes]
                top = jnp.maximum(block_max(scores, biases), before)
                total = jnp.dot(
                    values[head], shifted_weights(scores, top, biases), preferred_element_type=F32
                )
                finish(
                    head, lanes, total[0:72] + state[head, half, :, lanes] * jnp.exp2(before - top)
                )
            return carry

        lax.fori_loop(0, 8, per_head, 0)

    place = pl.ds(pl.multiple_of(half * 512, 512), 512)
    proj_t = proj[...].astype(F32).T.astype(BF16)
    copies = []
    for i in range(2):
        rows = slice(256 * i, 256 * i + 256)
        mixing = jnp.dot(wo_t[rows, :], attended[...], preferred_element_type=F32)
        lifted = lax.dot_general(
            proj_t[rows], pooled[place, 0:32], NT, preferred_element_type=F32
        )
        block = ((latent_t[rows, place].astype(F32) + lifted) + mixing).astype(BF16)
        if last:
            result[rows, :] = block
            copies.append(pltpu.make_async_copy(result.at[rows], out.at[rows, place], sems.at[i]))
            copies[-1].start()
        else:
            out[rows, :] = block
    if last:
        copies.append(send)
    for copy in copies:
        copy.wait()


def side_attention(me, stats, remote, *shared, other):
    last = other is not None
    return pl.pallas_call(
        side_kernel,
        name="last_attention" if last else "side_attention",
        out_shape=jax.ShapeDtypeStruct((512, 1024 if last else 512), BF16),
        in_specs=smem(2) + vmem(len(shared) + 1 + last),
        out_specs=pl.BlockSpec(memory_space=pltpu.HBM) if last else vmem(1)[0],
        scratch_shapes=[
            VM((4, 512, 128), BF16),
            VM((8, 80, 512), BF16),
            VM((512, 512), BF16),
            VM((4, 512, 256), F32),
            VM((4, 512, 256), F32),
            pltpu.SMEM((1,), F32),
        ]
        + ([VM((512, 512), BF16), pltpu.SemaphoreType.DMA((3,))] if last else []),
        compiler_params=PACKED,
        cost_estimate=cost(4 << 30, 6 << 20, 1 << 21),
    )(me, stats, remote, *shared, *([other] if last else []))


def pool_tables():
    pool = np.zeros((64, 64), np.float32)
    pick = np.zeros((64, 256), np.float32)
    for token in range(64):
        p = (token // 32) * 2 + token // 4 % 2
        q = (token // 16 % 2) * 2 + token // 2 % 2
        r = (token // 8 % 2) * 2 + token % 2
        for x in (2 * p, 2 * p + 1):
            for y in (2 * q, 2 * q + 1):
                pool[token, 8 * x + y] = 0.125
        pick[token, 64 * r : 64 * r + 64] = 1.0
    return jnp.asarray(pool, BF16), jnp.asarray(pick, F32)


def swapped(array):
    size = lax.axis_size(AXES)
    return lax.ppermute(array, AXES, [(i, i ^ 1) for i in range(size)])


def crossed(array, wrap):
    size = lax.axis_size(AXES)
    pairs = [(i, i - 1 if i % 2 == 0 else i + 1) for i in range(size)]
    pairs = [(i, j % size) for i, j in pairs if wrap or 0 <= j < size]
    return lax.ppermute(array, AXES, pairs)


def local(
    features, occupancy, neighbours, conv_weight, conv_bias, latent, token_proj, norm_gain,
    qkv_weight, out_weight,
):
    me = lax.axis_index(AXES)
    me_ref = me.astype(jnp.int32).reshape(1)
    faces = prep(occupancy, features)
    near = crossed(faces, False)
    partner = swapped(faces)
    far = crossed(partner, False)
    later, _ = lax.optimization_barrier((latent, partner))
    wv_t, wo_t, latent_t = turns(qkv_weight, out_weight, later)
    conv_weight, _ = lax.optimization_barrier((conv_weight, wo_t))
    band, band_z = bands(conv_weight)
    later, _ = lax.optimization_barrier((features, band_z))
    xb = spread(occupancy, later)
    near, xb = lax.optimization_barrier((near, xb))
    relay = swapped(near)
    acc, source = inner(neighbours.T, me_ref, xb, band)
    far, acc = lax.optimization_barrier((far, acc))
    blocks, pooled, to_partner, to_cross = outer(
        source, occupancy, me_ref, (faces, near, far, partner, relay), xb, acc, band, band_z,
        conv_bias[None, :], latent, token_proj, norm_gain[None, :],
    )
    from_cross = crossed(to_cross, True)
    from_partner = swapped(to_partner)
    query, state, peak, stats = own_attention(
        occupancy, me_ref, to_partner, to_cross, qkv_weight, wv_t
    )
    conv_out = restore(blocks)
    shared = (query, state, peak, qkv_weight, wv_t, wo_t, latent_t, token_proj, pooled)
    first = side_attention(me_ref, stats, from_partner, *shared, other=None)
    tokens_out = side_attention(me_ref, stats, from_cross, *shared, other=first)
    return (conv_out, tokens_out)


def solution(mesh):
    return jax.shard_map(
        local,
        mesh=mesh,
        in_specs=(
            P(AXES, None, None),
            P(AXES),
            P(AXES, None),
            P(),
            P(),
            P(AXES, None),
            P(),
            P(),
            P(),
            P(),
        ),
        out_specs=(P(AXES, None, None), P(None, AXES)),
        check_vma=False,
    )
```
